128 devices in a mesh: lat: 8 (over x, core), lon: 16 (over y, z).
Axes of the slice: x: 4, y: 4, z: 4, core: 2. Of those that a mesh axis runs over, the one named last changes fastest.
Arguments:
- probe_signs: int32 [16, 2048, 1024], P(None, 'lon', 'lat'), may hold values from -1 to 1, as said below
- ocean_mask: int32 [2048, 1024], P('lon', 'lat'), may hold values 0 or 1
- kappa_sq: float32 [2048, 1024], P('lon', 'lat'), may hold values from 0.02 to 0.5
- block_ids: int32 [2048, 1024], P('lon', 'lat'), may hold values from 0 to 63
Outputs:
- solution: float32 [16, 2048, 1024], P(None, 'lon', 'lat')
- trace_terms: float32 [16, 2048, 1024], P(None, 'lon', 'lat')
- traces: float32 [16, 64], replicated
The draws below stay inside these ranges and needn't reach their ends.
Inputs may be any that keep to these rules, and one draw needn't show every extreme that they name: `probe_signs`: each entry is -1 or +1.
All inputs are finite; a program needn't handle non-finite values. No bound on the sum of `ocean_mask` on one device may be relied on, other than what follows from the above.
Results may differ from the reference program's by a relative error of at most 0.0003.
Values sent between devices are 32-bit elements; how exact they have to be, the bound alone decides.
No kernel may reach another device: no remote copies, remote signals or barrier semaphores. Data moves between devices by JAX's collectives and lax.ppermute only.
A program may use at most 64 MiB of HBM per device.

```python
import math
import jax
import jax.numpy as jnp

PROBES = 16
ITERS = 3
NB = 64
NLAT = 1024
NLON = 2048


def draw_probe_signs(key, part):
    return 2 * jax.random.randint(key, (PROBES, NLON, NLAT), 0, 2, dtype=jnp.int32) - 1


def set_ends(array, stream_key, least, top_value):
    longest = array.shape.index(max(array.shape))
    spots = []
    for shift in (0, 1):
        where = [jax.random.randint(jax.random.fold_in(stream_key, axis), (), 0, length) for axis, length in enumerate(array.shape)]
        where[longest] = (where[longest] + shift) % array.shape[longest]
        spots.append(tuple(where))
    return array.at[spots[0]].set(least).at[spots[1]].set(top_value)


def block_scale(key, dims, shards, least, largest):
    level = 1.0
    for dim, shards_of in shards:
        draws = jax.random.uniform(jax.random.fold_in(jax.random.fold_in(key, 6), dim), (shards_of,), jnp.float32, least / len(shards), largest / len(shards))
        level = level * jnp.repeat(jnp.exp(draws), dims[dim] // shards_of).reshape((-1,) + (1,) * (len(dims) - 1 - dim))
    return level


def setup_inputs(seed: int = 0) -> dict:
    keys = jax.random.split(jax.random.key(seed), 5)
    probe_signs = draw_probe_signs(jax.random.fold_in(keys[4], 71), 0)
    ocean_mask = set_ends((jax.random.randint(keys[1], (NLON, NLAT), 0, 4) < 3).astype(jnp.int32), jax.random.fold_in(keys[1], 1), 0, 1)
    kappa_sq = jnp.clip(jnp.exp(math.log(0.5) - 3.218876 * jax.random.uniform(keys[2], (NLON, NLAT), jnp.float32) ** block_scale(keys[2], (NLON, NLAT), ((0, 16), (1, 8)), -0.2, 0.2)), 0.02, 0.5)
    block_ids = set_ends(jax.random.randint(keys[3], (NLON, NLAT), 0, NB), jax.random.fold_in(keys[3], 1), 0, NB - 1).astype(jnp.int32)
    return {"probe_signs": probe_signs, "ocean_mask": ocean_mask, "kappa_sq": kappa_sq, "block_ids": block_ids}


def operate(field, kappa_sq, ocean_mask):
    padded = jnp.pad(field, ((0, 0), (0, 0), (1, 1)))
    total = jnp.roll(field, 1, axis=1) + jnp.roll(field, -1, axis=1)
    total = total + padded[:, :, :-2] + padded[:, :, 2:]
    return ocean_mask * ((kappa_sq + 0.25) * field - 0.0625 * total)


def reference(probe_signs, ocean_mask, kappa_sq, block_ids):
    ocean_float = ocean_mask.astype(jnp.float32)
    probes = probe_signs.astype(jnp.float32) * ocean_float
    solution = jnp.zeros_like(probes)
    residual = probes
    direction = probes
    norm_now = jnp.sum(residual * residual, axis=(1, 2))
    for turn_index in range(ITERS):
        image = operate(operate(direction, kappa_sq, ocean_float), kappa_sq, ocean_float)
        alpha = norm_now / jnp.sum(direction * image, axis=(1, 2))
        solution = solution + alpha[:, None, None] * direction
        residual = residual - alpha[:, None, None] * image
        norm_next = jnp.sum(residual * residual, axis=(1, 2))
        direction = residual + (norm_next / norm_now)[:, None, None] * direction
        norm_now = norm_next
    applied_sol = operate(solution, kappa_sq, ocean_float)
    applied_probe = operate(probes, kappa_sq, ocean_float)
    trace_estimate = kappa_sq * (solution * applied_probe + applied_sol * probes)
    reduced_total = jax.ops.segment_sum(trace_estimate.reshape(PROBES, -1).T, block_ids.reshape(-1).astype(jnp.int32), num_segments=NB)
    traces = reduced_total.T / jnp.float32(NLAT * NLON // NB)
    return solution, trace_estimate, traces
```

```python
import jax
import jax.numpy as jnp
from jax import lax
from jax.experimental import pallas as pl
from jax.experimental.pallas import tpu as pltpu
from jax.sharding import PartitionSpec as P

F32 = jnp.float32
BF16 = jnp.bfloat16
NB = 64
NP = 16
N = 128
DEPTH = 5
W = DEPTH * NP
TOP = 16
ROWS = N + 2 * TOP
MIB = 1 << 20


def lanes(rows=8):
    return lax.broadcasted_iota(jnp.int32, (rows, N), 1)


def params(mib):
    return pltpu.CompilerParams(vmem_limit_bytes=mib * MIB)


def call(kernel, outs, mib, scratch=()):
    return pl.pallas_call(
        kernel,
        out_shape=[jax.ShapeDtypeStruct(shape, F32) for shape in outs],
        scratch_shapes=list(scratch),
        compiler_params=params(mib),
    )


def pack_kernel(signs, mask, kappa, even_ref, odd_ref, rows_ref):
    ocean = mask[...].astype(F32)
    lane = lax.broadcasted_iota(jnp.int32, (1, 2 * N), 1)
    side, spot = lane // N, lane % N
    column, probe = spot // NP, spot % NP
    row = lax.broadcasted_iota(jnp.int32, (2 * N, 2 * N), 0)
    total = jnp.zeros((N, 2 * N), F32)
    for pair in range(NP // 2):
        fields = []
        for q in (2 * pair, 2 * pair + 1):
            field = signs[q].astype(F32) * ocean
            rows_ref[0, q] = field[:8]
            rows_ref[1, q] = field[N - 8 :]
            fields.append(field.astype(BF16))
        source = column + (N - DEPTH) * side + N * (probe - 2 * pair)
        wanted = (probe // 2 == pair) & (column < DEPTH)
        source = jnp.where(wanted, source, -1)
        picks = (row == source).astype(F32).astype(BF16)
        total += jnp.dot(jnp.concatenate(fields, axis=1), picks, preferred_element_type=F32)
    here = lanes(N)
    in_kappa = (here >= W) & (here < W + DEPTH)
    left = jnp.where(in_kappa, pltpu.roll(kappa[...], W, 1), total[:, :N])
    right = jnp.where(in_kappa, pltpu.roll(kappa[...], W + DEPTH, 1), total[:, N:])
    low = lax.axis_index("lat") % 2 == 0
    even_ref[...] = jnp.where(low, right, left)
    odd_ref[...] = jnp.where(low, left, right)


def strips_kernel(even, odd, own_even, own_odd, kappa, rows, strips, kstrips, even_ref, odd_ref):
    low = lax.axis_index("lat") % 2 == 0
    from_left = jnp.where(low, odd[...], even[...])
    from_right = jnp.where(low, even[...], odd[...])
    own_left = jnp.where(low, own_odd[...], own_even[...])
    own_right = jnp.where(low, own_even[...], own_odd[...])
    here = lanes(N)
    pick_row = lax.broadcasted_iota(jnp.int32, (N, 2 * N), 0)
    pick_col = lax.broadcasted_iota(jnp.int32, (N, 2 * N), 1)
    spread = (pick_row == W + pick_col // NP) & (pick_col < 2 * W)
    spread = spread.astype(F32)
    for side, (first, second) in enumerate(((from_left, own_left), (own_right, from_right))):
        moved = pltpu.roll(second, W, 1)
        strips[2 * side] = jnp.where(here < W, first, moved)
        strips[2 * side + 1] = jnp.where(here < 2 * W - N, moved, 0.0)
        pair = jnp.where(here < W + DEPTH, first, pltpu.roll(second, DEPTH, 1))
        pair = jnp.where((here >= W) & (here < W + 2 * DEPTH), pair, 0.0)
        wide = jnp.dot(pair, spread, precision=lax.Precision.HIGHEST, preferred_element_type=F32)
        kstrips[2 * side] = wide[:, :N]
        kstrips[2 * side + 1] = wide[:, N:]
    low = lax.axis_index("lon") % 2 == 0
    for slot in range(NP + 9):
        if slot < NP:
            top, bottom = rows[0, slot], rows[1, slot]
        else:
            if slot < NP + 4:
                field = strips.at[slot - NP]
            elif slot < NP + 8:
                field = kstrips.at[slot - NP - 4]
            else:
                field = kappa
            top, bottom = field[:8], field[N - 8 :]
        even_ref[slot] = jnp.where(low, bottom, top)
        odd_ref[slot] = jnp.where(low, top, bottom)


def powers_kernel(
    signs, mask, kappa, ids, strips, kstrips, even, odd,
    u2, u4, basis, message,
    u0, u1, u3, s0, s1, centre, weight, scentre, sweight, kfull, moments,
):
    low = lax.axis_index("lon") % 2 == 0
    inner = slice(TOP, TOP + N)
    halos = ((TOP - 8, odd, even), (TOP + N, even, odd))
    ocean = mask[...].astype(F32)
    for q in range(NP):
        u0[q, inner] = signs[q].astype(F32) * ocean
    for i in range(4):
        s0[i, inner] = strips[i]
        square = strips[i] * strips[i]
        scentre[i, inner] = square * (kstrips[i] + 0.25)
        sweight[i, inner] = square * 0.0625
    centre[inner] = ocean * (kappa[...] + 0.25)
    weight[inner] = ocean * 0.0625
    for start, if_low, if_high in halos:
        rows = slice(start, start + 8)
        halo = [jnp.where(low, if_low[i], if_high[i]) for i in range(NP + 9)]
        for q in range(NP):
            u0[q, rows] = halo[q]
        for i in range(4):
            s0[i, rows] = halo[NP + i]
            square = halo[NP + i] * halo[NP + i]
            scentre[i, rows] = square * (halo[NP + 4 + i] + 0.25)
            sweight[i, rows] = square * 0.0625
        square = halo[0] * halo[0]
        centre[rows] = square * (halo[NP + 8] + 0.25)
        weight[rows] = square * 0.0625
    blank = jnp.zeros((8, N), F32)
    for field, count in ((u0, NP), (u1, NP), (u2, NP), (u3, NP), (u4, NP), (s0, 4), (s1, 4)):
        for q in range(count):
            field[q, TOP - 16 : TOP - 8] = blank
            field[q, TOP + N + 8 : TOP + N + 16] = blank

    fields = [u0, u1, u2, u3, u4]
    lane = lanes()
    even_lane = lane % 2 == 0

    def step(k, group, last):
        base = pl.multiple_of(group * 8, 8)
        rows, above, below = pl.ds(base, 8), pl.ds(base - 1, 8), pl.ds(base + 1, 8)
        source = fields[k]
        s_in, s_out = (s0, s1) if k % 2 == 0 else (s1, s0)
        now = [s_in[i, rows] for i in range(4)]
        if not last:
            for i in range(4):
                forth, back = pltpu.roll(now[i], NP, 1), pltpu.roll(now[i], N - NP, 1)
                if i % 2 == 0:
                    back = jnp.where(lane >= N - NP, pltpu.roll(now[i + 1], N - NP, 1), back)
                else:
                    forth = jnp.where(lane < NP, pltpu.roll(now[i - 1], NP, 1), forth)
                around = s_in[i, above] + s_in[i, below] + forth + back
                s_out[i, rows] = scentre[i, rows] * now[i] - sweight[i, rows] * around
        moved = pltpu.roll(now[2], N - NP - 1, 1)
        edges = (jnp.where(even_lane, now[0], moved), jnp.where(even_lane, moved, now[0]))
        middle, side = centre[rows], weight[rows]
        results = []
        for q in range(NP):
            field = source[q, rows]
            edge = pltpu.roll(edges[q % 2], N - NP * 4 - q, 1)
            forth = jnp.where(lane == 0, edge, pltpu.roll(field, 1, 1))
            back = jnp.where(lane == N - 1, edge, pltpu.roll(field, N - 1, 1))
            around = source[q, above] + source[q, below] + forth + back
            results.append(middle * field - side * around)
        return rows, results

    first, last = TOP // 8, (TOP + N) // 8
    for k in range(4):
        for group in (first - 1, last):
            rows, results = step(k, group, False)
            for q in range(NP):
                fields[k + 1][q, rows] = results[q]

        def body(group, sums, k=k):
            rows, results = step(k, group, False)
            for q in range(NP):
                fields[k + 1][q, rows] = results[q]
            return tuple(s + r * r for s, r in zip(sums, results))

        sums = lax.fori_loop(first, last, body, (blank,) * NP)
        for q in range(NP):
            moments[k, q] = sums[q]

    def finish(group, sums):
        rows, results = step(4, group, True)
        base = pl.multiple_of(group * 8 - TOP, 8)
        scale = kappa[pl.ds(base, 8)]
        for q in range(NP):
            v0, v1, v2, v3, v4 = (field[q, rows] for field in fields)
            one, zero = scale * v1, scale * v0
            basis[pl.ds(base + q * N, 8)] = one * (v0 + v0)
            basis[pl.ds(base + (NP + q) * N, 8)] = one * v2 + zero * v3
            basis[pl.ds(base + (2 * NP + q) * N, 8)] = one * v4 + zero * results[q]
        return tuple(s + r * r for s, r in zip(sums, results))

    sums = lax.fori_loop(first, last, finish, (blank,) * NP)
    for q in range(NP):
        moments[4, q] = sums[q]

    block = lax.broadcasted_iota(jnp.int32, (NB, N), 0)

    def blocks(row, total):
        data = basis[pl.ds(row, 3 * NP, stride=N)]
        high = data.astype(BF16)
        rest = (data - high.astype(F32)).astype(BF16)
        hot = (ids[pl.ds(row, 1)] == block).astype(F32).astype(BF16)
        both = jnp.concatenate([high, rest], axis=0)
        return total + lax.dot_general(both, hot, (((1,), (1,)), ((), ())), preferred_element_type=F32)

    total = lax.fori_loop(0, N, blocks, jnp.zeros((6 * NP, NB), F32), unroll=4)
    total = total[: 3 * NP] + total[3 * NP :]

    ocean_sum = jnp.sum(jnp.sum(ocean, axis=0, keepdims=True), axis=1, keepdims=True)
    columns = [jnp.broadcast_to(ocean_sum, (NP, 1))]
    for k in range(5):
        stacked = jnp.concatenate([jnp.sum(moments[k, q], axis=0, keepdims=True) for q in range(NP)], axis=0)
        columns.append(jnp.sum(stacked, axis=1, keepdims=True))
    wide = jnp.zeros((NP, NB), F32)
    spot = lax.broadcasted_iota(jnp.int32, (NP, NB), 1)
    coarse = F32(1.5 * 2**20)
    for k, column in enumerate(columns):
        head = (column + coarse) - coarse
        wide = jnp.where(spot == 2 * k, head, wide)
        wide = jnp.where(spot == 2 * k + 1, column - head, wide)
    message[:NP] = jnp.concatenate([total[:NP], wide], axis=1)
    message[NP:] = jnp.concatenate([total[NP:], jnp.zeros((2 * NP, NB), F32)], axis=1)


def two_sum(a, b):
    s = a + b
    t = s - a
    return s, (a - (s - t)) + (b - t)


def quick(a, b):
    s = a + b
    return s, b - (s - a)


def split(a):
    t = a * F32(4097.0)
    high = t - (t - a)
    return high, a - high


def mul(a, b):
    p = a[0] * b[0]
    ah, al = split(a[0])
    bh, bl = split(b[0])
    e = ((ah * bh - p) + ah * bl + al * bh) + al * bl
    return quick(p, e + (a[0] * b[1] + a[1] * b[0]))


def sub(a, b):
    s, e = two_sum(a[0], -b[0])
    return quick(s, e + (a[1] - b[1]))


def div(a, b):
    first = a[0] / b[0]
    zero = jnp.zeros_like(first)
    rest = sub(a, mul(b, (first, zero)))
    second = rest[0] / b[0]
    rest = sub(rest, mul(b, (second, zero)))
    return quick(*quick(first, second + rest[0] / b[0]))


def solve(moment):
    g0, g1, g2, h3, h4, h5 = moment
    h1, h2 = g1, g2
    tiny = F32(2e-8)
    l1, l2 = div(h2, h1), div(h3, h1)
    s11, s12, s22 = sub(h3, mul(h2, l1)), sub(h4, mul(h2, l2)), sub(h5, mul(h3, l2))
    y1, y2 = sub(g1, mul(g0, l1)), sub(g2, mul(g0, l2))
    ok1 = s11[0] > tiny * h3[0]
    one = (jnp.ones_like(h1[0]), jnp.zeros_like(h1[0]))

    def keep(ok, value, other):
        return tuple(jnp.where(ok, v, o) for v, o in zip(value, other))

    s11 = keep(ok1, s11, one)
    l21 = div(s12, s11)
    d2, z2 = sub(s22, mul(s12, l21)), sub(y2, mul(y1, l21))
    ok2 = ok1 & (d2[0] > tiny * h5[0])
    nil = (jnp.zeros_like(h1[0]),) * 2
    c2 = keep(ok2, div(z2, keep(ok2, d2, one)), nil)
    c1 = keep(ok1, div(sub(y1, mul(s12, c2)), s11), nil)
    c0 = div(sub(sub(g0, mul(h2, c1)), mul(h3, c2)), h1)
    return c0[0] + c0[1], c1[0] + c1[1], c2[0] + c2[1]


def combine_kernel(message, signs, mask, u2, u4, basis, solution, trace, traces):
    wide = message[:NP]
    moment = []
    for k in range(6):
        head = wide[:, NB + 2 * k : NB + 2 * k + 1]
        rest = wide[:, NB + 2 * k + 1 : NB + 2 * k + 2]
        moment.append(quick(jnp.broadcast_to(head, (NP, N)), jnp.broadcast_to(rest, (NP, N))))
    c0, c1, c2 = solve(moment)
    cells = F32(N * N * 128 // NB)
    total = c0 * message[:NP] + c1 * message[NP : 2 * NP] + c2 * message[2 * NP :]
    traces[...] = total[:, :NB] / cells
    ocean = mask[...].astype(F32)
    for q in range(NP):
        a0, a1, a2 = (c[q : q + 1] for c in (c0, c1, c2))
        probe = signs[q].astype(F32) * ocean
        solution[q] = a0 * probe + a1 * u2[q, TOP : TOP + N] + a2 * u4[q, TOP : TOP + N]
        rows = [slice((i * NP + q) * N, (i * NP + q + 1) * N) for i in range(3)]
        trace[q] = a0 * basis[rows[0]] + a1 * basis[rows[1]] + a2 * basis[rows[2]]


def pairs(count, offset, closed):
    out = []
    for i in range(offset, count, 2):
        j = (i + 1) % count
        if i + 1 < count or closed:
            out += [(i, j), (j, i)]
    return out


def swap(even, odd, axis, closed):
    count = lax.axis_size(axis)
    return (
        lax.ppermute(even, axis, pairs(count, 0, closed)),
        lax.ppermute(odd, axis, pairs(count, 1, closed)),
    )


def everywhere(value):
    for axis in ("lat", "lon"):
        count = lax.axis_size(axis)
        bit = 1
        while bit < count:
            value = value + lax.ppermute(value, axis, [(i, i ^ bit) for i in range(count)])
            bit *= 2
    return value


def per_device(signs, mask, kappa, ids):
    edge = (N, N)
    own_even, own_odd, rows = call(pack_kernel, [edge, edge, (2, NP, 8, N)], 8)(signs, mask, kappa)
    even, odd = swap(own_even, own_odd, "lat", False)
    halo = (NP + 9, 8, N)
    strips, kstrips, row_even, row_odd = call(strips_kernel, [(4, N, N), (4, N, N), halo, halo], 8)(
        even, odd, own_even, own_odd, kappa, rows
    )
    row_even, row_odd = swap(row_even, row_odd, "lon", True)
    field, strip, plane = (NP, ROWS, N), (4, ROWS, N), (ROWS, N)
    scratch = [field, field, field, strip, strip, plane, plane, strip, strip, (8, N), (5, NP, 8, N)]
    u2, u4, basis, message = call(
        powers_kernel,
        [field, field, (3 * NP * N, N), (3 * NP, N)],
        32,
        [pltpu.VMEM(shape, F32) for shape in scratch],
    )(signs, mask, kappa, ids, strips, kstrips, row_even, row_odd)
    message = everywhere(message)
    out = (NP, N, N)
    return tuple(call(combine_kernel, [out, out, (NP, NB)], 16)(message, signs, mask, u2, u4, basis))


def solution(mesh):
    placed = (P(None, "lon", "lat"), P("lon", "lat"), P("lon", "lat"), P("lon", "lat"))
    return jax.shard_map(
        per_device,
        mesh=mesh,
        in_specs=placed,
        out_specs=(P(None, "lon", "lat"), P(None, "lon", "lat"), P()),
        check_vma=False,
    )
```

```python
import jax
import jax.numpy as jnp
from jax import lax
from jax.experimental import pallas as pl
from jax.experimental.pallas import tpu as pltpu
from jax.sharding import PartitionSpec as P

F32 = jnp.float32
BF16 = jnp.bfloat16
NB = 64
NP = 16
N = 128
DEPTH = 5
W = DEPTH * NP
TOP = 16
ROWS = N + 2 * TOP
MIB = 1 << 20
CHUNK = 32
FINAL = 56
PARTS = 4


def lanes(rows=8):
    return lax.broadcasted_iota(jnp.int32, (rows, N), 1)


def call(kernel, outs, mib, scratch=(), aliases=None, specs=None, micros=1):
    extra = {} if specs is None else {"in_specs": specs}
    return pl.pallas_call(
        kernel,
        out_shape=[o if isinstance(o, jax.ShapeDtypeStruct) else jax.ShapeDtypeStruct(o, F32) for o in outs],
        scratch_shapes=list(scratch),
        input_output_aliases=aliases or {},
        compiler_params=pltpu.CompilerParams(vmem_limit_bytes=mib * MIB),
        cost_estimate=pl.CostEstimate(flops=0, bytes_accessed=micros * 3_000_000, transcendentals=0),
        **extra,
    )


def pack_kernel(
    signs_hbm, mask_hbm, kappa_hbm, ids_hbm,
    even_ref, odd_ref, u0, kappa, ids,
    signs, mask, sems,
):
    part = NP // PARTS
    copies = [
        pltpu.make_async_copy(mask_hbm, mask, sems.at[0]),
        pltpu.make_async_copy(kappa_hbm, kappa, sems.at[1]),
        pltpu.make_async_copy(ids_hbm, ids, sems.at[2]),
    ]
    for i in range(PARTS):
        probes = pl.ds(i * part, part)
        copies.append(pltpu.make_async_copy(signs_hbm.at[probes], signs.at[probes], sems.at[3 + i]))
    for copy in (copies[0], *copies[3:], copies[1], copies[2]):
        copy.start()
    lane = lax.broadcasted_iota(jnp.int32, (1, 2 * N), 1)
    side, spot = lane // N, lane % N
    column, probe = spot // NP, spot % NP
    row = lax.broadcasted_iota(jnp.int32, (2 * N, 2 * N), 0)
    total = jnp.zeros((N, 2 * N), F32)
    copies[0].wait()
    ocean = mask[...].astype(F32)
    for pair in range(NP // 2):
        if pair % (part // 2) == 0:
            copies[3 + pair // (part // 2)].wait()
        fields = []
        for q in (2 * pair, 2 * pair + 1):
            field = signs[q].astype(F32) * ocean
            u0[q, TOP : TOP + N] = field
            fields.append(field.astype(BF16))
        source = column + (N - DEPTH) * side + N * (probe - 2 * pair)
        wanted = (probe // 2 == pair) & (column < DEPTH)
        source = jnp.where(wanted, source, -1)
        picks = (row == source).astype(F32).astype(BF16)
        total += jnp.dot(jnp.concatenate(fields, axis=1), picks, preferred_element_type=F32)
    here = lanes(N)
    in_kappa = (here >= W) & (here < W + DEPTH)
    copies[1].wait()
    left = jnp.where(in_kappa, pltpu.roll(kappa[...], W, 1), total[:, :N])
    right = jnp.where(in_kappa, pltpu.roll(kappa[...], W + DEPTH, 1), total[:, N:])
    low = lax.axis_index("lat") % 2 == 0
    even_ref[...] = jnp.where(low, right, left)
    odd_ref[...] = jnp.where(low, left, right)
    copies[2].wait()


def strips_kernel(even, odd, own_even, own_odd, kappa, u0, strips, kstrips, even_ref, odd_ref):
    low = lax.axis_index("lat") % 2 == 0
    from_left = jnp.where(low, odd[...], even[...])
    from_right = jnp.where(low, even[...], odd[...])
    own_left = jnp.where(low, own_odd[...], own_even[...])
    own_right = jnp.where(low, own_even[...], own_odd[...])
    here = lanes(N)
    pick_row = lax.broadcasted_iota(jnp.int32, (N, 2 * N), 0)
    pick_col = lax.broadcasted_iota(jnp.int32, (N, 2 * N), 1)
    spread = (pick_row == W + pick_col // NP) & (pick_col < 2 * W)
    spread = spread.astype(F32)
    for side, (first, second) in enumerate(((from_left, own_left), (own_right, from_right))):
        moved = pltpu.roll(second, W, 1)
        strips[2 * side] = jnp.where(here < W, first, moved)
        strips[2 * side + 1] = jnp.where(here < 2 * W - N, moved, 0.0)
        pair = jnp.where(here < W + DEPTH, first, pltpu.roll(second, DEPTH, 1))
        pair = jnp.where((here >= W) & (here < W + 2 * DEPTH), pair, 0.0)
        wide = jnp.dot(pair, spread, precision=lax.Precision.HIGHEST, preferred_element_type=F32)
        kstrips[2 * side] = wide[:, :N]
        kstrips[2 * side + 1] = wide[:, N:]
    low = lax.axis_index("lon") % 2 == 0
    for slot in range(NP + 9):
        if slot < NP:
            top, bottom = u0[slot, TOP : TOP + 8], u0[slot, TOP + N - 8 : TOP + N]
        else:
            if slot < NP + 4:
                field = strips.at[slot - NP]
            elif slot < NP + 8:
                field = kstrips.at[slot - NP - 4]
            else:
                field = kappa
            top, bottom = field[:8], field[N - 8 :]
        even_ref[slot] = jnp.where(low, bottom, top)
        odd_ref[slot] = jnp.where(low, top, bottom)


def strip_step(k, s, edges, scentre, sweight, start, size):
    rows = slice(start, start + size)
    here = lanes(size)
    now = [s[k, i, rows] for i in range(4)]
    moved = pltpu.roll(now[2], N - NP - 1, 1)
    edges[k, 0, rows] = jnp.where(here % 2 == 0, now[0], moved)
    edges[k, 1, rows] = jnp.where(here % 2 == 0, moved, now[0])
    if k == DEPTH - 1:
        return
    for i in range(4):
        forth, back = pltpu.roll(now[i], NP, 1), pltpu.roll(now[i], N - NP, 1)
        if i % 2 == 0:
            back = jnp.where(here >= N - NP, pltpu.roll(now[i + 1], N - NP, 1), back)
        else:
            forth = jnp.where(here < NP, pltpu.roll(now[i - 1], NP, 1), forth)
        around = s[k, i, start - 1 : start + size - 1] + s[k, i, start + 1 : start + size + 1]
        s[k + 1, i, rows] = scentre[i, rows] * now[i] - sweight[i, rows] * (around + forth + back)


def applied(fields, edges, centre, weight, k, q, parity, start, size):
    rows = slice(start, start + size)
    here = lanes(size)
    field = fields[k][q, rows]
    edge = pltpu.roll(edges[k, parity, rows], N - NP * 4 - q, 1)
    forth = jnp.where(here == 0, edge, pltpu.roll(field, 1, 1))
    back = jnp.where(here == N - 1, edge, pltpu.roll(field, N - 1, 1))
    around = fields[k][q, start - 1 : start + size - 1] + fields[k][q, start + 1 : start + size + 1]
    return centre[rows] * field - weight[rows] * (around + forth + back)


def folded(value):
    return jnp.sum((value * value).reshape(-1, 8, N), axis=0)


def trace_basis(fields, basis, kappa, q, start, size, fifth):
    rows = slice(start, start + size)
    scale = kappa[start - TOP : start - TOP + size]
    v0, v1, v2, v3, v4 = (field[q, rows] for field in fields)
    one, zero = scale * v1, scale * v0
    for i, value in enumerate((one * (v0 + v0), one * v2 + zero * v3, one * v4 + zero * fifth)):
        base = pl.multiple_of((i * NP + q) * N + (start - TOP), 8)
        basis[pl.ds(base, size)] = value


def block_sums(basis, ids, first, last, unroll):
    block = lax.broadcasted_iota(jnp.int32, (NB, N), 0)

    def blocks(pair, total):
        high, rest, hot = [], [], []
        for row in (2 * pair, 2 * pair + 1):
            data = basis[pl.ds(row, 3 * NP, stride=N)]
            high.append(data.astype(BF16))
            rest.append((data - high[-1].astype(F32)).astype(BF16))
            hot.append((ids[pl.ds(row, 1)] == block).astype(F32).astype(BF16))
        both = jnp.concatenate([jnp.concatenate(high, axis=1), jnp.concatenate(rest, axis=1)], axis=0)
        hot = jnp.concatenate(hot, axis=1)
        return total + lax.dot_general(both, hot, (((1,), (1,)), ((), ())), preferred_element_type=F32)

    total = lax.fori_loop(first // 2, last // 2, blocks, jnp.zeros((6 * NP, NB), F32), unroll=unroll)
    return total[: 3 * NP] + total[3 * NP :]


def inner_kernel(
    u0, kappa, ids, strips, kstrips,
    u1, u2, u3, u4, s, basis, moments, sums,
    edges, centre, weight, scentre, sweight,
):
    inner = slice(TOP, TOP + N)
    ocean = u0[0, inner] * u0[0, inner]
    centre[inner] = ocean * (kappa[...] + 0.25)
    weight[inner] = ocean * 0.0625
    for i in range(4):
        s[0, i, inner] = strips[i]
        square = strips[i] * strips[i]
        scentre[i, inner] = square * (kstrips[i] + 0.25)
        sweight[i, inner] = square * 0.0625
    for k in range(DEPTH):
        for start in range(TOP, TOP + N, 32):
            strip_step(k, s, edges, scentre, sweight, start, 32)
    fields = [u0, u1, u2, u3, u4]

    def probe_pair(pair, carry):
        for parity in range(2):
            q = 2 * pair + parity
            for k in range(4):
                total = jnp.zeros((8, N), F32)
                for start in range(TOP, TOP + N, CHUNK):
                    result = applied(fields, edges, centre, weight, k, q, parity, start, CHUNK)
                    fields[k + 1][q, start : start + CHUNK] = result
                    low, high = max(start, TOP + 8), min(start + CHUNK, TOP + N - 8)
                    total += folded(result[low - start : high - start])
                moments[k, q] = total
            total = jnp.zeros((8, N), F32)
            for start in range(TOP + 8, TOP + N - 8, FINAL):
                result = applied(fields, edges, centre, weight, 4, q, parity, start, FINAL)
                total += folded(result)
                trace_basis(fields, basis, kappa, q, start, FINAL, result)
            moments[4, q] = total
        return carry

    lax.fori_loop(0, NP // 2, probe_pair, 0)
    sums[...] = block_sums(basis, ids, 8, N - 8, 14)


def outer_kernel(
    u0_in, u1_in, u2_in, u3_in, u4_in, s_in, basis_in,
    moments, sums, kappa, ids, kstrips, even, odd,
    u0, u1, u2, u3, u4, s, basis, message,
    edges, centre, weight, scentre, sweight,
):
    del u0_in, u1_in, u2_in, u3_in, u4_in, s_in, basis_in
    low = lax.axis_index("lon") % 2 == 0
    bands = (TOP - 8, TOP + N - 8)
    for start, inside, outside, if_low, if_high in (
        (bands[0], 8, 0, odd, even),
        (bands[1], 0, 8, even, odd),
    ):
        rows = slice(start + outside, start + outside + 8)
        own = slice(start + inside, start + inside + 8)
        here = slice(start + inside - TOP, start + inside - TOP + 8)
        halo = [jnp.where(low, if_low[i], if_high[i]) for i in range(NP + 9)]
        for q in range(NP):
            u0[q, rows] = halo[q]
        for i in range(4):
            s[0, i, rows] = halo[NP + i]
            for where, value, kvalue in ((rows, halo[NP + i], halo[NP + 4 + i]), (own, s[0, i, own], kstrips[i, here])):
                scentre[i, where] = value * value * (kvalue + 0.25)
                sweight[i, where] = value * value * 0.0625
        for where, value, kvalue in ((rows, halo[0], halo[NP + 8]), (own, u0[0, own], kappa[here])):
            centre[where] = value * value * (kvalue + 0.25)
            weight[where] = value * value * 0.0625
    fields = [u0, u1, u2, u3, u4]
    blank = jnp.zeros((8, N), F32)
    for row in (TOP - 16, TOP + N + 8):
        for field in fields:
            for q in range(NP):
                field[q, row : row + 8] = blank
        for k in range(DEPTH):
            for i in range(4):
                s[k, i, row : row + 8] = blank
    for k in range(DEPTH):
        for start in bands:
            strip_step(k, s, edges, scentre, sweight, start, 16)

    heads = []
    for k in range(4):
        stacked = []
        for q in range(NP):
            total = moments[k, q]
            for start, own in ((bands[0], 8), (bands[1], 0)):
                result = applied(fields, edges, centre, weight, k, q, q % 2, start, 16)
                fields[k + 1][q, start : start + 16] = result
                total += folded(result[own : own + 8])
            stacked.append(jnp.sum(total, axis=0, keepdims=True))
        heads.append(jnp.concatenate(stacked, axis=0))
    stacked = []
    for q in range(NP):
        total = moments[4, q]
        for start in (TOP, TOP + N - 8):
            result = applied(fields, edges, centre, weight, 4, q, q % 2, start, 8)
            total += folded(result)
            trace_basis(fields, basis, kappa, q, start, 8, result)
        stacked.append(jnp.sum(total, axis=0, keepdims=True))
    heads.append(jnp.concatenate(stacked, axis=0))
    total = sums[...] + block_sums(basis, ids, 0, 8, 4) + block_sums(basis, ids, N - 8, N, 4)
    ocean = u0[0, TOP : TOP + N]
    ocean = ocean * ocean

    ocean_sum = jnp.sum(jnp.sum(ocean, axis=0, keepdims=True), axis=1, keepdims=True)
    columns = [jnp.broadcast_to(ocean_sum, (NP, 1))]
    columns += [jnp.sum(head, axis=1, keepdims=True) for head in heads]
    wide = jnp.zeros((NP, NB), F32)
    spot = lax.broadcasted_iota(jnp.int32, (NP, NB), 1)
    coarse = F32(1.5 * 2**20)
    for k, column in enumerate(columns):
        head = (column + coarse) - coarse
        wide = jnp.where(spot == 2 * k, head, wide)
        wide = jnp.where(spot == 2 * k + 1, column - head, wide)
    message[:NP] = jnp.concatenate([total[:NP], wide], axis=1)
    message[NP:] = jnp.concatenate([total[NP:], jnp.zeros((2 * NP, NB), F32)], axis=1)


def two_sum(a, b):
    s = a + b
    t = s - a
    return s, (a - (s - t)) + (b - t)


def quick(a, b):
    s = a + b
    return s, b - (s - a)


def split(a):
    t = a * F32(4097.0)
    high = t - (t - a)
    return high, a - high


def mul(a, b):
    p = a[0] * b[0]
    ah, al = split(a[0])
    bh, bl = split(b[0])
    e = ((ah * bh - p) + ah * bl + al * bh) + al * bl
    return quick(p, e + (a[0] * b[1] + a[1] * b[0]))


def sub(a, b):
    s, e = two_sum(a[0], -b[0])
    return quick(s, e + (a[1] - b[1]))


def div(a, b):
    first = a[0] / b[0]
    zero = jnp.zeros_like(first)
    rest = sub(a, mul(b, (first, zero)))
    second = rest[0] / b[0]
    rest = sub(rest, mul(b, (second, zero)))
    return quick(*quick(first, second + rest[0] / b[0]))


def solve(moment):
    g0, g1, g2, h3, h4, h5 = moment
    h1, h2 = g1, g2
    tiny = F32(2e-8)
    l1, l2 = div(h2, h1), div(h3, h1)
    s11, s12, s22 = sub(h3, mul(h2, l1)), sub(h4, mul(h2, l2)), sub(h5, mul(h3, l2))
    y1, y2 = sub(g1, mul(g0, l1)), sub(g2, mul(g0, l2))
    ok1 = s11[0] > tiny * h3[0]
    one = (jnp.ones_like(h1[0]), jnp.zeros_like(h1[0]))

    def keep(ok, value, other):
        return tuple(jnp.where(ok, v, o) for v, o in zip(value, other))

    s11 = keep(ok1, s11, one)
    l21 = div(s12, s11)
    d2, z2 = sub(s22, mul(s12, l21)), sub(y2, mul(y1, l21))
    ok2 = ok1 & (d2[0] > tiny * h5[0])
    nil = (jnp.zeros_like(h1[0]),) * 2
    c2 = keep(ok2, div(z2, keep(ok2, d2, one)), nil)
    c1 = keep(ok1, div(sub(y1, mul(s12, c2)), s11), nil)
    c0 = div(sub(sub(g0, mul(h2, c1)), mul(h3, c2)), h1)
    return c0[0] + c0[1], c1[0] + c1[1], c2[0] + c2[1]


def combine_kernel(message, u0, u2, u4, basis, solution, trace, traces):
    wide = message[:NP]
    moment = []
    for k in range(6):
        head = wide[:, NB + 2 * k : NB + 2 * k + 1]
        rest = wide[:, NB + 2 * k + 1 : NB + 2 * k + 2]
        moment.append(quick(jnp.broadcast_to(head, (NP, N)), jnp.broadcast_to(rest, (NP, N))))
    c0, c1, c2 = solve(moment)
    cells = F32(N * N * 128 // NB)
    total = c0 * message[:NP] + c1 * message[NP : 2 * NP] + c2 * message[2 * NP :]
    traces[...] = total[:, :NB] / cells
    for q in range(NP):
        a0, a1, a2 = (c[q : q + 1] for c in (c0, c1, c2))
        solution[q] = a0 * u0[q, TOP : TOP + N] + a1 * u2[q, TOP : TOP + N] + a2 * u4[q, TOP : TOP + N]
        rows = [slice((i * NP + q) * N, (i * NP + q + 1) * N) for i in range(3)]
        trace[q] = a0 * basis[rows[0]] + a1 * basis[rows[1]] + a2 * basis[rows[2]]


def pairs(count, offset, closed):
    out = []
    for i in range(offset, count, 2):
        j = (i + 1) % count
        if i + 1 < count or closed:
            out += [(i, j), (j, i)]
    return out


def swap(even, odd, axis, closed):
    count = lax.axis_size(axis)
    return (
        lax.ppermute(even, axis, pairs(count, 0, closed)),
        lax.ppermute(odd, axis, pairs(count, 1, closed)),
    )


def everywhere(value):
    for axis in ("lat", "lon"):
        count = lax.axis_size(axis)
        bit = 1
        while bit < count:
            value = value + lax.ppermute(value, axis, [(i, i ^ bit) for i in range(count)])
            bit *= 2
    return value


def per_device(signs, mask, kappa, ids):
    edge, field, strip, plane = (N, N), (NP, ROWS, N), (4, ROWS, N), (ROWS, N)
    halo = (NP + 9, 8, N)
    flat = (3 * NP * N, N)
    ints = jax.ShapeDtypeStruct(edge, jnp.int32)
    own_even, own_odd, u0, kappa, ids = call(
        pack_kernel,
        [edge, edge, field, edge, ints],
        8,
        [pltpu.VMEM((NP, N, N), jnp.int32), pltpu.VMEM(edge, jnp.int32), pltpu.SemaphoreType.DMA((3 + PARTS,))],
        specs=[pl.BlockSpec(memory_space=pltpu.HBM)] * 4,
    )(*(pltpu.with_memory_space_constraint(x, pltpu.HBM) for x in (signs, mask, kappa, ids)))
    even, odd = swap(own_even, own_odd, "lat", False)
    strips, kstrips, row_even, row_odd = call(strips_kernel, [(4, N, N), (4, N, N), halo, halo], 8)(
        even, odd, own_even, own_odd, kappa, u0
    )
    row_even, row_odd = swap(row_even, row_odd, "lon", True)
    coefficients = [pltpu.VMEM(shape, F32) for shape in (plane, plane, strip, strip)]
    edges = pltpu.VMEM((DEPTH, 2, ROWS, N), F32)
    u1, u2, u3, u4, s, basis, moments, sums = call(
        inner_kernel,
        [field, field, field, field, (DEPTH, 4, ROWS, N), flat, (DEPTH, NP, 8, N), (3 * NP, NB)],
        24,
        [edges, *coefficients],
        micros=8,
    )(u0, kappa, ids, strips, kstrips)
    u0, u1, u2, u3, u4, s, basis, message = call(
        outer_kernel,
        [field, field, field, field, field, (DEPTH, 4, ROWS, N), flat, (3 * NP, N)],
        24,
        [edges, *coefficients],
        aliases={i: i for i in range(7)},
    )(u0, u1, u2, u3, u4, s, basis, moments, sums, kappa, ids, kstrips, row_even, row_odd)
    message = everywhere(message)
    out = (NP, N, N)
    return tuple(call(combine_kernel, [out, out, (NP, NB)], 16)(message, u0, u2, u4, basis))


def solution(mesh):
    placed = (P(None, "lon", "lat"), P("lon", "lat"), P("lon", "lat"), P("lon", "lat"))
    return jax.shard_map(
        per_device,
        mesh=mesh,
        in_specs=placed,
        out_specs=(P(None, "lon", "lat"), P(None, "lon", "lat"), P()),
        check_vma=False,
    )
```

```python
import jax
import jax.numpy as jnp
from jax import lax
from jax.experimental import pallas as pl
from jax.experimental.pallas import tpu as pltpu
from jax.sharding import PartitionSpec as P

F32 = jnp.float32
BF16 = jnp.bfloat16
NB = 64
NP = 16
N = 128
DEPTH = 5
W = DEPTH * NP
TOP = 16
ROWS = N + 2 * TOP
MIB = 1 << 20
FAR = pl.BlockSpec(memory_space=pltpu.HBM)
NEAR = pl.BlockSpec(memory_space=pltpu.VMEM)
CHUNK = 32
FINAL = 56
PARTS = 4


def lanes(rows=8):
    return lax.broadcasted_iota(jnp.int32, (rows, N), 1)


def call(kernel, outs, mib, scratch=(), aliases=None, specs=None, micros=1):
    extra = {} if specs is None else {"in_specs": specs}
    return pl.pallas_call(
        kernel,
        out_shape=[o if isinstance(o, jax.ShapeDtypeStruct) else jax.ShapeDtypeStruct(o, F32) for o in outs],
        scratch_shapes=list(scratch),
        input_output_aliases=aliases or {},
        compiler_params=pltpu.CompilerParams(vmem_limit_bytes=mib * MIB),
        cost_estimate=pl.CostEstimate(flops=0, bytes_accessed=micros * 3_000_000, transcendentals=0),
        **extra,
    )


def pack_kernel(
    signs_hbm, mask_hbm, kappa_hbm,
    odd_ref, even_ref, u0, kappa,
    signs, mask, picks, sems,
):
    part = NP // PARTS
    copies = [
        pltpu.make_async_copy(mask_hbm, mask, sems.at[0]),
        pltpu.make_async_copy(kappa_hbm, kappa, sems.at[1]),
    ]
    for i in range(PARTS):
        probes = pl.ds(i * part, part)
        copies.append(pltpu.make_async_copy(signs_hbm.at[probes], signs.at[probes], sems.at[2 + i]))
    for copy in (copies[0], *copies[2:], copies[1]):
        copy.start()
    lane = lax.broadcasted_iota(jnp.int32, (1, 2 * N), 1)
    side, spot = lane // N, lane % N
    column, probe = spot // NP, spot % NP
    row = lax.broadcasted_iota(jnp.int32, (2 * N, 2 * N), 0)
    for pair in range(NP // 2):
        source = column + (N - DEPTH) * side + N * (probe - 2 * pair)
        wanted = (probe // 2 == pair) & (column < DEPTH)
        source = jnp.where(wanted, source, -1)
        picks[pair] = (row == source).astype(F32).astype(BF16)
    total = jnp.zeros((N, 2 * N), F32)
    copies[0].wait()
    ocean = mask[...].astype(F32)
    for pair in range(NP // 2):
        if pair % (part // 2) == 0:
            copies[2 + pair // (part // 2)].wait()
        fields = []
        for q in (2 * pair, 2 * pair + 1):
            field = signs[q].astype(F32) * ocean
            u0[q, TOP : TOP + N] = field
            fields.append(field.astype(BF16))
        total += jnp.dot(jnp.concatenate(fields, axis=1), picks[pair], preferred_element_type=F32)
    here = lanes(N)
    in_kappa = (here >= W) & (here < W + DEPTH)
    copies[1].wait()
    left = jnp.where(in_kappa, pltpu.roll(kappa[...], W, 1), total[:, :N])
    right = jnp.where(in_kappa, pltpu.roll(kappa[...], W + DEPTH, 1), total[:, N:])
    low = lax.axis_index("lat") % 2 == 0
    even_ref[...] = jnp.where(low, right, left)
    odd_ref[...] = jnp.where(low, left, right)


def strips_kernel(odd, even, own_odd, own_even, kappa, u0, strips, kstrips, odd_ref, even_ref):
    low = lax.axis_index("lat") % 2 == 0
    from_left = jnp.where(low, odd[...], even[...])
    from_right = jnp.where(low, even[...], odd[...])
    own_left = jnp.where(low, own_odd[...], own_even[...])
    own_right = jnp.where(low, own_even[...], own_odd[...])
    here = lanes(N)
    pick_row = lax.broadcasted_iota(jnp.int32, (N, 2 * N), 0)
    pick_col = lax.broadcasted_iota(jnp.int32, (N, 2 * N), 1)
    spread = (pick_row == W + pick_col // NP) & (pick_col < 2 * W)
    spread = spread.astype(F32)
    for side, (first, second) in enumerate(((from_left, own_left), (own_right, from_right))):
        moved = pltpu.roll(second, W, 1)
        strips[2 * side] = jnp.where(here < W, first, moved)
        strips[2 * side + 1] = jnp.where(here < 2 * W - N, moved, 0.0)
        pair = jnp.where(here < W + DEPTH, first, pltpu.roll(second, DEPTH, 1))
        pair = jnp.where((here >= W) & (here < W + 2 * DEPTH), pair, 0.0)
        wide = jnp.dot(pair, spread, precision=lax.Precision.HIGHEST, preferred_element_type=F32)
        kstrips[2 * side] = wide[:, :N]
        kstrips[2 * side + 1] = wide[:, N:]
    low = lax.axis_index("lon") % 2 == 0
    for slot in range(NP + 9):
        if slot < NP:
            top, bottom = u0[slot, TOP : TOP + 8], u0[slot, TOP + N - 8 : TOP + N]
        else:
            if slot < NP + 4:
                field = strips.at[slot - NP]
            elif slot < NP + 8:
                field = kstrips.at[slot - NP - 4]
            else:
                field = kappa
            top, bottom = field[:8], field[N - 8 :]
        even_ref[slot] = jnp.where(low, bottom, top)
        odd_ref[slot] = jnp.where(low, top, bottom)


def strip_step(k, s, edges, scentre, sweight, start, size):
    rows = slice(start, start + size)
    here = lanes(size)
    now = [s[k, i, rows] for i in range(4)]
    moved = pltpu.roll(now[2], N - NP - 1, 1)
    edges[k, 0, rows] = jnp.where(here % 2 == 0, now[0], moved)
    edges[k, 1, rows] = jnp.where(here % 2 == 0, moved, now[0])
    if k == DEPTH - 1:
        return
    for i in range(4):
        forth, back = pltpu.roll(now[i], NP, 1), pltpu.roll(now[i], N - NP, 1)
        if i % 2 == 0:
            back = jnp.where(here >= N - NP, pltpu.roll(now[i + 1], N - NP, 1), back)
        else:
            forth = jnp.where(here < NP, pltpu.roll(now[i - 1], NP, 1), forth)
        around = s[k, i, start - 1 : start + size - 1] + s[k, i, start + 1 : start + size + 1]
        s[k + 1, i, rows] = scentre[i, rows] * now[i] - sweight[i, rows] * (around + forth + back)


def applied(fields, edges, centre, weight, k, q, parity, start, size):
    rows = slice(start, start + size)
    here = lanes(size)
    field = fields[k][q, rows]
    edge = pltpu.roll(edges[k, parity, rows], N - NP * 4 - q, 1)
    forth = jnp.where(here == 0, edge, pltpu.roll(field, 1, 1))
    back = jnp.where(here == N - 1, edge, pltpu.roll(field, N - 1, 1))
    around = fields[k][q, start - 1 : start + size - 1] + fields[k][q, start + 1 : start + size + 1]
    return centre[rows] * field - weight[rows] * (around + forth + back)


def folded(value):
    return jnp.sum((value * value).reshape(-1, 8, N), axis=0)


def trace_basis(fields, basis, kappa, q, start, size, fifth):
    rows = slice(start, start + size)
    scale = kappa[start - TOP : start - TOP + size]
    v0, v1, v2, v3, v4 = (field[q, rows] for field in fields)
    one, zero = scale * v1, scale * v0
    for i, value in enumerate((one * (v0 + v0), one * v2 + zero * v3, one * v4 + zero * fifth)):
        base = pl.multiple_of((i * NP + q) * N + (start - TOP), 8)
        basis[pl.ds(base, size)] = value


def block_sums(basis, ids, first, last, unroll):
    block = lax.broadcasted_iota(jnp.int32, (NB, N), 0)

    def blocks(pair, total):
        high, rest, hot = [], [], []
        for row in (2 * pair, 2 * pair + 1):
            data = basis[pl.ds(row, 3 * NP, stride=N)]
            high.append(data.astype(BF16))
            rest.append((data - high[-1].astype(F32)).astype(BF16))
            hot.append((ids[pl.ds(row, 1)] == block).astype(F32).astype(BF16))
        both = jnp.concatenate([jnp.concatenate(high, axis=1), jnp.concatenate(rest, axis=1)], axis=0)
        hot = jnp.concatenate(hot, axis=1)
        return total + lax.dot_general(both, hot, (((1,), (1,)), ((), ())), preferred_element_type=F32)

    total = lax.fori_loop(first // 2, last // 2, blocks, jnp.zeros((6 * NP, NB), F32), unroll=unroll)
    return total[: 3 * NP] + total[3 * NP :]


def inner_kernel(
    u0, kappa, ids_hbm, strips, kstrips,
    u1, u2, u3, u4, s, basis, moments, sums, ids,
    edges, sem, centre, weight, scentre, sweight,
):
    copy = pltpu.make_async_copy(ids_hbm, ids, sem)
    copy.start()
    inner = slice(TOP, TOP + N)
    ocean = u0[0, inner] * u0[0, inner]
    centre[inner] = ocean * (kappa[...] + 0.25)
    weight[inner] = ocean * 0.0625
    for i in range(4):
        s[0, i, inner] = strips[i]
        square = strips[i] * strips[i]
        scentre[i, inner] = square * (kstrips[i] + 0.25)
        sweight[i, inner] = square * 0.0625
    for k in range(DEPTH):
        for start in range(TOP, TOP + N, 32):
            strip_step(k, s, edges, scentre, sweight, start, 32)
    fields = [u0, u1, u2, u3, u4]

    def probe_pair(pair, carry):
        for parity in range(2):
            q = 2 * pair + parity
            for k in range(4):
                total = jnp.zeros((8, N), F32)
                for start in range(TOP, TOP + N, CHUNK):
                    result = applied(fields, edges, centre, weight, k, q, parity, start, CHUNK)
                    fields[k + 1][q, start : start + CHUNK] = result
                    low, high = max(start, TOP + 8), min(start + CHUNK, TOP + N - 8)
                    total += folded(result[low - start : high - start])
                moments[k, q] = total
            total = jnp.zeros((8, N), F32)
            for start in range(TOP + 8, TOP + N - 8, FINAL):
                result = applied(fields, edges, centre, weight, 4, q, parity, start, FINAL)
                total += folded(result)
                trace_basis(fields, basis, kappa, q, start, FINAL, result)
            moments[4, q] = total
        return carry

    lax.fori_loop(0, NP // 2, probe_pair, 0)
    copy.wait()
    sums[...] = block_sums(basis, ids, 8, N - 8, 14)


def outer_kernel(
    u0_in, u1_in, u2_in, u3_in, u4_in, s_in, basis_in,
    moments, sums, kappa, ids, kstrips, odd, even,
    u0, u1, u2, u3, u4, s, basis, message,
    edges, centre, weight, scentre, sweight,
):
    del u0_in, u1_in, u2_in, u3_in, u4_in, s_in, basis_in
    low = lax.axis_index("lon") % 2 == 0
    bands = (TOP - 8, TOP + N - 8)
    for start, inside, outside, if_low, if_high in (
        (bands[0], 8, 0, odd, even),
        (bands[1], 0, 8, even, odd),
    ):
        rows = slice(start + outside, start + outside + 8)
        own = slice(start + inside, start + inside + 8)
        here = slice(start + inside - TOP, start + inside - TOP + 8)
        halo = [jnp.where(low, if_low[i], if_high[i]) for i in range(NP + 9)]
        for q in range(NP):
            u0[q, rows] = halo[q]
        for i in range(4):
            s[0, i, rows] = halo[NP + i]
            for where, value, kvalue in ((rows, halo[NP + i], halo[NP + 4 + i]), (own, s[0, i, own], kstrips[i, here])):
                scentre[i, where] = value * value * (kvalue + 0.25)
                sweight[i, where] = value * value * 0.0625
        for where, value, kvalue in ((rows, halo[0], halo[NP + 8]), (own, u0[0, own], kappa[here])):
            centre[where] = value * value * (kvalue + 0.25)
            weight[where] = value * value * 0.0625
    fields = [u0, u1, u2, u3, u4]
    blank = jnp.zeros((8, N), F32)
    for row in (TOP - 16, TOP + N + 8):
        for field in fields:
            for q in range(NP):
                field[q, row : row + 8] = blank
        for k in range(DEPTH):
            for i in range(4):
                s[k, i, row : row + 8] = blank
    for k in range(DEPTH):
        for start in bands:
            strip_step(k, s, edges, scentre, sweight, start, 16)

    heads = []
    for k in range(4):
        stacked = []
        for q in range(NP):
            total = moments[k, q]
            for start, own in ((bands[0], 8), (bands[1], 0)):
                result = applied(fields, edges, centre, weight, k, q, q % 2, start, 16)
                fields[k + 1][q, start : start + 16] = result
                total += folded(result[own : own + 8])
            stacked.append(jnp.sum(total, axis=0, keepdims=True))
        heads.append(jnp.concatenate(stacked, axis=0))
    stacked = []
    for q in range(NP):
        total = moments[4, q]
        for start in (TOP, TOP + N - 8):
            result = applied(fields, edges, centre, weight, 4, q, q % 2, start, 8)
            total += folded(result)
            trace_basis(fields, basis, kappa, q, start, 8, result)
        stacked.append(jnp.sum(total, axis=0, keepdims=True))
    heads.append(jnp.concatenate(stacked, axis=0))
    total = sums[...] + block_sums(basis, ids, 0, 8, 4) + block_sums(basis, ids, N - 8, N, 4)
    ocean = u0[0, TOP : TOP + N]
    ocean = ocean * ocean

    ocean_sum = jnp.sum(jnp.sum(ocean, axis=0, keepdims=True), axis=1, keepdims=True)
    columns = [jnp.broadcast_to(ocean_sum, (NP, 1))]
    columns += [jnp.sum(head, axis=1, keepdims=True) for head in heads]
    wide = jnp.zeros((NP, NB), F32)
    spot = lax.broadcasted_iota(jnp.int32, (NP, NB), 1)
    coarse = F32(1.5 * 2**20)
    for k, column in enumerate(columns):
        head = (column + coarse) - coarse
        wide = jnp.where(spot == 2 * k, head, wide)
        wide = jnp.where(spot == 2 * k + 1, column - head, wide)
    message[:NP] = jnp.concatenate([total[:NP], wide], axis=1)
    message[NP:] = jnp.concatenate([total[NP:], jnp.zeros((2 * NP, NB), F32)], axis=1)


def two_sum(a, b):
    s = a + b
    t = s - a
    return s, (a - (s - t)) + (b - t)


def quick(a, b):
    s = a + b
    return s, b - (s - a)


def split(a):
    t = a * F32(4097.0)
    high = t - (t - a)
    return high, a - high


def mul(a, b):
    p = a[0] * b[0]
    ah, al = split(a[0])
    bh, bl = split(b[0])
    e = ((ah * bh - p) + ah * bl + al * bh) + al * bl
    return quick(p, e + (a[0] * b[1] + a[1] * b[0]))


def sub(a, b):
    s, e = two_sum(a[0], -b[0])
    return quick(s, e + (a[1] - b[1]))


def inverse(b):
    first = 1.0 / b[0]
    zero = jnp.zeros_like(first)
    rest = sub((jnp.ones_like(first), zero), mul(b, (first, zero)))
    return quick(first, first * rest[0])


def keep(ok, value, other):
    return tuple(jnp.where(ok, v, other) for v in value)


def solve(moment):
    g0, h1, h2, h3, h4, h5 = moment
    tiny = F32(2e-8)
    over = inverse(h1)
    l1, l2 = mul(h2, over), mul(h3, over)
    s11, s12, s22 = sub(h3, mul(h2, l1)), sub(h4, mul(h2, l2)), sub(h5, mul(h3, l2))
    y1, y2 = sub(h1, mul(g0, l1)), sub(h2, mul(g0, l2))
    ok1 = s11[0] > tiny * h3[0]
    over1 = keep(ok1, inverse(keep(ok1, s11, 1.0)), 0.0)
    l21 = mul(s12, over1)
    d2, z2 = sub(s22, mul(s12, l21)), sub(y2, mul(y1, l21))
    ok2 = ok1 & (d2[0] > tiny * h5[0])
    over2 = keep(ok2, inverse(keep(ok2, d2, 1.0)), 0.0)
    c2 = mul(z2, over2)
    c1 = mul(sub(y1, mul(s12, c2)), over1)
    c0 = mul(sub(sub(g0, mul(h2, c1)), mul(h3, c2)), over)
    return c0[0] + c0[1], c1[0] + c1[1], c2[0] + c2[1]


def combine_kernel(message, u0, u2, u4, basis, solution, trace, traces):
    wide = message[:NP]
    moment = []
    for k in range(6):
        head = wide[:, NB + 2 * k : NB + 2 * k + 1]
        rest = wide[:, NB + 2 * k + 1 : NB + 2 * k + 2]
        moment.append(quick(jnp.broadcast_to(head, (NP, N)), jnp.broadcast_to(rest, (NP, N))))
    c0, c1, c2 = solve(moment)
    cells = F32(N * N * 128 // NB)
    total = c0 * message[:NP] + c1 * message[NP : 2 * NP] + c2 * message[2 * NP :]
    traces[...] = total[:, :NB] / cells
    for q in range(NP):
        a0, a1, a2 = (c[q : q + 1] for c in (c0, c1, c2))
        solution[q] = a0 * u0[q, TOP : TOP + N] + a1 * u2[q, TOP : TOP + N] + a2 * u4[q, TOP : TOP + N]
        rows = [slice((i * NP + q) * N, (i * NP + q + 1) * N) for i in range(3)]
        trace[q] = a0 * basis[rows[0]] + a1 * basis[rows[1]] + a2 * basis[rows[2]]


def pairs(count, offset, closed):
    out = []
    for i in range(offset, count, 2):
        j = (i + 1) % count
        if i + 1 < count or closed:
            out += [(i, j), (j, i)]
    return out


def swap(odd, even, axis, closed):
    count = lax.axis_size(axis)
    odd = lax.ppermute(odd, axis, pairs(count, 1, closed))
    even = lax.ppermute(even, axis, pairs(count, 0, closed))
    return odd, even


def everywhere(value):
    for axis in ("lat", "lon"):
        count = lax.axis_size(axis)
        bit = 1
        while bit < count:
            value = value + lax.ppermute(value, axis, [(i, i ^ bit) for i in range(count)])
            bit *= 2
    return value


def per_device(signs, mask, kappa, ids):
    edge, field, strip, plane = (N, N), (NP, ROWS, N), (4, ROWS, N), (ROWS, N)
    halo = (NP + 9, 8, N)
    flat = (3 * NP * N, N)
    ints = jax.ShapeDtypeStruct(edge, jnp.int32)
    signs, mask, kappa, ids = (pltpu.with_memory_space_constraint(x, pltpu.HBM) for x in (signs, mask, kappa, ids))
    own_odd, own_even, u0, kappa = call(
        pack_kernel,
        [edge, edge, field, edge],
        8,
        [
            pltpu.VMEM((NP, N, N), jnp.int32),
            pltpu.VMEM(edge, jnp.int32),
            pltpu.VMEM((NP // 2, 2 * N, 2 * N), BF16),
            pltpu.SemaphoreType.DMA((2 + PARTS,)),
        ],
        specs=[FAR] * 3,
    )(signs, mask, kappa)
    odd, even = swap(own_odd, own_even, "lat", False)
    strips, kstrips, row_odd, row_even = call(strips_kernel, [(4, N, N), (4, N, N), halo, halo], 8)(
        odd, even, own_odd, own_even, kappa, u0
    )
    row_odd, row_even = swap(row_odd, row_even, "lon", True)
    coefficients = [pltpu.VMEM(shape, F32) for shape in (plane, plane, strip, strip)]
    edges = pltpu.VMEM((DEPTH, 2, ROWS, N), F32)
    u1, u2, u3, u4, s, basis, moments, sums, ids = call(
        inner_kernel,
        [field, field, field, field, (DEPTH, 4, ROWS, N), flat, (DEPTH, NP, 8, N), (3 * NP, NB), ints],
        24,
        [edges, pltpu.SemaphoreType.DMA, *coefficients],
        specs=[NEAR, NEAR, FAR, NEAR, NEAR],
        micros=8,
    )(u0, kappa, ids, strips, kstrips)
    u0, u1, u2, u3, u4, s, basis, message = call(
        outer_kernel,
        [field, field, field, field, field, (DEPTH, 4, ROWS, N), flat, (3 * NP, N)],
        24,
        [edges, *coefficients],
        aliases={i: i for i in range(7)},
    )(u0, u1, u2, u3, u4, s, basis, moments, sums, kappa, ids, kstrips, row_odd, row_even)
    message = everywhere(message)
    out = (NP, N, N)
    return tuple(call(combine_kernel, [out, out, (NP, NB)], 16)(message, u0, u2, u4, basis))


def solution(mesh):
    placed = (P(None, "lon", "lat"), P("lon", "lat"), P("lon", "lat"), P("lon", "lat"))
    return jax.shard_map(
        per_device,
        mesh=mesh,
        in_specs=placed,
        out_specs=(P(None, "lon", "lat"), P(None, "lon", "lat"), P()),
        check_vma=False,
    )
```

```python
import jax
import jax.numpy as jnp
from jax import lax
from jax.experimental import pallas as pl
from jax.experimental.pallas import tpu as pltpu
from jax.sharding import PartitionSpec as P

F32 = jnp.float32
BF16 = jnp.bfloat16
NB = 64
NP = 16
N = 128
DEPTH = 5
W = DEPTH * NP
TOP = 16
ROWS = N + 2 * TOP
MIB = 1 << 20
FAR = pl.BlockSpec(memory_space=pltpu.HBM)
NEAR = pl.BlockSpec(memory_space=pltpu.VMEM)
CHUNK = 32
FINAL = 56
PARTS = 4


def lanes(rows=8):
    return lax.broadcasted_iota(jnp.int32, (rows, N), 1)


def call(kernel, outs, mib, scratch=(), aliases=None, specs=None, micros=1):
    extra = {} if specs is None else {"in_specs": specs}
    return pl.pallas_call(
        kernel,
        out_shape=[o if isinstance(o, jax.ShapeDtypeStruct) else jax.ShapeDtypeStruct(o, F32) for o in outs],
        scratch_shapes=list(scratch),
        input_output_aliases=aliases or {},
        compiler_params=pltpu.CompilerParams(vmem_limit_bytes=mib * MIB),
        cost_estimate=pl.CostEstimate(flops=0, bytes_accessed=micros * 3_000_000, transcendentals=0),
        **extra,
    )


def pack_kernel(
    signs_hbm, mask_hbm, kappa_hbm,
    odd_ref, even_ref, u0, kappa,
    signs, mask, picks, sems,
):
    part = NP // PARTS
    copies = [
        pltpu.make_async_copy(mask_hbm, mask, sems.at[0]),
        pltpu.make_async_copy(kappa_hbm, kappa, sems.at[1]),
    ]
    for i in range(PARTS):
        probes = pl.ds(i * part, part)
        copies.append(pltpu.make_async_copy(signs_hbm.at[probes], signs.at[probes], sems.at[2 + i]))
    for copy in (copies[0], *copies[2:], copies[1]):
        copy.start()
    lane = lax.broadcasted_iota(jnp.int32, (1, 2 * N), 1)
    side, spot = lane // N, lane % N
    column, probe = spot // NP, spot % NP
    row = lax.broadcasted_iota(jnp.int32, (2 * N, 2 * N), 0)
    for pair in range(NP // 2):
        source = column + (N - DEPTH) * side + N * (probe - 2 * pair)
        wanted = (probe // 2 == pair) & (column < DEPTH)
        source = jnp.where(wanted, source, -1)
        picks[pair] = (row == source).astype(F32).astype(BF16)
    total = jnp.zeros((N, 2 * N), F32)
    copies[0].wait()
    ocean = mask[...].astype(F32)
    for pair in range(NP // 2):
        if pair % (part // 2) == 0:
            copies[2 + pair // (part // 2)].wait()
        fields = []
        for q in (2 * pair, 2 * pair + 1):
            field = signs[q].astype(F32) * ocean
            u0[q, TOP : TOP + N] = field
            fields.append(field.astype(BF16))
        total += jnp.dot(jnp.concatenate(fields, axis=1), picks[pair], preferred_element_type=F32)
    here = lanes(N)
    in_kappa = (here >= W) & (here < W + DEPTH)
    copies[1].wait()
    left = jnp.where(in_kappa, pltpu.roll(kappa[...], W, 1), total[:, :N])
    right = jnp.where(in_kappa, pltpu.roll(kappa[...], W + DEPTH, 1), total[:, N:])
    low = lax.axis_index("lat") % 2 == 0
    even_ref[...] = jnp.where(low, right, left)
    odd_ref[...] = jnp.where(low, left, right)


def strips_kernel(odd, even, own_odd, own_even, kappa, u0, strips, kstrips, odd_ref, even_ref):
    low = lax.axis_index("lat") % 2 == 0
    from_left = jnp.where(low, odd[...], even[...])
    from_right = jnp.where(low, even[...], odd[...])
    own_left = jnp.where(low, own_odd[...], own_even[...])
    own_right = jnp.where(low, own_even[...], own_odd[...])
    here = lanes(N)
    pick_row = lax.broadcasted_iota(jnp.int32, (N, 2 * N), 0)
    pick_col = lax.broadcasted_iota(jnp.int32, (N, 2 * N), 1)
    spread = (pick_row == W + pick_col // NP) & (pick_col < 2 * W)
    spread = spread.astype(F32)
    for side, (first, second) in enumerate(((from_left, own_left), (own_right, from_right))):
        moved = pltpu.roll(second, W, 1)
        strips[2 * side] = jnp.where(here < W, first, moved)
        strips[2 * side + 1] = jnp.where(here < 2 * W - N, moved, 0.0)
        pair = jnp.where(here < W + DEPTH, first, pltpu.roll(second, DEPTH, 1))
        pair = jnp.where((here >= W) & (here < W + 2 * DEPTH), pair, 0.0)
        wide = jnp.dot(pair, spread, precision=lax.Precision.HIGHEST, preferred_element_type=F32)
        kstrips[2 * side] = wide[:, :N]
        kstrips[2 * side + 1] = wide[:, N:]
    low = lax.axis_index("lon") % 2 == 0
    for slot in range(NP + 9):
        if slot < NP:
            top, bottom = u0[slot, TOP : TOP + 8], u0[slot, TOP + N - 8 : TOP + N]
        else:
            if slot < NP + 4:
                field = strips.at[slot - NP]
            elif slot < NP + 8:
                field = kstrips.at[slot - NP - 4]
            else:
                field = kappa
            top, bottom = field[:8], field[N - 8 :]
        even_ref[slot] = jnp.where(low, bottom, top)
        odd_ref[slot] = jnp.where(low, top, bottom)


def strip_step(k, s, edges, scentre, sweight, start, size):
    rows = slice(start, start + size)
    here = lanes(size)
    now = [s[k, i, rows] for i in range(4)]
    moved = pltpu.roll(now[2], N - NP - 1, 1)
    edges[k, 0, rows] = jnp.where(here % 2 == 0, now[0], moved)
    edges[k, 1, rows] = jnp.where(here % 2 == 0, moved, now[0])
    if k == DEPTH - 1:
        return
    for i in range(4):
        forth, back = pltpu.roll(now[i], NP, 1), pltpu.roll(now[i], N - NP, 1)
        if i % 2 == 0:
            back = jnp.where(here >= N - NP, pltpu.roll(now[i + 1], N - NP, 1), back)
        else:
            forth = jnp.where(here < NP, pltpu.roll(now[i - 1], NP, 1), forth)
        around = s[k, i, start - 1 : start + size - 1] + s[k, i, start + 1 : start + size + 1]
        s[k + 1, i, rows] = scentre[i, rows] * now[i] - sweight[i, rows] * (around + forth + back)


def applied(fields, edges, centre, weight, k, q, parity, start, size):
    rows = slice(start, start + size)
    here = lanes(size)
    field = fields[k][q, rows]
    edge = pltpu.roll(edges[k, parity, rows], N - NP * 4 - q, 1)
    forth = jnp.where(here == 0, edge, pltpu.roll(field, 1, 1))
    back = jnp.where(here == N - 1, edge, pltpu.roll(field, N - 1, 1))
    around = fields[k][q, start - 1 : start + size - 1] + fields[k][q, start + 1 : start + size + 1]
    return centre[rows] * field - weight[rows] * (around + forth + back)


def folded(value):
    return jnp.sum((value * value).reshape(-1, 8, N), axis=0)


def trace_basis(fields, basis, kappa, q, start, size, fifth):
    rows = slice(start, start + size)
    scale = kappa[start - TOP : start - TOP + size]
    v0, v1, v2, v3, v4 = (field[q, rows] for field in fields)
    one, zero = scale * v1, scale * v0
    for i, value in enumerate((one * (v0 + v0), one * v2 + zero * v3, one * v4 + zero * fifth)):
        base = pl.multiple_of((i * NP + q) * N + (start - TOP), 8)
        basis[pl.ds(base, size)] = value


def block_sums(basis, ids, first, last, unroll):
    block = lax.broadcasted_iota(jnp.int32, (NB, N), 0)

    def blocks(pair, total):
        high, rest, hot = [], [], []
        for row in (2 * pair, 2 * pair + 1):
            data = basis[pl.ds(row, 3 * NP, stride=N)]
            high.append(data.astype(BF16))
            rest.append((data - high[-1].astype(F32)).astype(BF16))
            hot.append((ids[pl.ds(row, 1)] == block).astype(F32).astype(BF16))
        both = jnp.concatenate([jnp.concatenate(high, axis=1), jnp.concatenate(rest, axis=1)], axis=0)
        hot = jnp.concatenate(hot, axis=1)
        return total + lax.dot_general(both, hot, (((1,), (1,)), ((), ())), preferred_element_type=F32)

    total = lax.fori_loop(first // 2, last // 2, blocks, jnp.zeros((6 * NP, NB), F32), unroll=unroll)
    return total[: 3 * NP] + total[3 * NP :]


def inner_kernel(
    u0, kappa, ids_hbm, strips, kstrips,
    u1, u2, u3, u4, s, basis, moments, sums, ids,
    edges, sem, centre, weight, scentre, sweight,
):
    copy = pltpu.make_async_copy(ids_hbm, ids, sem)
    copy.start()
    inner = slice(TOP, TOP + N)
    ocean = u0[0, inner] * u0[0, inner]
    centre[inner] = ocean * (kappa[...] + 0.25)
    weight[inner] = ocean * 0.0625
    for i in range(4):
        s[0, i, inner] = strips[i]
        square = strips[i] * strips[i]
        scentre[i, inner] = square * (kstrips[i] + 0.25)
        sweight[i, inner] = square * 0.0625
    for k in range(DEPTH):
        for start in range(TOP, TOP + N, 32):
            strip_step(k, s, edges, scentre, sweight, start, 32)
    fields = [u0, u1, u2, u3, u4]

    def probe_pair(pair, carry):
        for parity in range(2):
            q = 2 * pair + parity
            for k in range(4):
                total = jnp.zeros((8, N), F32)
                for start in range(TOP, TOP + N, CHUNK):
                    result = applied(fields, edges, centre, weight, k, q, parity, start, CHUNK)
                    fields[k + 1][q, start : start + CHUNK] = result
                    low, high = max(start, TOP + 8), min(start + CHUNK, TOP + N - 8)
                    total += folded(result[low - start : high - start])
                moments[k, q] = total
            total = jnp.zeros((8, N), F32)
            for start in range(TOP + 8, TOP + N - 8, FINAL):
                result = applied(fields, edges, centre, weight, 4, q, parity, start, FINAL)
                total += folded(result)
                trace_basis(fields, basis, kappa, q, start, FINAL, result)
            moments[4, q] = total
        return carry

    lax.fori_loop(0, NP // 2, probe_pair, 0)
    copy.wait()
    sums[...] = block_sums(basis, ids, 8, N - 8, 14)


def outer_kernel(
    u0_in, u1_in, u2_in, u3_in, u4_in, s_in, basis_in,
    moments, sums, kappa, ids, kstrips, odd, even,
    u0, u1, u2, u3, u4, s, basis, message,
    edges, centre, weight, scentre, sweight,
):
    del u0_in, u1_in, u2_in, u3_in, u4_in, s_in, basis_in
    low = lax.axis_index("lon") % 2 == 0
    bands = (TOP - 8, TOP + N - 8)
    for start, inside, outside, if_low, if_high in (
        (bands[0], 8, 0, odd, even),
        (bands[1], 0, 8, even, odd),
    ):
        rows = slice(start + outside, start + outside + 8)
        own = slice(start + inside, start + inside + 8)
        here = slice(start + inside - TOP, start + inside - TOP + 8)
        halo = [jnp.where(low, if_low[i], if_high[i]) for i in range(NP + 9)]
        for q in range(NP):
            u0[q, rows] = halo[q]
        for i in range(4):
            s[0, i, rows] = halo[NP + i]
            for where, value, kvalue in ((rows, halo[NP + i], halo[NP + 4 + i]), (own, s[0, i, own], kstrips[i, here])):
                scentre[i, where] = value * value * (kvalue + 0.25)
                sweight[i, where] = value * value * 0.0625
        for where, value, kvalue in ((rows, halo[0], halo[NP + 8]), (own, u0[0, own], kappa[here])):
            centre[where] = value * value * (kvalue + 0.25)
            weight[where] = value * value * 0.0625
    fields = [u0, u1, u2, u3, u4]
    blank = jnp.zeros((8, N), F32)
    for row in (TOP - 16, TOP + N + 8):
        for field in fields:
            for q in range(NP):
                field[q, row : row + 8] = blank
        for k in range(DEPTH):
            for i in range(4):
                s[k, i, row : row + 8] = blank
    for k in range(DEPTH):
        for start in bands:
            strip_step(k, s, edges, scentre, sweight, start, 16)

    heads = []
    for k in range(4):
        stacked = []
        for q in range(NP):
            total = moments[k, q]
            for start, own in ((bands[0], 8), (bands[1], 0)):
                result = applied(fields, edges, centre, weight, k, q, q % 2, start, 16)
                fields[k + 1][q, start : start + 16] = result
                total += folded(result[own : own + 8])
            stacked.append(jnp.sum(total, axis=0, keepdims=True))
        heads.append(jnp.concatenate(stacked, axis=0))
    stacked = []
    for q in range(NP):
        total = moments[4, q]
        for start in (TOP, TOP + N - 8):
            result = applied(fields, edges, centre, weight, 4, q, q % 2, start, 8)
            total += folded(result)
            trace_basis(fields, basis, kappa, q, start, 8, result)
        stacked.append(jnp.sum(total, axis=0, keepdims=True))
    heads.append(jnp.concatenate(stacked, axis=0))
    total = sums[...] + block_sums(basis, ids, 0, 8, 4) + block_sums(basis, ids, N - 8, N, 4)
    ocean = u0[0, TOP : TOP + N]
    ocean = ocean * ocean

    ocean_sum = jnp.sum(jnp.sum(ocean, axis=0, keepdims=True), axis=1, keepdims=True)
    columns = [jnp.broadcast_to(ocean_sum, (NP, 1))]
    columns += [jnp.sum(head, axis=1, keepdims=True) for head in heads]
    wide = jnp.zeros((NP, NB), F32)
    spot = lax.broadcasted_iota(jnp.int32, (NP, NB), 1)
    coarse = F32(1.5 * 2**20)
    for k, column in enumerate(columns):
        head = (column + coarse) - coarse
        wide = jnp.where(spot == 2 * k, head, wide)
        wide = jnp.where(spot == 2 * k + 1, column - head, wide)
    message[:NP] = jnp.concatenate([total[:NP], wide], axis=1)
    message[NP:] = jnp.concatenate([total[NP:], jnp.zeros((2 * NP, NB), F32)], axis=1)


def two_sum(a, b):
    s = a + b
    t = s - a
    return s, (a - (s - t)) + (b - t)


def quick(a, b):
    s = a + b
    return s, b - (s - a)


def split(a):
    t = a * F32(4097.0)
    high = t - (t - a)
    return high, a - high


def mul(a, b):
    p = a[0] * b[0]
    ah, al = split(a[0])
    bh, bl = split(b[0])
    e = ((ah * bh - p) + ah * bl + al * bh) + al * bl
    return quick(p, e + (a[0] * b[1] + a[1] * b[0]))


def sub(a, b):
    s, e = two_sum(a[0], -b[0])
    return quick(s, e + (a[1] - b[1]))


def inverse(b):
    first = 1.0 / b[0]
    zero = jnp.zeros_like(first)
    rest = sub((jnp.ones_like(first), zero), mul(b, (first, zero)))
    return quick(first, first * rest[0])


def keep(ok, value, other):
    return tuple(jnp.where(ok, v, other) for v in value)


def solve(moment):
    g0, h1, h2, h3, h4, h5 = moment
    tiny = F32(2e-8)
    over = inverse(h1)
    l1, l2 = mul(h2, over), mul(h3, over)
    s11, s12, s22 = sub(h3, mul(h2, l1)), sub(h4, mul(h2, l2)), sub(h5, mul(h3, l2))
    y1, y2 = sub(h1, mul(g0, l1)), sub(h2, mul(g0, l2))
    ok1 = s11[0] > tiny * h3[0]
    over1 = keep(ok1, inverse(keep(ok1, s11, 1.0)), 0.0)
    l21 = mul(s12, over1)
    d2, z2 = sub(s22, mul(s12, l21)), sub(y2, mul(y1, l21))
    ok2 = ok1 & (d2[0] > tiny * h5[0])
    over2 = keep(ok2, inverse(keep(ok2, d2, 1.0)), 0.0)
    c2 = mul(z2, over2)
    c1 = mul(sub(y1, mul(s12, c2)), over1)
    c0 = mul(sub(sub(g0, mul(h2, c1)), mul(h3, c2)), over)
    return c0[0] + c0[1], c1[0] + c1[1], c2[0] + c2[1]


def combine_kernel(message, u0, u2, u4, basis, solution, trace, traces):
    wide = message[:NP]
    moment = []
    for k in range(6):
        head = wide[:, NB + 2 * k : NB + 2 * k + 1]
        rest = wide[:, NB + 2 * k + 1 : NB + 2 * k + 2]
        moment.append(quick(jnp.broadcast_to(head, (NP, N)), jnp.broadcast_to(rest, (NP, N))))
    c0, c1, c2 = solve(moment)
    cells = F32(N * N * 128 // NB)
    total = c0 * message[:NP] + c1 * message[NP : 2 * NP] + c2 * message[2 * NP :]
    traces[...] = total[:, :NB] / cells
    for q in range(NP):
        a0, a1, a2 = (c[q : q + 1] for c in (c0, c1, c2))
        solution[q] = a0 * u0[q, TOP : TOP + N] + a1 * u2[q, TOP : TOP + N] + a2 * u4[q, TOP : TOP + N]
        rows = [slice((i * NP + q) * N, (i * NP + q + 1) * N) for i in range(3)]
        trace[q] = a0 * basis[rows[0]] + a1 * basis[rows[1]] + a2 * basis[rows[2]]


def pairs(count, offset, closed):
    out = []
    for i in range(offset, count, 2):
        j = (i + 1) % count
        if i + 1 < count or closed:
            out += [(i, j), (j, i)]
    return out


def swap(odd, even, axis, closed):
    count = lax.axis_size(axis)
    odd = lax.ppermute(odd, axis, pairs(count, 1, closed))
    even = lax.ppermute(even, axis, pairs(count, 0, closed))
    return odd, even


def everywhere(value):
    def sent(axis, bits):
        return lax.ppermute(value, axis, [(i, i ^ bits) for i in range(lax.axis_size(axis))])

    value = value + sent("lat", 1)
    for axis, unit in (("lat", 2), ("lon", 1), ("lon", 4)):
        near, far, across = sent(axis, unit), sent(axis, 3 * unit), sent(axis, 2 * unit)
        value = (value + near) + (far + across)
    return value


def per_device(signs, mask, kappa, ids):
    edge, field, strip, plane = (N, N), (NP, ROWS, N), (4, ROWS, N), (ROWS, N)
    halo = (NP + 9, 8, N)
    flat = (3 * NP * N, N)
    ints = jax.ShapeDtypeStruct(edge, jnp.int32)
    signs, mask, kappa, ids = (pltpu.with_memory_space_constraint(x, pltpu.HBM) for x in (signs, mask, kappa, ids))
    own_odd, own_even, u0, kappa = call(
        pack_kernel,
        [edge, edge, field, edge],
        8,
        [
            pltpu.VMEM((NP, N, N), jnp.int32),
            pltpu.VMEM(edge, jnp.int32),
            pltpu.VMEM((NP // 2, 2 * N, 2 * N), BF16),
            pltpu.SemaphoreType.DMA((2 + PARTS,)),
        ],
        specs=[FAR] * 3,
    )(signs, mask, kappa)
    odd, even = swap(own_odd, own_even, "lat", False)
    strips, kstrips, row_odd, row_even = call(strips_kernel, [(4, N, N), (4, N, N), halo, halo], 8)(
        odd, even, own_odd, own_even, kappa, u0
    )
    row_odd, row_even = swap(row_odd, row_even, "lon", True)
    coefficients = [pltpu.VMEM(shape, F32) for shape in (plane, plane, strip, strip)]
    edges = pltpu.VMEM((DEPTH, 2, ROWS, N), F32)
    u1, u2, u3, u4, s, basis, moments, sums, ids = call(
        inner_kernel,
        [field, field, field, field, (DEPTH, 4, ROWS, N), flat, (DEPTH, NP, 8, N), (3 * NP, NB), ints],
        24,
        [edges, pltpu.SemaphoreType.DMA, *coefficients],
        specs=[NEAR, NEAR, FAR, NEAR, NEAR],
        micros=8,
    )(u0, kappa, ids, strips, kstrips)
    u0, u1, u2, u3, u4, s, basis, message = call(
        outer_kernel,
        [field, field, field, field, field, (DEPTH, 4, ROWS, N), flat, (3 * NP, N)],
        24,
        [edges, *coefficients],
        aliases={i: i for i in range(7)},
    )(u0, u1, u2, u3, u4, s, basis, moments, sums, kappa, ids, kstrips, row_odd, row_even)
    message = everywhere(message)
    out = (NP, N, N)
    return tuple(call(combine_kernel, [out, out, (NP, NB)], 16)(message, u0, u2, u4, basis))


def solution(mesh):
    placed = (P(None, "lon", "lat"), P("lon", "lat"), P("lon", "lat"), P("lon", "lat"))
    return jax.shard_map(
        per_device,
        mesh=mesh,
        in_specs=placed,
        out_specs=(P(None, "lon", "lat"), P(None, "lon", "lat"), P()),
        check_vma=False,
    )
```

```python
import jax
import jax.numpy as jnp
from jax import lax
from jax.experimental import pallas as pl
from jax.experimental.pallas import tpu as pltpu
from jax.sharding import PartitionSpec as P

F32 = jnp.float32
BF16 = jnp.bfloat16
NB = 64
NP = 16
N = 128
DEPTH = 5
W = DEPTH * NP
SLOTS = NP + 6
TOP = 16
ROWS = N + 2 * TOP
MIB = 1 << 20
FAR = pl.BlockSpec(memory_space=pltpu.HBM)
NEAR = pl.BlockSpec(memory_space=pltpu.VMEM)
CHUNK = 32
FINAL = 56
TOGETHER = 4
PARTS = 4


def lanes(rows=8):
    return lax.broadcasted_iota(jnp.int32, (rows, N), 1)


def call(kernel, outs, mib, scratch=(), aliases=None, specs=None, micros=1):
    extra = {} if specs is None else {"in_specs": specs}
    return pl.pallas_call(
        kernel,
        out_shape=[o if isinstance(o, jax.ShapeDtypeStruct) else jax.ShapeDtypeStruct(o, F32) for o in outs],
        scratch_shapes=list(scratch),
        input_output_aliases=aliases or {},
        compiler_params=pltpu.CompilerParams(vmem_limit_bytes=mib * MIB),
        cost_estimate=pl.CostEstimate(flops=0, bytes_accessed=micros * 3_000_000, transcendentals=0),
        **extra,
    )


def pack_kernel(
    signs_hbm, mask_hbm, kappa_hbm,
    odd_ref, even_ref, u0, kappa,
    signs, mask, picks, sems,
):
    part = NP // PARTS
    copies = [
        pltpu.make_async_copy(mask_hbm, mask, sems.at[0]),
        pltpu.make_async_copy(kappa_hbm, kappa, sems.at[1]),
    ]
    for i in range(PARTS):
        probes = pl.ds(i * part, part)
        copies.append(pltpu.make_async_copy(signs_hbm.at[probes], signs.at[probes], sems.at[2 + i]))
    for copy in (copies[0], *copies[2:], copies[1]):
        copy.start()
    lane = lax.broadcasted_iota(jnp.int32, (1, 2 * N), 1)
    side, spot = lane // N, lane % N
    column, probe = spot // NP, spot % NP
    row = lax.broadcasted_iota(jnp.int32, (2 * N, 2 * N), 0)
    for pair in range(NP // 2):
        source = column + (N - DEPTH) * side + N * (probe - 2 * pair)
        wanted = (probe // 2 == pair) & (column < DEPTH)
        source = jnp.where(wanted, source, -1)
        picks[pair] = (row == source).astype(F32).astype(BF16)
    total = jnp.zeros((N, 2 * N), F32)
    copies[0].wait()
    ocean = mask[...].astype(F32)
    for pair in range(NP // 2):
        if pair % (part // 2) == 0:
            copies[2 + pair // (part // 2)].wait()
        fields = []
        for q in (2 * pair, 2 * pair + 1):
            field = signs[q].astype(F32) * ocean
            u0[q, TOP : TOP + N] = field
            fields.append(field.astype(BF16))
        total += jnp.dot(jnp.concatenate(fields, axis=1), picks[pair], preferred_element_type=F32)
    here = lanes(N)
    in_kappa = (here >= W) & (here < W + DEPTH)
    copies[1].wait()
    left = jnp.where(in_kappa, pltpu.roll(kappa[...], W, 1), total[:, :N])
    right = jnp.where(in_kappa, pltpu.roll(kappa[...], W + DEPTH, 1), total[:, N:])
    low = lax.axis_index("lat") % 2 == 0
    even_ref[...] = jnp.where(low, right, left)
    odd_ref[...] = jnp.where(low, left, right)


def strips_kernel(odd, even, own_odd, own_even, kappa, u0, strips, kstrips, odd_ref, even_ref):
    low = lax.axis_index("lat") % 2 == 0
    from_left = jnp.where(low, odd[...], even[...])
    from_right = jnp.where(low, even[...], odd[...])
    own_left = jnp.where(low, own_odd[...], own_even[...])
    own_right = jnp.where(low, own_even[...], own_odd[...])
    here = lanes(N)
    strips[0] = jnp.where(here < W, from_left, pltpu.roll(own_left, W, 1))
    strips[1] = jnp.where(here < 3 * NP, pltpu.roll(own_right, N - 2 * NP, 1), pltpu.roll(from_right, 3 * NP, 1))
    strips[2] = jnp.where(here < NP, pltpu.roll(own_right, N - NP, 1), pltpu.roll(own_left, N // 2, 1))
    pick_row = lax.broadcasted_iota(jnp.int32, (N, N), 0)
    pick_col = lax.broadcasted_iota(jnp.int32, (N, N), 1)
    for i, (first, second, skip) in enumerate(((from_left, own_left, 0), (own_right, from_right, 2))):
        pair = jnp.where(here < W + DEPTH, first, pltpu.roll(second, DEPTH, 1))
        spread = (pick_row == W + skip + pick_col // NP).astype(F32)
        kstrips[i] = jnp.dot(pair, spread, precision=lax.Precision.HIGHEST, preferred_element_type=F32)
    low = lax.axis_index("lon") % 2 == 0
    for slot in range(SLOTS):
        if slot < NP:
            top, bottom = u0[slot, TOP : TOP + 8], u0[slot, TOP + N - 8 : TOP + N]
        else:
            if slot < NP + 3:
                field = strips.at[slot - NP]
            elif slot < NP + 5:
                field = kstrips.at[slot - NP - 3]
            else:
                field = kappa
            top, bottom = field[:8], field[N - 8 :]
        even_ref[slot] = jnp.where(low, bottom, top)
        odd_ref[slot] = jnp.where(low, top, bottom)


def strip_step(k, s, edges, scentre, sweight, start, size):
    rows = slice(start, start + size)
    here = lanes(size)
    now = [s[k, i, rows] for i in range(2)]
    moved = pltpu.roll(now[1], NP - 1, 1)
    edges[k, 0, rows] = jnp.where(here % 2 == 0, now[0], moved)
    edges[k, 1, rows] = jnp.where(here % 2 == 0, moved, now[0])
    if k == DEPTH - 1:
        return
    for i in range(2):
        forth, back = pltpu.roll(now[i], NP, 1), pltpu.roll(now[i], N - NP, 1)
        if k == 0 and i == 0:
            back = jnp.where(here >= N - NP, s[0, 2, rows], back)
        if k == 0 and i == 1:
            forth = jnp.where(here < NP, s[0, 2, rows], forth)
        around = s[k, i, start - 1 : start + size - 1] + s[k, i, start + 1 : start + size + 1]
        s[k + 1, i, rows] = scentre[i, rows] * now[i] - sweight[i, rows] * (around + forth + back)


def applied(fields, edges, centre, weight, k, q, parity, start, size):
    rows = slice(start, start + size)
    here = lanes(size)
    field = fields[k][q, rows]
    edge = pltpu.roll(edges[k, parity, rows], N - NP * 4 - q, 1)
    forth = jnp.where(here == 0, edge, pltpu.roll(field, 1, 1))
    back = jnp.where(here == N - 1, edge, pltpu.roll(field, N - 1, 1))
    around = fields[k][q, start - 1 : start + size - 1] + fields[k][q, start + 1 : start + size + 1]
    return centre[rows] * field - weight[rows] * (around + forth + back)


def folded(value):
    return jnp.sum((value * value).reshape(-1, 8, N), axis=0)


def trace_basis(fields, basis, kappa, q, start, size, fifth):
    rows = slice(start, start + size)
    scale = kappa[start - TOP : start - TOP + size]
    v0, v1, v2, v3, v4 = (field[q, rows] for field in fields)
    one, zero = scale * v1, scale * v0
    for i, value in enumerate((one * (v0 + v0), one * v2 + zero * v3, one * v4 + zero * fifth)):
        base = pl.multiple_of((i * NP + q) * N + (start - TOP), 8)
        basis[pl.ds(base, size)] = value


def block_sums(basis, ids, first, last, unroll):
    block = lax.broadcasted_iota(jnp.int32, (NB, N), 0)

    def blocks(pair, total):
        high, rest, hot = [], [], []
        for row in (2 * pair, 2 * pair + 1):
            data = basis[pl.ds(row, 3 * NP, stride=N)]
            high.append(data.astype(BF16))
            rest.append((data - high[-1].astype(F32)).astype(BF16))
            hot.append((ids[pl.ds(row, 1)] == block).astype(F32).astype(BF16))
        both = jnp.concatenate([jnp.concatenate(high, axis=1), jnp.concatenate(rest, axis=1)], axis=0)
        hot = jnp.concatenate(hot, axis=1)
        return total + lax.dot_general(both, hot, (((1,), (1,)), ((), ())), preferred_element_type=F32)

    total = lax.fori_loop(first // 2, last // 2, blocks, jnp.zeros((6 * NP, NB), F32), unroll=unroll)
    return total[: 3 * NP] + total[3 * NP :]


def inner_kernel(
    u0, kappa, ids_hbm, strips, kstrips,
    u1, u2, u3, u4, s, basis, moments, sums, ids,
    edges, sem, centre, weight, scentre, sweight,
):
    copy = pltpu.make_async_copy(ids_hbm, ids, sem)
    copy.start()
    inner = slice(TOP, TOP + N)
    ocean = u0[0, inner] * u0[0, inner]
    centre[inner] = ocean * (kappa[...] + 0.25)
    weight[inner] = ocean * 0.0625
    s[0, 2, inner] = strips[2]
    for i in range(2):
        s[0, i, inner] = strips[i]
        square = strips[i] * strips[i]
        scentre[i, inner] = square * (kstrips[i] + 0.25)
        sweight[i, inner] = square * 0.0625
    for k in range(DEPTH):
        for start in range(TOP, TOP + N, 32):
            strip_step(k, s, edges, scentre, sweight, start, 32)
    fields = [u0, u1, u2, u3, u4]

    def probe_group(group, carry):
        probes = [(group * TOGETHER + j, j % 2) for j in range(TOGETHER)]
        for k in range(4):
            totals = [jnp.zeros((8, N), F32) for _ in probes]
            for start in range(TOP, TOP + N, CHUNK):
                for j, (q, parity) in enumerate(probes):
                    result = applied(fields, edges, centre, weight, k, q, parity, start, CHUNK)
                    fields[k + 1][q, start : start + CHUNK] = result
                    low, high = max(start, TOP + 8), min(start + CHUNK, TOP + N - 8)
                    totals[j] += folded(result[low - start : high - start])
            for (q, _), total in zip(probes, totals):
                moments[k, q] = total
        totals = [jnp.zeros((8, N), F32) for _ in probes]
        for start in range(TOP + 8, TOP + N - 8, FINAL):
            for j, (q, parity) in enumerate(probes):
                result = applied(fields, edges, centre, weight, 4, q, parity, start, FINAL)
                totals[j] += folded(result)
                trace_basis(fields, basis, kappa, q, start, FINAL, result)
        for (q, _), total in zip(probes, totals):
            moments[4, q] = total
        return carry

    lax.fori_loop(0, NP // TOGETHER, probe_group, 0)
    copy.wait()
    sums[...] = block_sums(basis, ids, 8, N - 8, 14)


def outer_kernel(
    u0_in, u1_in, u2_in, u3_in, u4_in, s_in, basis_in,
    moments, sums, kappa, ids, kstrips, odd, even,
    u0, u1, u2, u3, u4, s, basis, message,
    edges, centre, weight, scentre, sweight,
):
    del u0_in, u1_in, u2_in, u3_in, u4_in, s_in, basis_in
    low = lax.axis_index("lon") % 2 == 0
    bands = (TOP - 8, TOP + N - 8)
    for start, inside, outside, if_low, if_high in (
        (bands[0], 8, 0, odd, even),
        (bands[1], 0, 8, even, odd),
    ):
        rows = slice(start + outside, start + outside + 8)
        own = slice(start + inside, start + inside + 8)
        here = slice(start + inside - TOP, start + inside - TOP + 8)
        halo = [jnp.where(low, if_low[i], if_high[i]) for i in range(SLOTS)]
        for q in range(NP):
            u0[q, rows] = halo[q]
        s[0, 2, rows] = halo[NP + 2]
        for i in range(2):
            s[0, i, rows] = halo[NP + i]
            for where, value, kvalue in ((rows, halo[NP + i], halo[NP + 3 + i]), (own, s[0, i, own], kstrips[i, here])):
                scentre[i, where] = value * value * (kvalue + 0.25)
                sweight[i, where] = value * value * 0.0625
        for where, value, kvalue in ((rows, halo[0], halo[NP + 5]), (own, u0[0, own], kappa[here])):
            centre[where] = value * value * (kvalue + 0.25)
            weight[where] = value * value * 0.0625
    fields = [u0, u1, u2, u3, u4]
    blank = jnp.zeros((8, N), F32)
    for row in (TOP - 16, TOP + N + 8):
        for field in fields:
            for q in range(NP):
                field[q, row : row + 8] = blank
        for k in range(DEPTH):
            for i in range(2):
                s[k, i, row : row + 8] = blank
    for k in range(DEPTH):
        for start in bands:
            strip_step(k, s, edges, scentre, sweight, start, 16)

    heads = []
    for k in range(4):
        stacked = []
        for q in range(NP):
            total = moments[k, q]
            for start, own in ((bands[0], 8), (bands[1], 0)):
                result = applied(fields, edges, centre, weight, k, q, q % 2, start, 16)
                fields[k + 1][q, start : start + 16] = result
                total += folded(result[own : own + 8])
            stacked.append(jnp.sum(total, axis=0, keepdims=True))
        heads.append(jnp.concatenate(stacked, axis=0))
    stacked = []
    for q in range(NP):
        total = moments[4, q]
        for start in (TOP, TOP + N - 8):
            result = applied(fields, edges, centre, weight, 4, q, q % 2, start, 8)
            total += folded(result)
            trace_basis(fields, basis, kappa, q, start, 8, result)
        stacked.append(jnp.sum(total, axis=0, keepdims=True))
    heads.append(jnp.concatenate(stacked, axis=0))
    total = sums[...] + block_sums(basis, ids, 0, 8, 4) + block_sums(basis, ids, N - 8, N, 4)
    ocean = u0[0, TOP : TOP + N]
    ocean = ocean * ocean

    ocean_sum = jnp.sum(jnp.sum(ocean, axis=0, keepdims=True), axis=1, keepdims=True)
    columns = [jnp.broadcast_to(ocean_sum, (NP, 1))]
    columns += [jnp.sum(head, axis=1, keepdims=True) for head in heads]
    wide = jnp.zeros((NP, NB), F32)
    spot = lax.broadcasted_iota(jnp.int32, (NP, NB), 1)
    coarse = F32(1.5 * 2**20)
    for k, column in enumerate(columns):
        head = (column + coarse) - coarse
        wide = jnp.where(spot == 2 * k, head, wide)
        wide = jnp.where(spot == 2 * k + 1, column - head, wide)
    half = 3 * NP // 2
    message[:half] = jnp.concatenate([total[:half], total[half:]], axis=1)
    message[half:] = jnp.concatenate([wide[: NP // 2], wide[NP // 2 :]], axis=1)


def two_sum(a, b):
    s = a + b
    t = s - a
    return s, (a - (s - t)) + (b - t)


def quick(a, b):
    s = a + b
    return s, b - (s - a)


def split(a):
    t = a * F32(4097.0)
    high = t - (t - a)
    return high, a - high


def mul(a, b):
    p = a[0] * b[0]
    ah, al = split(a[0])
    bh, bl = split(b[0])
    e = ((ah * bh - p) + ah * bl + al * bh) + al * bl
    return quick(p, e + (a[0] * b[1] + a[1] * b[0]))


def sub(a, b):
    s, e = two_sum(a[0], -b[0])
    return quick(s, e + (a[1] - b[1]))


def inverse(b):
    first = 1.0 / b[0]
    zero = jnp.zeros_like(first)
    rest = sub((jnp.ones_like(first), zero), mul(b, (first, zero)))
    return quick(first, first * rest[0])


def keep(ok, value, other):
    return tuple(jnp.where(ok, v, other) for v in value)


def solve(moment):
    g0, h1, h2, h3, h4, h5 = moment
    tiny = F32(2e-8)
    over = inverse(h1)
    l1, l2 = mul(h2, over), mul(h3, over)
    s11, s12, s22 = sub(h3, mul(h2, l1)), sub(h4, mul(h2, l2)), sub(h5, mul(h3, l2))
    y1, y2 = sub(h1, mul(g0, l1)), sub(h2, mul(g0, l2))
    ok1 = s11[0] > tiny * h3[0]
    over1 = keep(ok1, inverse(keep(ok1, s11, 1.0)), 0.0)
    l21 = mul(s12, over1)
    d2, z2 = sub(s22, mul(s12, l21)), sub(y2, mul(y1, l21))
    ok2 = ok1 & (d2[0] > tiny * h5[0])
    over2 = keep(ok2, inverse(keep(ok2, d2, 1.0)), 0.0)
    c2 = mul(z2, over2)
    c1 = mul(sub(y1, mul(s12, c2)), over1)
    c0 = mul(sub(sub(g0, mul(h2, c1)), mul(h3, c2)), over)
    return c0[0] + c0[1], c1[0] + c1[1], c2[0] + c2[1]


def combine_kernel(message, u0, u2, u4, basis, solution, trace, traces):
    half = 3 * NP // 2
    wide = jnp.concatenate([message[half:, :NB], message[half:, NB:]], axis=0)
    sums = jnp.concatenate([message[:half, :NB], message[:half, NB:]], axis=0)
    moment = []
    for k in range(6):
        head = wide[:, 2 * k : 2 * k + 1]
        rest = wide[:, 2 * k + 1 : 2 * k + 2]
        moment.append(quick(jnp.broadcast_to(head, (NP, N)), jnp.broadcast_to(rest, (NP, N))))
    c0, c1, c2 = solve(moment)
    cells = F32(N * N * 128 // NB)
    total = c0[:, :NB] * sums[:NP] + c1[:, :NB] * sums[NP : 2 * NP] + c2[:, :NB] * sums[2 * NP :]
    traces[...] = total / cells
    for q in range(NP):
        a0, a1, a2 = (c[q : q + 1] for c in (c0, c1, c2))
        solution[q] = a0 * u0[q, TOP : TOP + N] + a1 * u2[q, TOP : TOP + N] + a2 * u4[q, TOP : TOP + N]
        rows = [slice((i * NP + q) * N, (i * NP + q + 1) * N) for i in range(3)]
        trace[q] = a0 * basis[rows[0]] + a1 * basis[rows[1]] + a2 * basis[rows[2]]


def pairs(count, offset, closed):
    out = []
    for i in range(offset, count, 2):
        j = (i + 1) % count
        if i + 1 < count or closed:
            out += [(i, j), (j, i)]
    return out


def swap(odd, even, axis, closed):
    count = lax.axis_size(axis)
    odd = lax.ppermute(odd, axis, pairs(count, 1, closed))
    even = lax.ppermute(even, axis, pairs(count, 0, closed))
    return odd, even


def everywhere(value):
    def sent(axis, bits):
        return lax.ppermute(value, axis, [(i, i ^ bits) for i in range(lax.axis_size(axis))])

    value = value + sent("lat", 1)
    for axis, unit in (("lat", 2), ("lon", 1), ("lon", 4)):
        near, far, across = sent(axis, unit), sent(axis, 3 * unit), sent(axis, 2 * unit)
        value = (value + near) + (far + across)
    return value


def per_device(signs, mask, kappa, ids):
    edge, field, strip, plane = (N, N), (NP, ROWS, N), (2, ROWS, N), (ROWS, N)
    halo = (SLOTS, 8, N)
    flat = (3 * NP * N, N)
    ints = jax.ShapeDtypeStruct(edge, jnp.int32)
    signs, mask, kappa, ids = (pltpu.with_memory_space_constraint(x, pltpu.HBM) for x in (signs, mask, kappa, ids))
    own_odd, own_even, u0, kappa = call(
        pack_kernel,
        [edge, edge, field, edge],
        8,
        [
            pltpu.VMEM((NP, N, N), jnp.int32),
            pltpu.VMEM(edge, jnp.int32),
            pltpu.VMEM((NP // 2, 2 * N, 2 * N), BF16),
            pltpu.SemaphoreType.DMA((2 + PARTS,)),
        ],
        specs=[FAR] * 3,
    )(signs, mask, kappa)
    odd, even = swap(own_odd, own_even, "lat", False)
    strips, kstrips, row_odd, row_even = call(strips_kernel, [(3, N, N), (2, N, N), halo, halo], 8)(
        odd, even, own_odd, own_even, kappa, u0
    )
    row_odd, row_even = swap(row_odd, row_even, "lon", True)
    coefficients = [pltpu.VMEM(shape, F32) for shape in (plane, plane, strip, strip)]
    edges = pltpu.VMEM((DEPTH, 2, ROWS, N), F32)
    u1, u2, u3, u4, s, basis, moments, sums, ids = call(
        inner_kernel,
        [field, field, field, field, (DEPTH, 3, ROWS, N), flat, (DEPTH, NP, 8, N), (3 * NP, NB), ints],
        24,
        [edges, pltpu.SemaphoreType.DMA, *coefficients],
        specs=[NEAR, NEAR, FAR, NEAR, NEAR],
        micros=8,
    )(u0, kappa, ids, strips, kstrips)
    u0, u1, u2, u3, u4, s, basis, message = call(
        outer_kernel,
        [field, field, field, field, field, (DEPTH, 3, ROWS, N), flat, (2 * NP, N)],
        24,
        [edges, *coefficients],
        aliases={i: i for i in range(7)},
    )(u0, u1, u2, u3, u4, s, basis, moments, sums, kappa, ids, kstrips, row_odd, row_even)
    message = everywhere(message)
    out = (NP, N, N)
    return tuple(call(combine_kernel, [out, out, (NP, NB)], 16)(message, u0, u2, u4, basis))


def solution(mesh):
    placed = (P(None, "lon", "lat"), P("lon", "lat"), P("lon", "lat"), P("lon", "lat"))
    return jax.shard_map(
        per_device,
        mesh=mesh,
        in_specs=placed,
        out_specs=(P(None, "lon", "lat"), P(None, "lon", "lat"), P()),
        check_vma=False,
    )
```

```python
import jax
import jax.numpy as jnp
from jax import lax
from jax.experimental import pallas as pl
from jax.experimental.pallas import tpu as pltpu
from jax.sharding import PartitionSpec as P

F32 = jnp.float32
BF16 = jnp.bfloat16
NB = 64
NP = 16
N = 128
DEPTH = 5
W = DEPTH * NP
SLOTS = NP + 6
TOP = 16
ROWS = N + 2 * TOP
MIB = 1 << 20
FAR = pl.BlockSpec(memory_space=pltpu.HBM)
NEAR = pl.BlockSpec(memory_space=pltpu.VMEM)
CHUNK = 32
FINAL = 56
PITCH = N + 8
UNROLL = 14
ABREAST = 4
TOGETHER = 8
PARTS = 4


def lanes(rows=8):
    return lax.broadcasted_iota(jnp.int32, (rows, N), 1)


def call(kernel, outs, mib, scratch=(), aliases=None, specs=None, micros=1):
    extra = {} if specs is None else {"in_specs": specs}
    return pl.pallas_call(
        kernel,
        out_shape=[o if isinstance(o, jax.ShapeDtypeStruct) else jax.ShapeDtypeStruct(o, F32) for o in outs],
        scratch_shapes=list(scratch),
        input_output_aliases=aliases or {},
        compiler_params=pltpu.CompilerParams(vmem_limit_bytes=mib * MIB),
        cost_estimate=pl.CostEstimate(flops=0, bytes_accessed=micros * 3_000_000, transcendentals=0),
        **extra,
    )


def pack_kernel(
    signs_hbm, mask_hbm, kappa_hbm,
    odd_ref, even_ref, u0, kappa,
    signs, mask, picks, sems,
):
    part = NP // PARTS
    copies = [
        pltpu.make_async_copy(mask_hbm, mask, sems.at[0]),
        pltpu.make_async_copy(kappa_hbm, kappa, sems.at[1]),
    ]
    for i in range(PARTS):
        probes = pl.ds(i * part, part)
        copies.append(pltpu.make_async_copy(signs_hbm.at[probes], signs.at[probes], sems.at[2 + i]))
    for copy in (copies[0], *copies[2:], copies[1]):
        copy.start()
    lane = lax.broadcasted_iota(jnp.int32, (1, 2 * N), 1)
    side, spot = lane // N, lane % N
    column, probe = spot // NP, spot % NP
    row = lax.broadcasted_iota(jnp.int32, (2 * N, 2 * N), 0)
    for pair in range(NP // 2):
        source = column + (N - DEPTH) * side + N * (probe - 2 * pair)
        wanted = (probe // 2 == pair) & (column < DEPTH)
        source = jnp.where(wanted, source, -1)
        picks[pair] = (row == source).astype(F32).astype(BF16)
    total = jnp.zeros((N, 2 * N), F32)
    copies[0].wait()
    ocean = mask[...].astype(F32)
    for pair in range(NP // 2):
        if pair % (part // 2) == 0:
            copies[2 + pair // (part // 2)].wait()
        fields = []
        for q in (2 * pair, 2 * pair + 1):
            field = signs[q].astype(F32) * ocean
            u0[q, TOP : TOP + N] = field
            fields.append(field.astype(BF16))
        total += jnp.dot(jnp.concatenate(fields, axis=1), picks[pair], preferred_element_type=F32)
    here = lanes(N)
    in_kappa = (here >= W) & (here < W + DEPTH)
    copies[1].wait()
    left = jnp.where(in_kappa, pltpu.roll(kappa[...], W, 1), total[:, :N])
    right = jnp.where(in_kappa, pltpu.roll(kappa[...], W + DEPTH, 1), total[:, N:])
    low = lax.axis_index("lat") % 2 == 0
    even_ref[...] = jnp.where(low, right, left)
    odd_ref[...] = jnp.where(low, left, right)


def strips_kernel(odd, even, own_odd, own_even, kappa, u0, strips, kstrips, odd_ref, even_ref):
    low = lax.axis_index("lat") % 2 == 0
    from_left = jnp.where(low, odd[...], even[...])
    from_right = jnp.where(low, even[...], odd[...])
    own_left = jnp.where(low, own_odd[...], own_even[...])
    own_right = jnp.where(low, own_even[...], own_odd[...])
    here = lanes(N)
    strips[0] = jnp.where(here < W, from_left, pltpu.roll(own_left, W, 1))
    strips[1] = jnp.where(here < 3 * NP, pltpu.roll(own_right, N - 2 * NP, 1), pltpu.roll(from_right, 3 * NP, 1))
    strips[2] = jnp.where(here < NP, pltpu.roll(own_right, N - NP, 1), pltpu.roll(own_left, N // 2, 1))
    pick_row = lax.broadcasted_iota(jnp.int32, (N, N), 0)
    pick_col = lax.broadcasted_iota(jnp.int32, (N, N), 1)
    for i, (first, second, skip) in enumerate(((from_left, own_left, 0), (own_right, from_right, 2))):
        pair = jnp.where(here < W + DEPTH, first, pltpu.roll(second, DEPTH, 1))
        spread = (pick_row == W + skip + pick_col // NP).astype(F32)
        kstrips[i] = jnp.dot(pair, spread, precision=lax.Precision.HIGHEST, preferred_element_type=F32)
    low = lax.axis_index("lon") % 2 == 0
    for slot in range(SLOTS):
        if slot < NP:
            top, bottom = u0[slot, TOP : TOP + 8], u0[slot, TOP + N - 8 : TOP + N]
        else:
            if slot < NP + 3:
                field = strips.at[slot - NP]
            elif slot < NP + 5:
                field = kstrips.at[slot - NP - 3]
            else:
                field = kappa
            top, bottom = field[:8], field[N - 8 :]
        even_ref[slot] = jnp.where(low, bottom, top)
        odd_ref[slot] = jnp.where(low, top, bottom)


def strip_step(k, s, edges, scentre, sweight, start, size):
    rows = slice(start, start + size)
    here = lanes(size)
    now = [s[k, i, rows] for i in range(2)]
    moved = pltpu.roll(now[1], NP - 1, 1)
    edges[k, 0, rows] = jnp.where(here % 2 == 0, now[0], moved)
    edges[k, 1, rows] = jnp.where(here % 2 == 0, moved, now[0])
    if k == DEPTH - 1:
        return
    for i in range(2):
        forth, back = pltpu.roll(now[i], NP, 1), pltpu.roll(now[i], N - NP, 1)
        if k == 0 and i == 0:
            back = jnp.where(here >= N - NP, s[0, 2, rows], back)
        if k == 0 and i == 1:
            forth = jnp.where(here < NP, s[0, 2, rows], forth)
        around = s[k, i, start - 1 : start + size - 1] + s[k, i, start + 1 : start + size + 1]
        s[k + 1, i, rows] = scentre[i, rows] * now[i] - sweight[i, rows] * (around + forth + back)


def applied(fields, edges, centre, weight, k, q, parity, start, size):
    rows = slice(start, start + size)
    here = lanes(size)
    field = fields[k][q, rows]
    edge = pltpu.roll(edges[k, parity, rows], N - NP * 4 - q, 1)
    forth = jnp.where(here == 0, edge, pltpu.roll(field, 1, 1))
    back = jnp.where(here == N - 1, edge, pltpu.roll(field, N - 1, 1))
    around = fields[k][q, start - 1 : start + size - 1] + fields[k][q, start + 1 : start + size + 1]
    return centre[rows] * field - weight[rows] * (around + forth + back)


def folded(value):
    return jnp.sum((value * value).reshape(-1, 8, N), axis=0)


def trace_basis(fields, basis, kappa, q, start, size, fifth):
    rows = slice(start, start + size)
    scale = kappa[start - TOP : start - TOP + size]
    v0, v1, v2, v3, v4 = (field[q, rows] for field in fields)
    one, zero = scale * v1, scale * v0
    for i, value in enumerate((one * (v0 + v0), one * v2 + zero * v3, one * v4 + zero * fifth)):
        base = pl.multiple_of((i * NP + q) * PITCH + (start - TOP), 8)
        basis[pl.ds(base, size)] = value


def block_sums(basis, ids, first, last, unroll):
    block = lax.broadcasted_iota(jnp.int32, (NB, N), 0)

    def blocks(step, total):
        high, rest, hot = [], [], []
        for row in [step * ABREAST + i for i in range(ABREAST)]:
            data = basis[pl.ds(row, 3 * NP, stride=PITCH)]
            high.append(data.astype(BF16))
            rest.append((data - high[-1].astype(F32)).astype(BF16))
            hot.append((ids[pl.ds(row, 1)] == block).astype(F32).astype(BF16))
        both = jnp.concatenate([jnp.concatenate(high, axis=1), jnp.concatenate(rest, axis=1)], axis=0)
        hot = jnp.concatenate(hot, axis=1)
        return total + lax.dot_general(both, hot, (((1,), (1,)), ((), ())), preferred_element_type=F32)

    total = lax.fori_loop(first // ABREAST, last // ABREAST, blocks, jnp.zeros((6 * NP, NB), F32), unroll=unroll)
    return total[: 3 * NP] + total[3 * NP :]


def inner_kernel(
    u0, kappa, ids_hbm, strips, kstrips,
    u1, u2, u3, u4, s, basis, moments, sums, ids,
    edges, sem, centre, weight, scentre, sweight,
):
    copy = pltpu.make_async_copy(ids_hbm, ids, sem)
    copy.start()
    inner = slice(TOP, TOP + N)
    ocean = u0[0, inner] * u0[0, inner]
    centre[inner] = ocean * (kappa[...] + 0.25)
    weight[inner] = ocean * 0.0625
    s[0, 2, inner] = strips[2]
    for i in range(2):
        s[0, i, inner] = strips[i]
        square = strips[i] * strips[i]
        scentre[i, inner] = square * (kstrips[i] + 0.25)
        sweight[i, inner] = square * 0.0625
    for k in range(DEPTH):
        for start in range(TOP, TOP + N, 32):
            strip_step(k, s, edges, scentre, sweight, start, 32)
    fields = [u0, u1, u2, u3, u4]

    def probe_group(group, carry):
        probes = [(group * TOGETHER + j, j % 2) for j in range(TOGETHER)]
        for k in range(4):
            totals = [jnp.zeros((8, N), F32) for _ in probes]
            for start in range(TOP, TOP + N, CHUNK):
                for j, (q, parity) in enumerate(probes):
                    result = applied(fields, edges, centre, weight, k, q, parity, start, CHUNK)
                    fields[k + 1][q, start : start + CHUNK] = result
                    low, high = max(start, TOP + 8), min(start + CHUNK, TOP + N - 8)
                    totals[j] += folded(result[low - start : high - start])
            for (q, _), total in zip(probes, totals):
                moments[k, q] = total
        totals = [jnp.zeros((8, N), F32) for _ in probes]
        for start in range(TOP + 8, TOP + N - 8, FINAL):
            for j, (q, parity) in enumerate(probes):
                result = applied(fields, edges, centre, weight, 4, q, parity, start, FINAL)
                totals[j] += folded(result)
                trace_basis(fields, basis, kappa, q, start, FINAL, result)
        for (q, _), total in zip(probes, totals):
            moments[4, q] = total
        return carry

    lax.fori_loop(0, NP // TOGETHER, probe_group, 0)
    copy.wait()
    sums[...] = block_sums(basis, ids, 8, N - 8, UNROLL)


def outer_kernel(
    u0_in, u1_in, u2_in, u3_in, u4_in, s_in, basis_in,
    moments, sums, kappa, ids, kstrips, odd, even,
    u0, u1, u2, u3, u4, s, basis, message,
    edges, centre, weight, scentre, sweight,
):
    del u0_in, u1_in, u2_in, u3_in, u4_in, s_in, basis_in
    low = lax.axis_index("lon") % 2 == 0
    bands = (TOP - 8, TOP + N - 8)
    for start, inside, outside, if_low, if_high in (
        (bands[0], 8, 0, odd, even),
        (bands[1], 0, 8, even, odd),
    ):
        rows = slice(start + outside, start + outside + 8)
        own = slice(start + inside, start + inside + 8)
        here = slice(start + inside - TOP, start + inside - TOP + 8)
        halo = [jnp.where(low, if_low[i], if_high[i]) for i in range(SLOTS)]
        for q in range(NP):
            u0[q, rows] = halo[q]
        s[0, 2, rows] = halo[NP + 2]
        for i in range(2):
            s[0, i, rows] = halo[NP + i]
            for where, value, kvalue in ((rows, halo[NP + i], halo[NP + 3 + i]), (own, s[0, i, own], kstrips[i, here])):
                scentre[i, where] = value * value * (kvalue + 0.25)
                sweight[i, where] = value * value * 0.0625
        for where, value, kvalue in ((rows, halo[0], halo[NP + 5]), (own, u0[0, own], kappa[here])):
            centre[where] = value * value * (kvalue + 0.25)
            weight[where] = value * value * 0.0625
    fields = [u0, u1, u2, u3, u4]
    blank = jnp.zeros((8, N), F32)
    for row in (TOP - 16, TOP + N + 8):
        for field in fields:
            for q in range(NP):
                field[q, row : row + 8] = blank
        for k in range(DEPTH):
            for i in range(2):
                s[k, i, row : row + 8] = blank
    for k in range(DEPTH):
        for start in bands:
            strip_step(k, s, edges, scentre, sweight, start, 16)

    heads = []
    for k in range(4):
        stacked = []
        for q in range(NP):
            total = moments[k, q]
            for start, own in ((bands[0], 8), (bands[1], 0)):
                result = applied(fields, edges, centre, weight, k, q, q % 2, start, 16)
                fields[k + 1][q, start : start + 16] = result
                total += folded(result[own : own + 8])
            stacked.append(jnp.sum(total, axis=0, keepdims=True))
        heads.append(jnp.concatenate(stacked, axis=0))
    stacked = []
    for q in range(NP):
        total = moments[4, q]
        for start in (TOP, TOP + N - 8):
            result = applied(fields, edges, centre, weight, 4, q, q % 2, start, 8)
            total += folded(result)
            trace_basis(fields, basis, kappa, q, start, 8, result)
        stacked.append(jnp.sum(total, axis=0, keepdims=True))
    heads.append(jnp.concatenate(stacked, axis=0))
    total = sums[...] + block_sums(basis, ids, 0, 8, 8 // ABREAST) + block_sums(basis, ids, N - 8, N, 8 // ABREAST)
    ocean = u0[0, TOP : TOP + N]
    ocean = ocean * ocean

    ocean_sum = jnp.sum(jnp.sum(ocean, axis=0, keepdims=True), axis=1, keepdims=True)
    columns = [jnp.broadcast_to(ocean_sum, (NP, 1))]
    columns += [jnp.sum(head, axis=1, keepdims=True) for head in heads]
    wide = jnp.zeros((NP, NB), F32)
    spot = lax.broadcasted_iota(jnp.int32, (NP, NB), 1)
    coarse = F32(1.5 * 2**20)
    for k, column in enumerate(columns):
        head = (column + coarse) - coarse
        wide = jnp.where(spot == 2 * k, head, wide)
        wide = jnp.where(spot == 2 * k + 1, column - head, wide)
    half = 3 * NP // 2
    message[:half] = jnp.concatenate([total[:half], total[half:]], axis=1)
    message[half:] = jnp.concatenate([wide[: NP // 2], wide[NP // 2 :]], axis=1)


def two_sum(a, b):
    s = a + b
    t = s - a
    return s, (a - (s - t)) + (b - t)


def quick(a, b):
    s = a + b
    return s, b - (s - a)


def split(a):
    t = a * F32(4097.0)
    high = t - (t - a)
    return high, a - high


def mul(a, b):
    p = a[0] * b[0]
    ah, al = split(a[0])
    bh, bl = split(b[0])
    e = ((ah * bh - p) + ah * bl + al * bh) + al * bl
    return quick(p, e + (a[0] * b[1] + a[1] * b[0]))


def sub(a, b):
    s, e = two_sum(a[0], -b[0])
    return quick(s, e + (a[1] - b[1]))


def inverse(b):
    first = 1.0 / b[0]
    zero = jnp.zeros_like(first)
    rest = sub((jnp.ones_like(first), zero), mul(b, (first, zero)))
    return quick(first, first * rest[0])


def keep(ok, value, other):
    return tuple(jnp.where(ok, v, other) for v in value)


def solve(moment):
    g0, h1, h2, h3, h4, h5 = moment
    tiny = F32(2e-8)
    over = inverse(h1)
    l1, l2 = mul(h2, over), mul(h3, over)
    s11, s12, s22 = sub(h3, mul(h2, l1)), sub(h4, mul(h2, l2)), sub(h5, mul(h3, l2))
    y1, y2 = sub(h1, mul(g0, l1)), sub(h2, mul(g0, l2))
    ok1 = s11[0] > tiny * h3[0]
    over1 = keep(ok1, inverse(keep(ok1, s11, 1.0)), 0.0)
    l21 = mul(s12, over1)
    d2, z2 = sub(s22, mul(s12, l21)), sub(y2, mul(y1, l21))
    ok2 = ok1 & (d2[0] > tiny * h5[0])
    over2 = keep(ok2, inverse(keep(ok2, d2, 1.0)), 0.0)
    c2 = mul(z2, over2)
    c1 = mul(sub(y1, mul(s12, c2)), over1)
    c0 = mul(sub(sub(g0, mul(h2, c1)), mul(h3, c2)), over)
    return c0[0] + c0[1], c1[0] + c1[1], c2[0] + c2[1]


def combine_kernel(message, u0, u2, u4, basis, solution, trace, traces):
    half = 3 * NP // 2
    wide = jnp.concatenate([message[half:, :NB], message[half:, NB:]], axis=0)
    sums = jnp.concatenate([message[:half, :NB], message[:half, NB:]], axis=0)
    moment = []
    for k in range(6):
        head = wide[:, 2 * k : 2 * k + 1]
        rest = wide[:, 2 * k + 1 : 2 * k + 2]
        moment.append(quick(jnp.broadcast_to(head, (NP, N)), jnp.broadcast_to(rest, (NP, N))))
    c0, c1, c2 = solve(moment)
    cells = F32(N * N * 128 // NB)
    total = c0[:, :NB] * sums[:NP] + c1[:, :NB] * sums[NP : 2 * NP] + c2[:, :NB] * sums[2 * NP :]
    traces[...] = total / cells
    for q in range(NP):
        a0, a1, a2 = (c[q : q + 1] for c in (c0, c1, c2))
        solution[q] = a0 * u0[q, TOP : TOP + N] + a1 * u2[q, TOP : TOP + N] + a2 * u4[q, TOP : TOP + N]
        rows = [slice((i * NP + q) * PITCH, (i * NP + q) * PITCH + N) for i in range(3)]
        trace[q] = a0 * basis[rows[0]] + a1 * basis[rows[1]] + a2 * basis[rows[2]]


def pairs(count, offset, closed):
    out = []
    for i in range(offset, count, 2):
        j = (i + 1) % count
        if i + 1 < count or closed:
            out += [(i, j), (j, i)]
    return out


def swap(odd, even, axis, closed):
    count = lax.axis_size(axis)
    odd = lax.ppermute(odd, axis, pairs(count, 1, closed))
    even = lax.ppermute(even, axis, pairs(count, 0, closed))
    return odd, even


def everywhere(value):
    def sent(axis, bits):
        return lax.ppermute(value, axis, [(i, i ^ bits) for i in range(lax.axis_size(axis))])

    value = value + sent("lat", 1)
    for axis, unit in (("lat", 2), ("lon", 1), ("lon", 4)):
        near, far, across = sent(axis, unit), sent(axis, 3 * unit), sent(axis, 2 * unit)
        value = (value + near) + (far + across)
    return value


def per_device(signs, mask, kappa, ids):
    edge, field, strip, plane = (N, N), (NP, ROWS, N), (2, ROWS, N), (ROWS, N)
    halo = (SLOTS, 8, N)
    flat = (3 * NP * PITCH, N)
    ints = jax.ShapeDtypeStruct(edge, jnp.int32)
    signs, mask, kappa, ids = (pltpu.with_memory_space_constraint(x, pltpu.HBM) for x in (signs, mask, kappa, ids))
    own_odd, own_even, u0, kappa = call(
        pack_kernel,
        [edge, edge, field, edge],
        8,
        [
            pltpu.VMEM((NP, N, N), jnp.int32),
            pltpu.VMEM(edge, jnp.int32),
            pltpu.VMEM((NP // 2, 2 * N, 2 * N), BF16),
            pltpu.SemaphoreType.DMA((2 + PARTS,)),
        ],
        specs=[FAR] * 3,
    )(signs, mask, kappa)
    odd, even = swap(own_odd, own_even, "lat", False)
    strips, kstrips, row_odd, row_even = call(strips_kernel, [(3, N, N), (2, N, N), halo, halo], 8)(
        odd, even, own_odd, own_even, kappa, u0
    )
    row_odd, row_even = swap(row_odd, row_even, "lon", True)
    coefficients = [pltpu.VMEM(shape, F32) for shape in (plane, plane, strip, strip)]
    edges = pltpu.VMEM((DEPTH, 2, ROWS, N), F32)
    u1, u2, u3, u4, s, basis, moments, sums, ids = call(
        inner_kernel,
        [field, field, field, field, (DEPTH, 3, ROWS, N), flat, (DEPTH, NP, 8, N), (3 * NP, NB), ints],
        24,
        [edges, pltpu.SemaphoreType.DMA, *coefficients],
        specs=[NEAR, NEAR, FAR, NEAR, NEAR],
        micros=8,
    )(u0, kappa, ids, strips, kstrips)
    u0, u1, u2, u3, u4, s, basis, message = call(
        outer_kernel,
        [field, field, field, field, field, (DEPTH, 3, ROWS, N), flat, (2 * NP, N)],
        24,
        [edges, *coefficients],
        aliases={i: i for i in range(7)},
    )(u0, u1, u2, u3, u4, s, basis, moments, sums, kappa, ids, kstrips, row_odd, row_even)
    message = everywhere(message)
    out = (NP, N, N)
    return tuple(call(combine_kernel, [out, out, (NP, NB)], 16)(message, u0, u2, u4, basis))


def solution(mesh):
    placed = (P(None, "lon", "lat"), P("lon", "lat"), P("lon", "lat"), P("lon", "lat"))
    return jax.shard_map(
        per_device,
        mesh=mesh,
        in_specs=placed,
        out_specs=(P(None, "lon", "lat"), P(None, "lon", "lat"), P()),
        check_vma=False,
    )
```

```python
import jax
import jax.numpy as jnp
from jax import lax
from jax.experimental import pallas as pl
from jax.experimental.pallas import tpu as pltpu
from jax.sharding import PartitionSpec as P

F32 = jnp.float32
BF16 = jnp.bfloat16
NB = 64
NP = 16
N = 128
DEPTH = 5
W = DEPTH * NP
SLOTS = NP + 6
TOP = 16
ROWS = N + 2 * TOP
MIB = 1 << 20
FAR = pl.BlockSpec(memory_space=pltpu.HBM)
NEAR = pl.BlockSpec(memory_space=pltpu.VMEM)
CHUNK = 32
FINAL = 56
PITCH = N + 8
UNROLL = 14
ABREAST = 4
TOGETHER = 8
PARTS = 4


def lanes(rows=8):
    return lax.broadcasted_iota(jnp.int32, (rows, N), 1)


def call(kernel, outs, mib, scratch=(), aliases=None, specs=None, micros=1):
    extra = {} if specs is None else {"in_specs": specs}
    return pl.pallas_call(
        kernel,
        out_shape=[o if isinstance(o, jax.ShapeDtypeStruct) else jax.ShapeDtypeStruct(o, F32) for o in outs],
        scratch_shapes=list(scratch),
        input_output_aliases=aliases or {},
        compiler_params=pltpu.CompilerParams(vmem_limit_bytes=mib * MIB),
        cost_estimate=pl.CostEstimate(flops=0, bytes_accessed=micros * 3_000_000, transcendentals=0),
        **extra,
    )


def pack_kernel(
    signs_hbm, mask_hbm, kappa_hbm,
    odd_ref, even_ref, u0, kappa,
    signs, mask, picks, sems,
):
    part = NP // PARTS
    copies = [
        pltpu.make_async_copy(mask_hbm, mask, sems.at[0]),
        pltpu.make_async_copy(kappa_hbm, kappa, sems.at[1]),
    ]
    for i in range(PARTS):
        probes = pl.ds(i * part, part)
        copies.append(pltpu.make_async_copy(signs_hbm.at[probes], signs.at[probes], sems.at[2 + i]))
    for copy in (copies[0], *copies[2:], copies[1]):
        copy.start()
    lane = lax.broadcasted_iota(jnp.int32, (1, 2 * N), 1)
    side, spot = lane // N, lane % N
    column, probe = spot // NP, spot % NP
    row = lax.broadcasted_iota(jnp.int32, (2 * N, 2 * N), 0)
    for pair in range(NP // 2):
        source = column + (N - DEPTH) * side + N * (probe - 2 * pair)
        wanted = (probe // 2 == pair) & (column < DEPTH)
        source = jnp.where(wanted, source, -1)
        picks[pair] = (row == source).astype(F32).astype(BF16)
    total = jnp.zeros((N, 2 * N), F32)
    copies[0].wait()
    ocean = mask[...].astype(F32)
    for pair in range(NP // 2):
        if pair % (part // 2) == 0:
            copies[2 + pair // (part // 2)].wait()
        fields = []
        for q in (2 * pair, 2 * pair + 1):
            field = signs[q].astype(F32) * ocean
            u0[q, TOP : TOP + N] = field
            fields.append(field.astype(BF16))
        total += jnp.dot(jnp.concatenate(fields, axis=1), picks[pair], preferred_element_type=F32)
    here = lanes(N)
    in_kappa = (here >= W) & (here < W + DEPTH)
    copies[1].wait()
    left = jnp.where(in_kappa, pltpu.roll(kappa[...], W, 1), total[:, :N])
    right = jnp.where(in_kappa, pltpu.roll(kappa[...], W + DEPTH, 1), total[:, N:])
    low = lax.axis_index("lat") % 2 == 0
    even_ref[...] = jnp.where(low, right, left)
    odd_ref[...] = jnp.where(low, left, right)


def strips_kernel(odd, even, own_odd, own_even, kappa, u0, strips, kstrips, odd_ref, even_ref):
    low = lax.axis_index("lat") % 2 == 0
    from_left = jnp.where(low, odd[...], even[...])
    from_right = jnp.where(low, even[...], odd[...])
    own_left = jnp.where(low, own_odd[...], own_even[...])
    own_right = jnp.where(low, own_even[...], own_odd[...])
    here = lanes(N)
    strips[0] = jnp.where(here < W, from_left, pltpu.roll(own_left, W, 1))
    strips[1] = jnp.where(here < 3 * NP, pltpu.roll(own_right, N - 2 * NP, 1), pltpu.roll(from_right, 3 * NP, 1))
    strips[2] = jnp.where(here < NP, pltpu.roll(own_right, N - NP, 1), pltpu.roll(own_left, N // 2, 1))
    pick_row = lax.broadcasted_iota(jnp.int32, (N, N), 0)
    pick_col = lax.broadcasted_iota(jnp.int32, (N, N), 1)
    for i, (first, second, skip) in enumerate(((from_left, own_left, 0), (own_right, from_right, 2))):
        pair = jnp.where(here < W + DEPTH, first, pltpu.roll(second, DEPTH, 1))
        spread = (pick_row == W + skip + pick_col // NP).astype(F32)
        kstrips[i] = jnp.dot(pair, spread, precision=lax.Precision.HIGHEST, preferred_element_type=F32)
    low = lax.axis_index("lon") % 2 == 0
    for slot in range(SLOTS):
        if slot < NP:
            top, bottom = u0[slot, TOP : TOP + 8], u0[slot, TOP + N - 8 : TOP + N]
        else:
            if slot < NP + 3:
                field = strips.at[slot - NP]
            elif slot < NP + 5:
                field = kstrips.at[slot - NP - 3]
            else:
                field = kappa
            top, bottom = field[:8], field[N - 8 :]
        even_ref[slot] = jnp.where(low, bottom, top)
        odd_ref[slot] = jnp.where(low, top, bottom)


def strip_step(k, s, edges, scentre, sweight, start, size):
    rows = slice(start, start + size)
    here = lanes(size)
    now = [s[k, i, rows] for i in range(2)]
    moved = pltpu.roll(now[1], NP - 1, 1)
    edges[k, 0, rows] = jnp.where(here % 2 == 0, now[0], moved)
    edges[k, 1, rows] = jnp.where(here % 2 == 0, moved, now[0])
    if k == DEPTH - 1:
        return
    for i in range(2):
        forth, back = pltpu.roll(now[i], NP, 1), pltpu.roll(now[i], N - NP, 1)
        if k == 0 and i == 0:
            back = jnp.where(here >= N - NP, s[0, 2, rows], back)
        if k == 0 and i == 1:
            forth = jnp.where(here < NP, s[0, 2, rows], forth)
        around = s[k, i, start - 1 : start + size - 1] + s[k, i, start + 1 : start + size + 1]
        s[k + 1, i, rows] = scentre[i, rows] * now[i] - sweight[i, rows] * (around + forth + back)


def applied(fields, edges, centre, weight, k, q, parity, start, size):
    rows = slice(start, start + size)
    here = lanes(size)
    field = fields[k][q, rows]
    edge = pltpu.roll(edges[k, parity, rows], N - NP * 4 - q, 1)
    forth = jnp.where(here == 0, edge, pltpu.roll(field, 1, 1))
    back = jnp.where(here == N - 1, edge, pltpu.roll(field, N - 1, 1))
    around = fields[k][q, start - 1 : start + size - 1] + fields[k][q, start + 1 : start + size + 1]
    return centre[rows] * field - weight[rows] * (around + forth + back)


def completed(u1, edges, weight, q, parity, start, size):
    rows = slice(start, start + size)
    here = lanes(size)
    edge = pltpu.roll(edges[0, parity, rows], N - NP * 4 - q, 1)
    edge = jnp.where((here == 0) | (here == N - 1), edge, 0.0)
    return u1[q, rows] - weight[rows] * edge


def folded(value):
    return jnp.sum((value * value).reshape(-1, 8, N), axis=0)


def trace_basis(fields, basis, kappa, q, start, size, fifth):
    rows = slice(start, start + size)
    scale = kappa[start - TOP : start - TOP + size]
    v0, v1, v2, v3, v4 = (field[q, rows] for field in fields)
    one, zero = scale * v1, scale * v0
    for i, value in enumerate((one * (v0 + v0), one * v2 + zero * v3, one * v4 + zero * fifth)):
        base = pl.multiple_of((i * NP + q) * PITCH + (start - TOP), 8)
        basis[pl.ds(base, size)] = value


def block_sums(basis, ids, first, last, unroll):
    block = lax.broadcasted_iota(jnp.int32, (NB, N), 0)

    def blocks(step, total):
        high, rest, hot = [], [], []
        for row in [step * ABREAST + i for i in range(ABREAST)]:
            data = basis[pl.ds(row, 3 * NP, stride=PITCH)]
            high.append(data.astype(BF16))
            rest.append((data - high[-1].astype(F32)).astype(BF16))
            hot.append((ids[pl.ds(row, 1)] == block).astype(F32).astype(BF16))
        both = jnp.concatenate([jnp.concatenate(high, axis=1), jnp.concatenate(rest, axis=1)], axis=0)
        hot = jnp.concatenate(hot, axis=1)
        return total + lax.dot_general(both, hot, (((1,), (1,)), ((), ())), preferred_element_type=F32)

    total = lax.fori_loop(first // ABREAST, last // ABREAST, blocks, jnp.zeros((6 * NP, NB), F32), unroll=unroll)
    return total[: 3 * NP] + total[3 * NP :]


def first_kernel(u0, kappa, ids_hbm, u1, centre, weight, ids, sem):
    copy = pltpu.make_async_copy(ids_hbm, ids, sem)
    copy.start()
    inner = slice(TOP, TOP + N)
    ocean = u0[0, inner] * u0[0, inner]
    centre[inner] = ocean * (kappa[...] + 0.25)
    weight[inner] = ocean * 0.0625
    here = lanes(CHUNK)

    def probe_group(group, carry):
        for start in range(TOP, TOP + N, CHUNK):
            for j in range(TOGETHER):
                q = group * TOGETHER + j
                field = u0[q, start : start + CHUNK]
                forth = jnp.where(here == 0, 0.0, pltpu.roll(field, 1, 1))
                back = jnp.where(here == N - 1, 0.0, pltpu.roll(field, N - 1, 1))
                around = u0[q, start - 1 : start + CHUNK - 1] + u0[q, start + 1 : start + CHUNK + 1] + forth + back
                rows = slice(start, start + CHUNK)
                u1[q, rows] = centre[rows] * field - weight[rows] * around
        return carry

    lax.fori_loop(0, NP // TOGETHER, probe_group, 0)
    copy.wait()


def inner_kernel(
    u1_in, u0, kappa, ids, strips, kstrips, centre, weight,
    u1, u2, u3, u4, s, basis, moments, sums,
    edges, scentre, sweight,
):
    del u1_in
    inner = slice(TOP, TOP + N)
    s[0, 2, inner] = strips[2]
    for i in range(2):
        s[0, i, inner] = strips[i]
        square = strips[i] * strips[i]
        scentre[i, inner] = square * (kstrips[i] + 0.25)
        sweight[i, inner] = square * 0.0625
    for k in range(DEPTH):
        for start in range(TOP, TOP + N, 32):
            strip_step(k, s, edges, scentre, sweight, start, 32)
    fields = [u0, u1, u2, u3, u4]

    def probe_group(group, carry):
        probes = [(group * TOGETHER + j, j % 2) for j in range(TOGETHER)]
        for k in range(4):
            totals = [jnp.zeros((8, N), F32) for _ in probes]
            for start in range(TOP, TOP + N, CHUNK):
                for j, (q, parity) in enumerate(probes):
                    if k == 0:
                        result = completed(u1, edges, weight, q, parity, start, CHUNK)
                    else:
                        result = applied(fields, edges, centre, weight, k, q, parity, start, CHUNK)
                    fields[k + 1][q, start : start + CHUNK] = result
                    low, high = max(start, TOP + 8), min(start + CHUNK, TOP + N - 8)
                    totals[j] += folded(result[low - start : high - start])
            for (q, _), total in zip(probes, totals):
                moments[k, q] = total
        totals = [jnp.zeros((8, N), F32) for _ in probes]
        for start in range(TOP + 8, TOP + N - 8, FINAL):
            for j, (q, parity) in enumerate(probes):
                result = applied(fields, edges, centre, weight, 4, q, parity, start, FINAL)
                totals[j] += folded(result)
                trace_basis(fields, basis, kappa, q, start, FINAL, result)
        for (q, _), total in zip(probes, totals):
            moments[4, q] = total
        return carry

    lax.fori_loop(0, NP // TOGETHER, probe_group, 0)
    sums[...] = block_sums(basis, ids, 8, N - 8, UNROLL)


def outer_kernel(
    u0_in, u1_in, u2_in, u3_in, u4_in, s_in, basis_in,
    moments, sums, kappa, ids, kstrips, odd, even,
    u0, u1, u2, u3, u4, s, basis, message,
    edges, centre, weight, scentre, sweight,
):
    del u0_in, u1_in, u2_in, u3_in, u4_in, s_in, basis_in
    low = lax.axis_index("lon") % 2 == 0
    bands = (TOP - 8, TOP + N - 8)
    for start, inside, outside, if_low, if_high in (
        (bands[0], 8, 0, odd, even),
        (bands[1], 0, 8, even, odd),
    ):
        rows = slice(start + outside, start + outside + 8)
        own = slice(start + inside, start + inside + 8)
        here = slice(start + inside - TOP, start + inside - TOP + 8)
        halo = [jnp.where(low, if_low[i], if_high[i]) for i in range(SLOTS)]
        for q in range(NP):
            u0[q, rows] = halo[q]
        s[0, 2, rows] = halo[NP + 2]
        for i in range(2):
            s[0, i, rows] = halo[NP + i]
            for where, value, kvalue in ((rows, halo[NP + i], halo[NP + 3 + i]), (own, s[0, i, own], kstrips[i, here])):
                scentre[i, where] = value * value * (kvalue + 0.25)
                sweight[i, where] = value * value * 0.0625
        for where, value, kvalue in ((rows, halo[0], halo[NP + 5]), (own, u0[0, own], kappa[here])):
            centre[where] = value * value * (kvalue + 0.25)
            weight[where] = value * value * 0.0625
    fields = [u0, u1, u2, u3, u4]
    blank = jnp.zeros((8, N), F32)
    for row in (TOP - 16, TOP + N + 8):
        for field in fields:
            for q in range(NP):
                field[q, row : row + 8] = blank
        for k in range(DEPTH):
            for i in range(2):
                s[k, i, row : row + 8] = blank
    for k in range(DEPTH):
        for start in bands:
            strip_step(k, s, edges, scentre, sweight, start, 16)

    heads = []
    for k in range(4):
        stacked = []
        for q in range(NP):
            total = moments[k, q]
            for start, own in ((bands[0], 8), (bands[1], 0)):
                result = applied(fields, edges, centre, weight, k, q, q % 2, start, 16)
                fields[k + 1][q, start : start + 16] = result
                total += folded(result[own : own + 8])
            stacked.append(jnp.sum(total, axis=0, keepdims=True))
        heads.append(jnp.concatenate(stacked, axis=0))
    stacked = []
    for q in range(NP):
        total = moments[4, q]
        for start in (TOP, TOP + N - 8):
            result = applied(fields, edges, centre, weight, 4, q, q % 2, start, 8)
            total += folded(result)
            trace_basis(fields, basis, kappa, q, start, 8, result)
        stacked.append(jnp.sum(total, axis=0, keepdims=True))
    heads.append(jnp.concatenate(stacked, axis=0))
    total = sums[...] + block_sums(basis, ids, 0, 8, 8 // ABREAST) + block_sums(basis, ids, N - 8, N, 8 // ABREAST)
    ocean = u0[0, TOP : TOP + N]
    ocean = ocean * ocean

    ocean_sum = jnp.sum(jnp.sum(ocean, axis=0, keepdims=True), axis=1, keepdims=True)
    columns = [jnp.broadcast_to(ocean_sum, (NP, 1))]
    columns += [jnp.sum(head, axis=1, keepdims=True) for head in heads]
    wide = jnp.zeros((NP, NB), F32)
    spot = lax.broadcasted_iota(jnp.int32, (NP, NB), 1)
    coarse = F32(1.5 * 2**20)
    for k, column in enumerate(columns):
        head = (column + coarse) - coarse
        wide = jnp.where(spot == 2 * k, head, wide)
        wide = jnp.where(spot == 2 * k + 1, column - head, wide)
    half = 3 * NP // 2
    message[:half] = jnp.concatenate([total[:half], total[half:]], axis=1)
    message[half:] = jnp.concatenate([wide[: NP // 2], wide[NP // 2 :]], axis=1)


def two_sum(a, b):
    s = a + b
    t = s - a
    return s, (a - (s - t)) + (b - t)


def quick(a, b):
    s = a + b
    return s, b - (s - a)


def split(a):
    t = a * F32(4097.0)
    high = t - (t - a)
    return high, a - high


def mul(a, b):
    p = a[0] * b[0]
    ah, al = split(a[0])
    bh, bl = split(b[0])
    e = ((ah * bh - p) + ah * bl + al * bh) + al * bl
    return quick(p, e + (a[0] * b[1] + a[1] * b[0]))


def sub(a, b):
    s, e = two_sum(a[0], -b[0])
    return quick(s, e + (a[1] - b[1]))


def inverse(b):
    first = 1.0 / b[0]
    zero = jnp.zeros_like(first)
    rest = sub((jnp.ones_like(first), zero), mul(b, (first, zero)))
    return quick(first, first * rest[0])


def keep(ok, value, other):
    return tuple(jnp.where(ok, v, other) for v in value)


def solve(moment):
    g0, h1, h2, h3, h4, h5 = moment
    tiny = F32(2e-8)
    over = inverse(h1)
    l1, l2 = mul(h2, over), mul(h3, over)
    s11, s12, s22 = sub(h3, mul(h2, l1)), sub(h4, mul(h2, l2)), sub(h5, mul(h3, l2))
    y1, y2 = sub(h1, mul(g0, l1)), sub(h2, mul(g0, l2))
    ok1 = s11[0] > tiny * h3[0]
    over1 = keep(ok1, inverse(keep(ok1, s11, 1.0)), 0.0)
    l21 = mul(s12, over1)
    d2, z2 = sub(s22, mul(s12, l21)), sub(y2, mul(y1, l21))
    ok2 = ok1 & (d2[0] > tiny * h5[0])
    over2 = keep(ok2, inverse(keep(ok2, d2, 1.0)), 0.0)
    c2 = mul(z2, over2)
    c1 = mul(sub(y1, mul(s12, c2)), over1)
    c0 = mul(sub(sub(g0, mul(h2, c1)), mul(h3, c2)), over)
    return c0[0] + c0[1], c1[0] + c1[1], c2[0] + c2[1]


def combine_kernel(message, u0, u2, u4, basis, solution, trace, traces):
    half = 3 * NP // 2
    wide = jnp.concatenate([message[half:, :NB], message[half:, NB:]], axis=0)
    sums = jnp.concatenate([message[:half, :NB], message[:half, NB:]], axis=0)
    moment = []
    for k in range(6):
        head = wide[:, 2 * k : 2 * k + 1]
        rest = wide[:, 2 * k + 1 : 2 * k + 2]
        moment.append(quick(jnp.broadcast_to(head, (NP, N)), jnp.broadcast_to(rest, (NP, N))))
    c0, c1, c2 = solve(moment)
    cells = F32(N * N * 128 // NB)
    total = c0[:, :NB] * sums[:NP] + c1[:, :NB] * sums[NP : 2 * NP] + c2[:, :NB] * sums[2 * NP :]
    traces[...] = total / cells
    for q in range(NP):
        a0, a1, a2 = (c[q : q + 1] for c in (c0, c1, c2))
        solution[q] = a0 * u0[q, TOP : TOP + N] + a1 * u2[q, TOP : TOP + N] + a2 * u4[q, TOP : TOP + N]
        rows = [slice((i * NP + q) * PITCH, (i * NP + q) * PITCH + N) for i in range(3)]
        trace[q] = a0 * basis[rows[0]] + a1 * basis[rows[1]] + a2 * basis[rows[2]]


def pairs(count, offset, closed):
    out = []
    for i in range(offset, count, 2):
        j = (i + 1) % count
        if i + 1 < count or closed:
            out += [(i, j), (j, i)]
    return out


def swap(odd, even, axis, closed):
    count = lax.axis_size(axis)
    odd = lax.ppermute(odd, axis, pairs(count, 1, closed))
    even = lax.ppermute(even, axis, pairs(count, 0, closed))
    return odd, even


def everywhere(value):
    def sent(axis, bits):
        return lax.ppermute(value, axis, [(i, i ^ bits) for i in range(lax.axis_size(axis))])

    value = value + sent("lat", 1)
    for axis, unit in (("lat", 2), ("lon", 1), ("lon", 4)):
        near, far, across = sent(axis, unit), sent(axis, 3 * unit), sent(axis, 2 * unit)
        value = (value + near) + (far + across)
    return value


def per_device(signs, mask, kappa, ids):
    edge, field, strip, plane = (N, N), (NP, ROWS, N), (2, ROWS, N), (ROWS, N)
    halo = (SLOTS, 8, N)
    flat = (3 * NP * PITCH, N)
    ints = jax.ShapeDtypeStruct(edge, jnp.int32)
    signs, mask, kappa, ids = (pltpu.with_memory_space_constraint(x, pltpu.HBM) for x in (signs, mask, kappa, ids))
    own_odd, own_even, u0, kappa = call(
        pack_kernel,
        [edge, edge, field, edge],
        8,
        [
            pltpu.VMEM((NP, N, N), jnp.int32),
            pltpu.VMEM(edge, jnp.int32),
            pltpu.VMEM((NP // 2, 2 * N, 2 * N), BF16),
            pltpu.SemaphoreType.DMA((2 + PARTS,)),
        ],
        specs=[FAR] * 3,
    )(signs, mask, kappa)
    odd, even = swap(own_odd, own_even, "lat", False)
    u1, centre, weight, ids = call(
        first_kernel,
        [field, plane, plane, ints],
        8,
        [pltpu.SemaphoreType.DMA],
        specs=[NEAR, NEAR, FAR],
        micros=2,
    )(u0, kappa, ids)
    strips, kstrips, row_odd, row_even = call(strips_kernel, [(3, N, N), (2, N, N), halo, halo], 8)(
        odd, even, own_odd, own_even, kappa, u0
    )
    row_odd, row_even = swap(row_odd, row_even, "lon", True)
    coefficients = [pltpu.VMEM(shape, F32) for shape in (plane, plane, strip, strip)]
    edges = pltpu.VMEM((DEPTH, 2, ROWS, N), F32)
    u1, u2, u3, u4, s, basis, moments, sums = call(
        inner_kernel,
        [field, field, field, field, (DEPTH, 3, ROWS, N), flat, (DEPTH, NP, 8, N), (3 * NP, NB)],
        24,
        [edges, *coefficients[2:]],
        aliases={0: 0},
        micros=8,
    )(u1, u0, kappa, ids, strips, kstrips, centre, weight)
    u0, u1, u2, u3, u4, s, basis, message = call(
        outer_kernel,
        [field, field, field, field, field, (DEPTH, 3, ROWS, N), flat, (2 * NP, N)],
        24,
        [edges, *coefficients],
        aliases={i: i for i in range(7)},
    )(u0, u1, u2, u3, u4, s, basis, moments, sums, kappa, ids, kstrips, row_odd, row_even)
    message = everywhere(message)
    out = (NP, N, N)
    return tuple(call(combine_kernel, [out, out, (NP, NB)], 16)(message, u0, u2, u4, basis))


def solution(mesh):
    placed = (P(None, "lon", "lat"), P("lon", "lat"), P("lon", "lat"), P("lon", "lat"))
    return jax.shard_map(
        per_device,
        mesh=mesh,
        in_specs=placed,
        out_specs=(P(None, "lon", "lat"), P(None, "lon", "lat"), P()),
        check_vma=False,
    )
```

```python
import jax
import jax.numpy as jnp
from jax import lax
from jax.experimental import pallas as pl
from jax.experimental.pallas import tpu as pltpu
from jax.sharding import PartitionSpec as P

F32 = jnp.float32
BF16 = jnp.bfloat16
NB = 64
NP = 16
N = 128
DEPTH = 5
W = DEPTH * NP
SLOTS = NP + 6
TOP = 16
ROWS = N + 2 * TOP
MIB = 1 << 20
FAR = pl.BlockSpec(memory_space=pltpu.HBM)
NEAR = pl.BlockSpec(memory_space=pltpu.VMEM)
CHUNK = 32
FINAL = 56
PITCH = N + 8
UNROLL = 14
ABREAST = 4
TOGETHER = 8
PARTS = 4


def lanes(rows=8):
    return lax.broadcasted_iota(jnp.int32, (rows, N), 1)


def call(kernel, outs, mib, scratch=(), aliases=None, specs=None, micros=1):
    extra = {} if specs is None else {"in_specs": specs}
    return pl.pallas_call(
        kernel,
        out_shape=[o if isinstance(o, jax.ShapeDtypeStruct) else jax.ShapeDtypeStruct(o, F32) for o in outs],
        scratch_shapes=list(scratch),
        input_output_aliases=aliases or {},
        compiler_params=pltpu.CompilerParams(vmem_limit_bytes=mib * MIB),
        cost_estimate=pl.CostEstimate(flops=0, bytes_accessed=micros * 3_000_000, transcendentals=0),
        **extra,
    )


def pack_kernel(
    signs_hbm, mask_hbm, kappa_hbm,
    odd_ref, even_ref, u0, kappa,
    signs, mask, picks, sems,
):
    part = NP // PARTS
    copies = [
        pltpu.make_async_copy(mask_hbm, mask, sems.at[0]),
        pltpu.make_async_copy(kappa_hbm, kappa, sems.at[1]),
    ]
    for i in range(PARTS):
        probes = pl.ds(i * part, part)
        copies.append(pltpu.make_async_copy(signs_hbm.at[probes], signs.at[probes], sems.at[2 + i]))
    for copy in (copies[0], *copies[2:], copies[1]):
        copy.start()
    lane = lax.broadcasted_iota(jnp.int32, (1, 2 * N), 1)
    side, spot = lane // N, lane % N
    column, probe = spot // NP, spot % NP
    row = lax.broadcasted_iota(jnp.int32, (2 * N, 2 * N), 0)
    for pair in range(NP // 2):
        source = column + (N - DEPTH) * side + N * (probe - 2 * pair)
        wanted = (probe // 2 == pair) & (column < DEPTH)
        source = jnp.where(wanted, source, -1)
        picks[pair] = (row == source).astype(F32).astype(BF16)
    total = jnp.zeros((N, 2 * N), F32)
    copies[0].wait()
    ocean = mask[...].astype(F32)
    for pair in range(NP // 2):
        if pair % (part // 2) == 0:
            copies[2 + pair // (part // 2)].wait()
        fields = []
        for q in (2 * pair, 2 * pair + 1):
            field = signs[q].astype(F32) * ocean
            u0[q, TOP : TOP + N] = field
            fields.append(field.astype(BF16))
        total += jnp.dot(jnp.concatenate(fields, axis=1), picks[pair], preferred_element_type=F32)
    here = lanes(N)
    in_kappa = (here >= W) & (here < W + DEPTH)
    copies[1].wait()
    left = jnp.where(in_kappa, pltpu.roll(kappa[...], W, 1), total[:, :N])
    right = jnp.where(in_kappa, pltpu.roll(kappa[...], W + DEPTH, 1), total[:, N:])
    low = lax.axis_index("lat") % 2 == 0
    even_ref[...] = jnp.where(low, right, left)
    odd_ref[...] = jnp.where(low, left, right)


def strips_kernel(odd, even, own_odd, own_even, kappa, u0, after, strips, kstrips, odd_ref, even_ref):
    del after
    low = lax.axis_index("lat") % 2 == 0
    from_left = jnp.where(low, odd[...], even[...])
    from_right = jnp.where(low, even[...], odd[...])
    own_left = jnp.where(low, own_odd[...], own_even[...])
    own_right = jnp.where(low, own_even[...], own_odd[...])
    here = lanes(N)
    strips[0] = jnp.where(here < W, from_left, pltpu.roll(own_left, W, 1))
    strips[1] = jnp.where(here < 3 * NP, pltpu.roll(own_right, N - 2 * NP, 1), pltpu.roll(from_right, 3 * NP, 1))
    strips[2] = jnp.where(here < NP, pltpu.roll(own_right, N - NP, 1), pltpu.roll(own_left, N // 2, 1))
    pick_row = lax.broadcasted_iota(jnp.int32, (N, N), 0)
    pick_col = lax.broadcasted_iota(jnp.int32, (N, N), 1)
    for i, (first, second, skip) in enumerate(((from_left, own_left, 0), (own_right, from_right, 2))):
        pair = jnp.where(here < W + DEPTH, first, pltpu.roll(second, DEPTH, 1))
        spread = (pick_row == W + skip + pick_col // NP).astype(F32)
        kstrips[i] = jnp.dot(pair, spread, precision=lax.Precision.HIGHEST, preferred_element_type=F32)
    low = lax.axis_index("lon") % 2 == 0
    for slot in range(SLOTS):
        if slot < NP:
            top, bottom = u0[slot, TOP : TOP + 8], u0[slot, TOP + N - 8 : TOP + N]
        else:
            if slot < NP + 3:
                field = strips.at[slot - NP]
            elif slot < NP + 5:
                field = kstrips.at[slot - NP - 3]
            else:
                field = kappa
            top, bottom = field[:8], field[N - 8 :]
        even_ref[slot] = jnp.where(low, bottom, top)
        odd_ref[slot] = jnp.where(low, top, bottom)


def strip_step(k, s, edges, scentre, sweight, start, size):
    rows = slice(start, start + size)
    here = lanes(size)
    now = [s[k, i, rows] for i in range(2)]
    moved = pltpu.roll(now[1], NP - 1, 1)
    edges[k, 0, rows] = jnp.where(here % 2 == 0, now[0], moved)
    edges[k, 1, rows] = jnp.where(here % 2 == 0, moved, now[0])
    if k == DEPTH - 1:
        return
    for i in range(2):
        forth, back = pltpu.roll(now[i], NP, 1), pltpu.roll(now[i], N - NP, 1)
        if k == 0 and i == 0:
            back = jnp.where(here >= N - NP, s[0, 2, rows], back)
        if k == 0 and i == 1:
            forth = jnp.where(here < NP, s[0, 2, rows], forth)
        around = s[k, i, start - 1 : start + size - 1] + s[k, i, start + 1 : start + size + 1]
        s[k + 1, i, rows] = scentre[i, rows] * now[i] - sweight[i, rows] * (around + forth + back)


def applied(fields, edges, centre, weight, k, q, parity, start, size):
    rows = slice(start, start + size)
    here = lanes(size)
    field = fields[k][q, rows]
    edge = pltpu.roll(edges[k, parity, rows], N - NP * 4 - q, 1)
    forth = jnp.where(here == 0, edge, pltpu.roll(field, 1, 1))
    back = jnp.where(here == N - 1, edge, pltpu.roll(field, N - 1, 1))
    around = fields[k][q, start - 1 : start + size - 1] + fields[k][q, start + 1 : start + size + 1]
    return centre[rows] * field - weight[rows] * (around + forth + back)


def completed(u1, edges, weight, q, parity, start, size):
    rows = slice(start, start + size)
    here = lanes(size)
    edge = pltpu.roll(edges[0, parity, rows], N - NP * 4 - q, 1)
    edge = jnp.where((here == 0) | (here == N - 1), edge, 0.0)
    return u1[q, rows] - weight[rows] * edge


def folded(value):
    return jnp.sum((value * value).reshape(-1, 8, N), axis=0)


def trace_basis(fields, basis, kappa, q, start, size, fifth):
    rows = slice(start, start + size)
    scale = kappa[start - TOP : start - TOP + size]
    v0, v1, v2, v3, v4 = (field[q, rows] for field in fields)
    one, zero = scale * v1, scale * v0
    for i, value in enumerate((one * (v0 + v0), one * v2 + zero * v3, one * v4 + zero * fifth)):
        base = pl.multiple_of((i * NP + q) * PITCH + (start - TOP), 8)
        basis[pl.ds(base, size)] = value


def block_sums(basis, ids, first, last, unroll):
    block = lax.broadcasted_iota(jnp.int32, (NB, N), 0)

    def blocks(step, total):
        high, rest, hot = [], [], []
        for row in [step * ABREAST + i for i in range(ABREAST)]:
            data = basis[pl.ds(row, 3 * NP, stride=PITCH)]
            high.append(data.astype(BF16))
            rest.append((data - high[-1].astype(F32)).astype(BF16))
            hot.append((ids[pl.ds(row, 1)] == block).astype(F32).astype(BF16))
        both = jnp.concatenate([jnp.concatenate(high, axis=1), jnp.concatenate(rest, axis=1)], axis=0)
        hot = jnp.concatenate(hot, axis=1)
        return total + lax.dot_general(both, hot, (((1,), (1,)), ((), ())), preferred_element_type=F32)

    total = lax.fori_loop(first // ABREAST, last // ABREAST, blocks, jnp.zeros((6 * NP, NB), F32), unroll=unroll)
    return total[: 3 * NP] + total[3 * NP :]


def first_kernel(u0, kappa, ids_hbm, u1, centre, weight, ids, sem):
    copy = pltpu.make_async_copy(ids_hbm, ids, sem)
    copy.start()
    inner = slice(TOP, TOP + N)
    ocean = u0[0, inner] * u0[0, inner]
    centre[inner] = ocean * (kappa[...] + 0.25)
    weight[inner] = ocean * 0.0625
    here = lanes(CHUNK)

    def probe_group(group, carry):
        for start in range(TOP, TOP + N, CHUNK):
            for j in range(TOGETHER):
                q = group * TOGETHER + j
                field = u0[q, start : start + CHUNK]
                forth = jnp.where(here == 0, 0.0, pltpu.roll(field, 1, 1))
                back = jnp.where(here == N - 1, 0.0, pltpu.roll(field, N - 1, 1))
                around = u0[q, start - 1 : start + CHUNK - 1] + u0[q, start + 1 : start + CHUNK + 1] + forth + back
                rows = slice(start, start + CHUNK)
                u1[q, rows] = centre[rows] * field - weight[rows] * around
        return carry

    lax.fori_loop(0, NP // TOGETHER, probe_group, 0)
    copy.wait()


def inner_kernel(
    u1_in, u0, kappa, ids, strips, kstrips, centre, weight,
    u1, u2, u3, u4, s, basis, moments, sums,
    edges, scentre, sweight,
):
    del u1_in
    inner = slice(TOP, TOP + N)
    s[0, 2, inner] = strips[2]
    for i in range(2):
        s[0, i, inner] = strips[i]
        square = strips[i] * strips[i]
        scentre[i, inner] = square * (kstrips[i] + 0.25)
        sweight[i, inner] = square * 0.0625
    for k in range(DEPTH):
        for start in range(TOP, TOP + N, 32):
            strip_step(k, s, edges, scentre, sweight, start, 32)
    fields = [u0, u1, u2, u3, u4]

    def probe_group(group, carry):
        probes = [(group * TOGETHER + j, j % 2) for j in range(TOGETHER)]
        for k in range(4):
            totals = [jnp.zeros((8, N), F32) for _ in probes]
            for start in range(TOP, TOP + N, CHUNK):
                for j, (q, parity) in enumerate(probes):
                    if k == 0:
                        result = completed(u1, edges, weight, q, parity, start, CHUNK)
                    else:
                        result = applied(fields, edges, centre, weight, k, q, parity, start, CHUNK)
                    fields[k + 1][q, start : start + CHUNK] = result
                    low, high = max(start, TOP + 8), min(start + CHUNK, TOP + N - 8)
                    totals[j] += folded(result[low - start : high - start])
            for (q, _), total in zip(probes, totals):
                moments[k, q] = total
        totals = [jnp.zeros((8, N), F32) for _ in probes]
        for start in range(TOP + 8, TOP + N - 8, FINAL):
            for j, (q, parity) in enumerate(probes):
                result = applied(fields, edges, centre, weight, 4, q, parity, start, FINAL)
                totals[j] += folded(result)
                trace_basis(fields, basis, kappa, q, start, FINAL, result)
        for (q, _), total in zip(probes, totals):
            moments[4, q] = total
        return carry

    lax.fori_loop(0, NP // TOGETHER, probe_group, 0)
    sums[...] = block_sums(basis, ids, 8, N - 8, UNROLL)


def outer_kernel(
    u0_in, u1_in, u2_in, u3_in, u4_in, s_in, basis_in,
    moments, sums, kappa, ids, kstrips, odd, even,
    u0, u1, u2, u3, u4, s, basis, message,
    edges, centre, weight, scentre, sweight,
):
    del u0_in, u1_in, u2_in, u3_in, u4_in, s_in, basis_in
    low = lax.axis_index("lon") % 2 == 0
    bands = (TOP - 8, TOP + N - 8)
    for start, inside, outside, if_low, if_high in (
        (bands[0], 8, 0, odd, even),
        (bands[1], 0, 8, even, odd),
    ):
        rows = slice(start + outside, start + outside + 8)
        own = slice(start + inside, start + inside + 8)
        here = slice(start + inside - TOP, start + inside - TOP + 8)
        halo = [jnp.where(low, if_low[i], if_high[i]) for i in range(SLOTS)]
        for q in range(NP):
            u0[q, rows] = halo[q]
        s[0, 2, rows] = halo[NP + 2]
        for i in range(2):
            s[0, i, rows] = halo[NP + i]
            for where, value, kvalue in ((rows, halo[NP + i], halo[NP + 3 + i]), (own, s[0, i, own], kstrips[i, here])):
                scentre[i, where] = value * value * (kvalue + 0.25)
                sweight[i, where] = value * value * 0.0625
        for where, value, kvalue in ((rows, halo[0], halo[NP + 5]), (own, u0[0, own], kappa[here])):
            centre[where] = value * value * (kvalue + 0.25)
            weight[where] = value * value * 0.0625
    fields = [u0, u1, u2, u3, u4]
    blank = jnp.zeros((8, N), F32)
    for row in (TOP - 16, TOP + N + 8):
        for field in fields:
            for q in range(NP):
                field[q, row : row + 8] = blank
        for k in range(DEPTH):
            for i in range(2):
                s[k, i, row : row + 8] = blank
    for k in range(DEPTH):
        for start in bands:
            strip_step(k, s, edges, scentre, sweight, start, 16)

    heads = []
    for k in range(4):
        stacked = []
        for q in range(NP):
            total = moments[k, q]
            for start, own in ((bands[0], 8), (bands[1], 0)):
                result = applied(fields, edges, centre, weight, k, q, q % 2, start, 16)
                fields[k + 1][q, start : start + 16] = result
                total += folded(result[own : own + 8])
            stacked.append(jnp.sum(total, axis=0, keepdims=True))
        heads.append(jnp.concatenate(stacked, axis=0))
    stacked = []
    for q in range(NP):
        total = moments[4, q]
        for start in (TOP, TOP + N - 8):
            result = applied(fields, edges, centre, weight, 4, q, q % 2, start, 8)
            total += folded(result)
            trace_basis(fields, basis, kappa, q, start, 8, result)
        stacked.append(jnp.sum(total, axis=0, keepdims=True))
    heads.append(jnp.concatenate(stacked, axis=0))
    total = sums[...] + block_sums(basis, ids, 0, 8, 8 // ABREAST) + block_sums(basis, ids, N - 8, N, 8 // ABREAST)
    ocean = u0[0, TOP : TOP + N]
    ocean = ocean * ocean

    ocean_sum = jnp.sum(jnp.sum(ocean, axis=0, keepdims=True), axis=1, keepdims=True)
    columns = [jnp.broadcast_to(ocean_sum, (NP, 1))]
    columns += [jnp.sum(head, axis=1, keepdims=True) for head in heads]
    wide = jnp.zeros((NP, NB), F32)
    spot = lax.broadcasted_iota(jnp.int32, (NP, NB), 1)
    coarse = F32(1.5 * 2**20)
    for k, column in enumerate(columns):
        head = (column + coarse) - coarse
        wide = jnp.where(spot == 2 * k, head, wide)
        wide = jnp.where(spot == 2 * k + 1, column - head, wide)
    half = 3 * NP // 2
    message[:half] = jnp.concatenate([total[:half], total[half:]], axis=1)
    message[half:] = jnp.concatenate([wide[: NP // 2], wide[NP // 2 :]], axis=1)


def two_sum(a, b):
    s = a + b
    t = s - a
    return s, (a - (s - t)) + (b - t)


def quick(a, b):
    s = a + b
    return s, b - (s - a)


def split(a):
    t = a * F32(4097.0)
    high = t - (t - a)
    return high, a - high


def mul(a, b):
    p = a[0] * b[0]
    ah, al = split(a[0])
    bh, bl = split(b[0])
    e = ((ah * bh - p) + ah * bl + al * bh) + al * bl
    return quick(p, e + (a[0] * b[1] + a[1] * b[0]))


def sub(a, b):
    s, e = two_sum(a[0], -b[0])
    return quick(s, e + (a[1] - b[1]))


def inverse(b):
    first = 1.0 / b[0]
    zero = jnp.zeros_like(first)
    rest = sub((jnp.ones_like(first), zero), mul(b, (first, zero)))
    return quick(first, first * rest[0])


def keep(ok, value, other):
    return tuple(jnp.where(ok, v, other) for v in value)


def solve(moment):
    g0, h1, h2, h3, h4, h5 = moment
    tiny = F32(2e-8)
    over = inverse(h1)
    l1, l2 = mul(h2, over), mul(h3, over)
    s11, s12, s22 = sub(h3, mul(h2, l1)), sub(h4, mul(h2, l2)), sub(h5, mul(h3, l2))
    y1, y2 = sub(h1, mul(g0, l1)), sub(h2, mul(g0, l2))
    ok1 = s11[0] > tiny * h3[0]
    over1 = keep(ok1, inverse(keep(ok1, s11, 1.0)), 0.0)
    l21 = mul(s12, over1)
    d2, z2 = sub(s22, mul(s12, l21)), sub(y2, mul(y1, l21))
    ok2 = ok1 & (d2[0] > tiny * h5[0])
    over2 = keep(ok2, inverse(keep(ok2, d2, 1.0)), 0.0)
    c2 = mul(z2, over2)
    c1 = mul(sub(y1, mul(s12, c2)), over1)
    c0 = mul(sub(sub(g0, mul(h2, c1)), mul(h3, c2)), over)
    return c0[0] + c0[1], c1[0] + c1[1], c2[0] + c2[1]


def combine_kernel(message, u0, u2, u4, basis, solution, trace, traces):
    half = 3 * NP // 2
    wide = jnp.concatenate([message[half:, :NB], message[half:, NB:]], axis=0)
    sums = jnp.concatenate([message[:half, :NB], message[:half, NB:]], axis=0)
    moment = []
    for k in range(6):
        head = wide[:, 2 * k : 2 * k + 1]
        rest = wide[:, 2 * k + 1 : 2 * k + 2]
        moment.append(quick(jnp.broadcast_to(head, (NP, N)), jnp.broadcast_to(rest, (NP, N))))
    c0, c1, c2 = solve(moment)
    cells = F32(N * N * 128 // NB)
    total = c0[:, :NB] * sums[:NP] + c1[:, :NB] * sums[NP : 2 * NP] + c2[:, :NB] * sums[2 * NP :]
    traces[...] = total / cells
    for q in range(NP):
        a0, a1, a2 = (c[q : q + 1] for c in (c0, c1, c2))
        solution[q] = a0 * u0[q, TOP : TOP + N] + a1 * u2[q, TOP : TOP + N] + a2 * u4[q, TOP : TOP + N]
        rows = [slice((i * NP + q) * PITCH, (i * NP + q) * PITCH + N) for i in range(3)]
        trace[q] = a0 * basis[rows[0]] + a1 * basis[rows[1]] + a2 * basis[rows[2]]


def pairs(count, offset, closed):
    out = []
    for i in range(offset, count, 2):
        j = (i + 1) % count
        if i + 1 < count or closed:
            out += [(i, j), (j, i)]
    return out


def swap(odd, even, axis, closed):
    count = lax.axis_size(axis)
    odd = lax.ppermute(odd, axis, pairs(count, 1, closed))
    even = lax.ppermute(even, axis, pairs(count, 0, closed))
    return odd, even


def everywhere(value):
    def sent(axis, bits):
        return lax.ppermute(value, axis, [(i, i ^ bits) for i in range(lax.axis_size(axis))])

    value = value + sent("lat", 1)
    for axis, unit in (("lat", 2), ("lon", 1), ("lon", 4)):
        near, far, across = sent(axis, unit), sent(axis, 3 * unit), sent(axis, 2 * unit)
        value = (value + near) + (far + across)
    return value


def per_device(signs, mask, kappa, ids):
    edge, field, strip, plane = (N, N), (NP, ROWS, N), (2, ROWS, N), (ROWS, N)
    halo = (SLOTS, 8, N)
    flat = (3 * NP * PITCH, N)
    ints = jax.ShapeDtypeStruct(edge, jnp.int32)
    signs, mask, kappa, ids = (pltpu.with_memory_space_constraint(x, pltpu.HBM) for x in (signs, mask, kappa, ids))
    own_odd, own_even, u0, kappa = call(
        pack_kernel,
        [edge, edge, field, edge],
        8,
        [
            pltpu.VMEM((NP, N, N), jnp.int32),
            pltpu.VMEM(edge, jnp.int32),
            pltpu.VMEM((NP // 2, 2 * N, 2 * N), BF16),
            pltpu.SemaphoreType.DMA((2 + PARTS,)),
        ],
        specs=[FAR] * 3,
    )(signs, mask, kappa)
    odd, even = swap(own_odd, own_even, "lat", False)
    u1, centre, weight, ids = call(
        first_kernel,
        [field, plane, plane, ints],
        8,
        [pltpu.SemaphoreType.DMA],
        specs=[NEAR, NEAR, FAR],
        micros=2,
    )(u0, kappa, ids)
    strips, kstrips, row_odd, row_even = call(strips_kernel, [(3, N, N), (2, N, N), halo, halo], 8)(
        odd, even, own_odd, own_even, kappa, u0, centre
    )
    row_odd, row_even = swap(row_odd, row_even, "lon", True)
    coefficients = [pltpu.VMEM(shape, F32) for shape in (plane, plane, strip, strip)]
    edges = pltpu.VMEM((DEPTH, 2, ROWS, N), F32)
    u1, u2, u3, u4, s, basis, moments, sums = call(
        inner_kernel,
        [field, field, field, field, (DEPTH, 3, ROWS, N), flat, (DEPTH, NP, 8, N), (3 * NP, NB)],
        24,
        [edges, *coefficients[2:]],
        aliases={0: 0},
        micros=8,
    )(u1, u0, kappa, ids, strips, kstrips, centre, weight)
    u0, u1, u2, u3, u4, s, basis, message = call(
        outer_kernel,
        [field, field, field, field, field, (DEPTH, 3, ROWS, N), flat, (2 * NP, N)],
        24,
        [edges, *coefficients],
        aliases={i: i for i in range(7)},
    )(u0, u1, u2, u3, u4, s, basis, moments, sums, kappa, ids, kstrips, row_odd, row_even)
    message = everywhere(message)
    out = (NP, N, N)
    return tuple(call(combine_kernel, [out, out, (NP, NB)], 16)(message, u0, u2, u4, basis))


def solution(mesh):
    placed = (P(None, "lon", "lat"), P("lon", "lat"), P("lon", "lat"), P("lon", "lat"))
    return jax.shard_map(
        per_device,
        mesh=mesh,
        in_specs=placed,
        out_specs=(P(None, "lon", "lat"), P(None, "lon", "lat"), P()),
        check_vma=False,
    )
```

```python
import jax
import jax.numpy as jnp
from jax import lax
from jax.experimental import pallas as pl
from jax.experimental.pallas import tpu as pltpu
from jax.sharding import PartitionSpec as P

F32 = jnp.float32
BF16 = jnp.bfloat16
NB = 64
NP = 16
N = 128
DEPTH = 5
W = DEPTH * NP
SLOTS = NP + 6
TOP = 16
ROWS = N + 2 * TOP
MIB = 1 << 20
FAR = pl.BlockSpec(memory_space=pltpu.HBM)
NEAR = pl.BlockSpec(memory_space=pltpu.VMEM)
CHUNK = 32
FINAL = 56
PITCH = N + 8
UNROLL = 14
ABREAST = 4
TOGETHER = 16
PARTS = 4


def lanes(rows=8):
    return lax.broadcasted_iota(jnp.int32, (rows, N), 1)


def call(kernel, outs, mib, scratch=(), aliases=None, specs=None, micros=1):
    extra = {} if specs is None else {"in_specs": specs}
    return pl.pallas_call(
        kernel,
        out_shape=[o if isinstance(o, jax.ShapeDtypeStruct) else jax.ShapeDtypeStruct(o, F32) for o in outs],
        scratch_shapes=list(scratch),
        input_output_aliases=aliases or {},
        compiler_params=pltpu.CompilerParams(vmem_limit_bytes=mib * MIB),
        cost_estimate=pl.CostEstimate(flops=0, bytes_accessed=micros * 3_000_000, transcendentals=0),
        **extra,
    )


def pack_kernel(
    signs_hbm, mask_hbm, kappa_hbm,
    odd_ref, even_ref, u0, kappa,
    signs, mask, picks, sems,
):
    part = NP // PARTS
    copies = [
        pltpu.make_async_copy(mask_hbm, mask, sems.at[0]),
        pltpu.make_async_copy(kappa_hbm, kappa, sems.at[1]),
    ]
    for i in range(PARTS):
        probes = pl.ds(i * part, part)
        copies.append(pltpu.make_async_copy(signs_hbm.at[probes], signs.at[probes], sems.at[2 + i]))
    for copy in (copies[0], *copies[2:], copies[1]):
        copy.start()
    lane = lax.broadcasted_iota(jnp.int32, (1, 2 * N), 1)
    side, spot = lane // N, lane % N
    column, probe = spot // NP, spot % NP
    row = lax.broadcasted_iota(jnp.int32, (2 * N, 2 * N), 0)
    for pair in range(NP // 2):
        source = column + (N - DEPTH) * side + N * (probe - 2 * pair)
        wanted = (probe // 2 == pair) & (column < DEPTH)
        source = jnp.where(wanted, source, -1)
        picks[pair] = (row == source).astype(F32).astype(BF16)
    total = jnp.zeros((N, 2 * N), F32)
    copies[0].wait()
    ocean = mask[...].astype(F32)
    for pair in range(NP // 2):
        if pair % (part // 2) == 0:
            copies[2 + pair // (part // 2)].wait()
        fields = []
        for q in (2 * pair, 2 * pair + 1):
            field = signs[q].astype(F32) * ocean
            u0[q, TOP : TOP + N] = field
            fields.append(field.astype(BF16))
        total += jnp.dot(jnp.concatenate(fields, axis=1), picks[pair], preferred_element_type=F32)
    here = lanes(N)
    in_kappa = (here >= W) & (here < W + DEPTH)
    copies[1].wait()
    left = jnp.where(in_kappa, pltpu.roll(kappa[...], W, 1), total[:, :N])
    right = jnp.where(in_kappa, pltpu.roll(kappa[...], W + DEPTH, 1), total[:, N:])
    low = lax.axis_index("lat") % 2 == 0
    even_ref[...] = jnp.where(low, right, left)
    odd_ref[...] = jnp.where(low, left, right)


def strips_kernel(odd, even, own_odd, own_even, kappa, u0, after, strips, kstrips, odd_ref, even_ref):
    del after
    low = lax.axis_index("lat") % 2 == 0
    from_left = jnp.where(low, odd[...], even[...])
    from_right = jnp.where(low, even[...], odd[...])
    own_left = jnp.where(low, own_odd[...], own_even[...])
    own_right = jnp.where(low, own_even[...], own_odd[...])
    here = lanes(N)
    strips[0] = jnp.where(here < W, from_left, pltpu.roll(own_left, W, 1))
    strips[1] = jnp.where(here < 3 * NP, pltpu.roll(own_right, N - 2 * NP, 1), pltpu.roll(from_right, 3 * NP, 1))
    strips[2] = jnp.where(here < NP, pltpu.roll(own_right, N - NP, 1), pltpu.roll(own_left, N // 2, 1))
    pick_row = lax.broadcasted_iota(jnp.int32, (N, N), 0)
    pick_col = lax.broadcasted_iota(jnp.int32, (N, N), 1)
    for i, (first, second, skip) in enumerate(((from_left, own_left, 0), (own_right, from_right, 2))):
        pair = jnp.where(here < W + DEPTH, first, pltpu.roll(second, DEPTH, 1))
        spread = (pick_row == W + skip + pick_col // NP).astype(F32)
        kstrips[i] = jnp.dot(pair, spread, precision=lax.Precision.HIGHEST, preferred_element_type=F32)
    low = lax.axis_index("lon") % 2 == 0
    for slot in range(SLOTS):
        if slot < NP:
            top, bottom = u0[slot, TOP : TOP + 8], u0[slot, TOP + N - 8 : TOP + N]
        else:
            if slot < NP + 3:
                field = strips.at[slot - NP]
            elif slot < NP + 5:
                field = kstrips.at[slot - NP - 3]
            else:
                field = kappa
            top, bottom = field[:8], field[N - 8 :]
        even_ref[slot] = jnp.where(low, bottom, top)
        odd_ref[slot] = jnp.where(low, top, bottom)


def strip_step(k, s, edges, scentre, sweight, start, size):
    rows = slice(start, start + size)
    here = lanes(size)
    now = [s[k, i, rows] for i in range(2)]
    moved = pltpu.roll(now[1], NP - 1, 1)
    edges[k, 0, rows] = jnp.where(here % 2 == 0, now[0], moved)
    edges[k, 1, rows] = jnp.where(here % 2 == 0, moved, now[0])
    if k == DEPTH - 1:
        return
    for i in range(2):
        forth, back = pltpu.roll(now[i], NP, 1), pltpu.roll(now[i], N - NP, 1)
        if k == 0 and i == 0:
            back = jnp.where(here >= N - NP, s[0, 2, rows], back)
        if k == 0 and i == 1:
            forth = jnp.where(here < NP, s[0, 2, rows], forth)
        around = s[k, i, start - 1 : start + size - 1] + s[k, i, start + 1 : start + size + 1]
        s[k + 1, i, rows] = scentre[i, rows] * now[i] - sweight[i, rows] * (around + forth + back)


def applied(fields, edges, centre, weight, k, q, parity, start, size):
    rows = slice(start, start + size)
    here = lanes(size)
    field = fields[k][q, rows]
    edge = pltpu.roll(edges[k, parity, rows], N - NP * 4 - q, 1)
    forth = jnp.where(here == 0, edge, pltpu.roll(field, 1, 1))
    back = jnp.where(here == N - 1, edge, pltpu.roll(field, N - 1, 1))
    around = fields[k][q, start - 1 : start + size - 1] + fields[k][q, start + 1 : start + size + 1]
    return centre[rows] * field - weight[rows] * (around + forth + back)


def completed(u1, edges, weight, q, parity, start, size):
    rows = slice(start, start + size)
    here = lanes(size)
    edge = pltpu.roll(edges[0, parity, rows], N - NP * 4 - q, 1)
    edge = jnp.where((here == 0) | (here == N - 1), edge, 0.0)
    return u1[q, rows] - weight[rows] * edge


def outer_columns(s, margins, start, size):
    rows = slice(start, start + size)
    here = lanes(size)
    left, right = s[2, 0, rows], s[2, 1, rows]
    columns = (
        pltpu.roll(left, N - NP, 1),
        pltpu.roll(left, N - 2 * NP + 1, 1),
        pltpu.roll(right, 3 * NP - 2, 1),
        pltpu.roll(right, 2 * NP - 1, 1),
    )
    for j in range(4):
        place = (here + 4 - j) % 4
        value = jnp.where(place == 0, columns[0], columns[1])
        margins[j, rows] = jnp.where(place == 2, columns[2], jnp.where(place == 3, columns[3], value))


def second_completed(u2, margins, q, j, start, size):
    rows = slice(start, start + size)
    here = lanes(size)
    margin = pltpu.roll(margins[j % 4, rows], N - NP * 4 - q, 1)
    return jnp.where((here < 2) | (here >= N - 2), margin, u2[q, rows])


def folded(value):
    return jnp.sum((value * value).reshape(-1, 8, N), axis=0)


def trace_basis(fields, basis, kappa, q, start, size, fifth):
    rows = slice(start, start + size)
    scale = kappa[start - TOP : start - TOP + size]
    v0, v1, v2, v3, v4 = (field[q, rows] for field in fields)
    one, zero = scale * v1, scale * v0
    for i, value in enumerate((one * (v0 + v0), one * v2 + zero * v3, one * v4 + zero * fifth)):
        base = pl.multiple_of((i * NP + q) * PITCH + (start - TOP), 8)
        basis[pl.ds(base, size)] = value


def block_sums(basis, ids, first, last, unroll):
    block = lax.broadcasted_iota(jnp.int32, (NB, N), 0)

    def blocks(step, total):
        high, rest, hot = [], [], []
        for row in [step * ABREAST + i for i in range(ABREAST)]:
            data = basis[pl.ds(row, 3 * NP, stride=PITCH)]
            high.append(data.astype(BF16))
            rest.append((data - high[-1].astype(F32)).astype(BF16))
            hot.append((ids[pl.ds(row, 1)] == block).astype(F32).astype(BF16))
        both = jnp.concatenate([jnp.concatenate(high, axis=1), jnp.concatenate(rest, axis=1)], axis=0)
        hot = jnp.concatenate(hot, axis=1)
        return total + lax.dot_general(both, hot, (((1,), (1,)), ((), ())), preferred_element_type=F32)

    total = lax.fori_loop(first // ABREAST, last // ABREAST, blocks, jnp.zeros((6 * NP, NB), F32), unroll=unroll)
    return total[: 3 * NP] + total[3 * NP :]


def first_kernel(u0, kappa, ids_hbm, u1, u2, centre, weight, ids, sem):
    copy = pltpu.make_async_copy(ids_hbm, ids, sem)
    copy.start()
    inner = slice(TOP, TOP + N)
    ocean = u0[0, inner] * u0[0, inner]
    centre[inner] = ocean * (kappa[...] + 0.25)
    weight[inner] = ocean * 0.0625
    here = lanes(CHUNK)

    def probe_group(group, carry):
        for source, target in ((u0, u1), (u1, u2)):
            for start in range(TOP, TOP + N, CHUNK):
                for j in range(TOGETHER):
                    q = group * TOGETHER + j
                    rows = slice(start, start + CHUNK)
                    field = source[q, rows]
                    forth = jnp.where(here == 0, 0.0, pltpu.roll(field, 1, 1))
                    back = jnp.where(here == N - 1, 0.0, pltpu.roll(field, N - 1, 1))
                    around = source[q, start - 1 : start + CHUNK - 1] + source[q, start + 1 : start + CHUNK + 1]
                    target[q, rows] = centre[rows] * field - weight[rows] * (around + forth + back)
        return carry

    lax.fori_loop(0, NP // TOGETHER, probe_group, 0)
    copy.wait()


def inner_kernel(
    u1_in, u2_in, u0, kappa, ids, strips, kstrips, centre, weight,
    u1, u2, u3, u4, s, basis, moments, sums,
    edges, margins, scentre, sweight,
):
    del u1_in, u2_in
    inner = slice(TOP, TOP + N)
    s[0, 2, inner] = strips[2]
    for i in range(2):
        s[0, i, inner] = strips[i]
        square = strips[i] * strips[i]
        scentre[i, inner] = square * (kstrips[i] + 0.25)
        sweight[i, inner] = square * 0.0625
    for k in range(DEPTH):
        for start in range(TOP, TOP + N, 32):
            strip_step(k, s, edges, scentre, sweight, start, 32)
            if k == 2:
                outer_columns(s, margins, start, 32)
    fields = [u0, u1, u2, u3, u4]

    def probe_group(group, carry):
        probes = [(group * TOGETHER + j, j % 2) for j in range(TOGETHER)]
        for k in range(4):
            totals = [jnp.zeros((8, N), F32) for _ in probes]
            for start in range(TOP, TOP + N, CHUNK):
                for j, (q, parity) in enumerate(probes):
                    if k == 0:
                        result = completed(u1, edges, weight, q, parity, start, CHUNK)
                    elif k == 1:
                        result = second_completed(u2, margins, q, j, start, CHUNK)
                    else:
                        result = applied(fields, edges, centre, weight, k, q, parity, start, CHUNK)
                    fields[k + 1][q, start : start + CHUNK] = result
                    low, high = max(start, TOP + 8), min(start + CHUNK, TOP + N - 8)
                    totals[j] += folded(result[low - start : high - start])
            for (q, _), total in zip(probes, totals):
                moments[k, q] = total
        totals = [jnp.zeros((8, N), F32) for _ in probes]
        for start in range(TOP + 8, TOP + N - 8, FINAL):
            for j, (q, parity) in enumerate(probes):
                result = applied(fields, edges, centre, weight, 4, q, parity, start, FINAL)
                totals[j] += folded(result)
                trace_basis(fields, basis, kappa, q, start, FINAL, result)
        for (q, _), total in zip(probes, totals):
            moments[4, q] = total
        return carry

    lax.fori_loop(0, NP // TOGETHER, probe_group, 0)
    sums[...] = block_sums(basis, ids, 8, N - 8, UNROLL)


def outer_kernel(
    u0_in, u1_in, u2_in, u3_in, u4_in, s_in, basis_in,
    moments, sums, kappa, ids, kstrips, odd, even,
    u0, u1, u2, u3, u4, s, basis, message,
    edges, centre, weight, scentre, sweight,
):
    del u0_in, u1_in, u2_in, u3_in, u4_in, s_in, basis_in
    low = lax.axis_index("lon") % 2 == 0
    bands = (TOP - 8, TOP + N - 8)
    for start, inside, outside, if_low, if_high in (
        (bands[0], 8, 0, odd, even),
        (bands[1], 0, 8, even, odd),
    ):
        rows = slice(start + outside, start + outside + 8)
        own = slice(start + inside, start + inside + 8)
        here = slice(start + inside - TOP, start + inside - TOP + 8)
        halo = [jnp.where(low, if_low[i], if_high[i]) for i in range(SLOTS)]
        for q in range(NP):
            u0[q, rows] = halo[q]
        s[0, 2, rows] = halo[NP + 2]
        for i in range(2):
            s[0, i, rows] = halo[NP + i]
            for where, value, kvalue in ((rows, halo[NP + i], halo[NP + 3 + i]), (own, s[0, i, own], kstrips[i, here])):
                scentre[i, where] = value * value * (kvalue + 0.25)
                sweight[i, where] = value * value * 0.0625
        for where, value, kvalue in ((rows, halo[0], halo[NP + 5]), (own, u0[0, own], kappa[here])):
            centre[where] = value * value * (kvalue + 0.25)
            weight[where] = value * value * 0.0625
    fields = [u0, u1, u2, u3, u4]
    blank = jnp.zeros((8, N), F32)
    for row in (TOP - 16, TOP + N + 8):
        for field in fields:
            for q in range(NP):
                field[q, row : row + 8] = blank
        for k in range(DEPTH):
            for i in range(2):
                s[k, i, row : row + 8] = blank
    for k in range(DEPTH):
        for start in bands:
            strip_step(k, s, edges, scentre, sweight, start, 16)

    heads = []
    for k in range(4):
        stacked = []
        for q in range(NP):
            total = moments[k, q]
            for start, own in ((bands[0], 8), (bands[1], 0)):
                result = applied(fields, edges, centre, weight, k, q, q % 2, start, 16)
                fields[k + 1][q, start : start + 16] = result
                total += folded(result[own : own + 8])
            stacked.append(jnp.sum(total, axis=0, keepdims=True))
        heads.append(jnp.concatenate(stacked, axis=0))
    stacked = []
    for q in range(NP):
        total = moments[4, q]
        for start in (TOP, TOP + N - 8):
            result = applied(fields, edges, centre, weight, 4, q, q % 2, start, 8)
            total += folded(result)
            trace_basis(fields, basis, kappa, q, start, 8, result)
        stacked.append(jnp.sum(total, axis=0, keepdims=True))
    heads.append(jnp.concatenate(stacked, axis=0))
    total = sums[...] + block_sums(basis, ids, 0, 8, 8 // ABREAST) + block_sums(basis, ids, N - 8, N, 8 // ABREAST)
    ocean = u0[0, TOP : TOP + N]
    ocean = ocean * ocean

    ocean_sum = jnp.sum(jnp.sum(ocean, axis=0, keepdims=True), axis=1, keepdims=True)
    columns = [jnp.broadcast_to(ocean_sum, (NP, 1))]
    columns += [jnp.sum(head, axis=1, keepdims=True) for head in heads]
    wide = jnp.zeros((NP, NB), F32)
    spot = lax.broadcasted_iota(jnp.int32, (NP, NB), 1)
    coarse = F32(1.5 * 2**20)
    for k, column in enumerate(columns):
        head = (column + coarse) - coarse
        wide = jnp.where(spot == 2 * k, head, wide)
        wide = jnp.where(spot == 2 * k + 1, column - head, wide)
    half = 3 * NP // 2
    message[:half] = jnp.concatenate([total[:half], total[half:]], axis=1)
    message[half:] = jnp.concatenate([wide[: NP // 2], wide[NP // 2 :]], axis=1)


def two_sum(a, b):
    s = a + b
    t = s - a
    return s, (a - (s - t)) + (b - t)


def quick(a, b):
    s = a + b
    return s, b - (s - a)


def split(a):
    t = a * F32(4097.0)
    high = t - (t - a)
    return high, a - high


def mul(a, b):
    p = a[0] * b[0]
    ah, al = split(a[0])
    bh, bl = split(b[0])
    e = ((ah * bh - p) + ah * bl + al * bh) + al * bl
    return quick(p, e + (a[0] * b[1] + a[1] * b[0]))


def sub(a, b):
    s, e = two_sum(a[0], -b[0])
    return quick(s, e + (a[1] - b[1]))


def inverse(b):
    first = 1.0 / b[0]
    zero = jnp.zeros_like(first)
    rest = sub((jnp.ones_like(first), zero), mul(b, (first, zero)))
    return quick(first, first * rest[0])


def keep(ok, value, other):
    return tuple(jnp.where(ok, v, other) for v in value)


def solve(moment):
    g0, h1, h2, h3, h4, h5 = moment
    tiny = F32(2e-8)
    over = inverse(h1)
    l1, l2 = mul(h2, over), mul(h3, over)
    s11, s12, s22 = sub(h3, mul(h2, l1)), sub(h4, mul(h2, l2)), sub(h5, mul(h3, l2))
    y1, y2 = sub(h1, mul(g0, l1)), sub(h2, mul(g0, l2))
    ok1 = s11[0] > tiny * h3[0]
    over1 = keep(ok1, inverse(keep(ok1, s11, 1.0)), 0.0)
    l21 = mul(s12, over1)
    d2, z2 = sub(s22, mul(s12, l21)), sub(y2, mul(y1, l21))
    ok2 = ok1 & (d2[0] > tiny * h5[0])
    over2 = keep(ok2, inverse(keep(ok2, d2, 1.0)), 0.0)
    c2 = mul(z2, over2)
    c1 = mul(sub(y1, mul(s12, c2)), over1)
    c0 = mul(sub(sub(g0, mul(h2, c1)), mul(h3, c2)), over)
    return c0[0] + c0[1], c1[0] + c1[1], c2[0] + c2[1]


def combine_kernel(message, u0, u2, u4, basis, solution, trace, traces):
    half = 3 * NP // 2
    wide = jnp.concatenate([message[half:, :NB], message[half:, NB:]], axis=0)
    sums = jnp.concatenate([message[:half, :NB], message[:half, NB:]], axis=0)
    moment = []
    for k in range(6):
        head = wide[:, 2 * k : 2 * k + 1]
        rest = wide[:, 2 * k + 1 : 2 * k + 2]
        moment.append(quick(jnp.broadcast_to(head, (NP, N)), jnp.broadcast_to(rest, (NP, N))))
    c0, c1, c2 = solve(moment)
    cells = F32(N * N * 128 // NB)
    total = c0[:, :NB] * sums[:NP] + c1[:, :NB] * sums[NP : 2 * NP] + c2[:, :NB] * sums[2 * NP :]
    traces[...] = total / cells
    for q in range(NP):
        a0, a1, a2 = (c[q : q + 1] for c in (c0, c1, c2))
        solution[q] = a0 * u0[q, TOP : TOP + N] + a1 * u2[q, TOP : TOP + N] + a2 * u4[q, TOP : TOP + N]
        rows = [slice((i * NP + q) * PITCH, (i * NP + q) * PITCH + N) for i in range(3)]
        trace[q] = a0 * basis[rows[0]] + a1 * basis[rows[1]] + a2 * basis[rows[2]]


def pairs(count, offset, closed):
    out = []
    for i in range(offset, count, 2):
        j = (i + 1) % count
        if i + 1 < count or closed:
            out += [(i, j), (j, i)]
    return out


def swap(odd, even, axis, closed):
    count = lax.axis_size(axis)
    odd = lax.ppermute(odd, axis, pairs(count, 1, closed))
    even = lax.ppermute(even, axis, pairs(count, 0, closed))
    return odd, even


def everywhere(value):
    def sent(axis, bits):
        return lax.ppermute(value, axis, [(i, i ^ bits) for i in range(lax.axis_size(axis))])

    value = value + sent("lat", 1)
    for axis, unit in (("lat", 2), ("lon", 1), ("lon", 4)):
        near, far, across = sent(axis, unit), sent(axis, 3 * unit), sent(axis, 2 * unit)
        value = (value + near) + (far + across)
    return value


def per_device(signs, mask, kappa, ids):
    edge, field, strip, plane = (N, N), (NP, ROWS, N), (2, ROWS, N), (ROWS, N)
    halo = (SLOTS, 8, N)
    flat = (3 * NP * PITCH, N)
    ints = jax.ShapeDtypeStruct(edge, jnp.int32)
    signs, mask, kappa, ids = (pltpu.with_memory_space_constraint(x, pltpu.HBM) for x in (signs, mask, kappa, ids))
    own_odd, own_even, u0, kappa = call(
        pack_kernel,
        [edge, edge, field, edge],
        8,
        [
            pltpu.VMEM((NP, N, N), jnp.int32),
            pltpu.VMEM(edge, jnp.int32),
            pltpu.VMEM((NP // 2, 2 * N, 2 * N), BF16),
            pltpu.SemaphoreType.DMA((2 + PARTS,)),
        ],
        specs=[FAR] * 3,
    )(signs, mask, kappa)
    odd, even = swap(own_odd, own_even, "lat", False)
    u1, u2, centre, weight, ids = call(
        first_kernel,
        [field, field, plane, plane, ints],
        8,
        [pltpu.SemaphoreType.DMA],
        specs=[NEAR, NEAR, FAR],
        micros=2,
    )(u0, kappa, ids)
    strips, kstrips, row_odd, row_even = call(strips_kernel, [(3, N, N), (2, N, N), halo, halo], 8)(
        odd, even, own_odd, own_even, kappa, u0, centre
    )
    row_odd, row_even = swap(row_odd, row_even, "lon", True)
    coefficients = [pltpu.VMEM(shape, F32) for shape in (plane, plane, strip, strip)]
    edges = pltpu.VMEM((DEPTH, 2, ROWS, N), F32)
    u1, u2, u3, u4, s, basis, moments, sums = call(
        inner_kernel,
        [field, field, field, field, (DEPTH, 3, ROWS, N), flat, (DEPTH, NP, 8, N), (3 * NP, NB)],
        24,
        [edges, pltpu.VMEM((4, ROWS, N), F32), *coefficients[2:]],
        aliases={0: 0, 1: 1},
        micros=8,
    )(u1, u2, u0, kappa, ids, strips, kstrips, centre, weight)
    u0, u1, u2, u3, u4, s, basis, message = call(
        outer_kernel,
        [field, field, field, field, field, (DEPTH, 3, ROWS, N), flat, (2 * NP, N)],
        24,
        [edges, *coefficients],
        aliases={i: i for i in range(7)},
    )(u0, u1, u2, u3, u4, s, basis, moments, sums, kappa, ids, kstrips, row_odd, row_even)
    message = everywhere(message)
    out = (NP, N, N)
    return tuple(call(combine_kernel, [out, out, (NP, NB)], 16)(message, u0, u2, u4, basis))


def solution(mesh):
    placed = (P(None, "lon", "lat"), P("lon", "lat"), P("lon", "lat"), P("lon", "lat"))
    return jax.shard_map(
        per_device,
        mesh=mesh,
        in_specs=placed,
        out_specs=(P(None, "lon", "lat"), P(None, "lon", "lat"), P()),
        check_vma=False,
    )
```

```python
import jax
import jax.numpy as jnp
from jax import lax
from jax.experimental import pallas as pl
from jax.experimental.pallas import tpu as pltpu
from jax.sharding import PartitionSpec as P

F32 = jnp.float32
BF16 = jnp.bfloat16
NB = 64
NP = 16
N = 128
DEPTH = 5
W = DEPTH * NP
SLOTS = NP + 6
TOP = 16
ROWS = N + 2 * TOP
MIB = 1 << 20
FAR = pl.BlockSpec(memory_space=pltpu.HBM)
NEAR = pl.BlockSpec(memory_space=pltpu.VMEM)
CHUNK = 32
FINAL = 56
PITCH = N + 8
UNROLL = 28
ABREAST = 4
TOGETHER = 16
PARTS = 4


def lanes(rows=8):
    return lax.broadcasted_iota(jnp.int32, (rows, N), 1)


def call(kernel, outs, mib, scratch=(), aliases=None, specs=None, micros=1):
    extra = {} if specs is None else {"in_specs": specs}
    return pl.pallas_call(
        kernel,
        out_shape=[o if isinstance(o, jax.ShapeDtypeStruct) else jax.ShapeDtypeStruct(o, F32) for o in outs],
        scratch_shapes=list(scratch),
        input_output_aliases=aliases or {},
        compiler_params=pltpu.CompilerParams(vmem_limit_bytes=mib * MIB),
        cost_estimate=pl.CostEstimate(flops=0, bytes_accessed=micros * 3_000_000, transcendentals=0),
        **extra,
    )


def pack_kernel(
    signs_hbm, mask_hbm, kappa_hbm,
    odd_ref, even_ref, u0, kappa,
    signs, mask, picks, sems,
):
    part = NP // PARTS
    copies = [
        pltpu.make_async_copy(mask_hbm, mask, sems.at[0]),
        pltpu.make_async_copy(kappa_hbm, kappa, sems.at[1]),
    ]
    for i in range(PARTS):
        probes = pl.ds(i * part, part)
        copies.append(pltpu.make_async_copy(signs_hbm.at[probes], signs.at[probes], sems.at[2 + i]))
    for copy in (copies[0], *copies[2:], copies[1]):
        copy.start()
    lane = lax.broadcasted_iota(jnp.int32, (1, 2 * N), 1)
    side, spot = lane // N, lane % N
    column, probe = spot // NP, spot % NP
    row = lax.broadcasted_iota(jnp.int32, (2 * N, 2 * N), 0)
    for pair in range(NP // 2):
        source = column + (N - DEPTH) * side + N * (probe - 2 * pair)
        wanted = (probe // 2 == pair) & (column < DEPTH)
        source = jnp.where(wanted, source, -1)
        picks[pair] = (row == source).astype(F32).astype(BF16)
    total = jnp.zeros((N, 2 * N), F32)
    copies[0].wait()
    ocean = mask[...].astype(F32)
    for pair in range(NP // 2):
        if pair % (part // 2) == 0:
            copies[2 + pair // (part // 2)].wait()
        fields = []
        for q in (2 * pair, 2 * pair + 1):
            field = signs[q].astype(F32) * ocean
            u0[q, TOP : TOP + N] = field
            fields.append(field.astype(BF16))
        total += jnp.dot(jnp.concatenate(fields, axis=1), picks[pair], preferred_element_type=F32)
    here = lanes(N)
    in_kappa = (here >= W) & (here < W + DEPTH)
    copies[1].wait()
    left = jnp.where(in_kappa, pltpu.roll(kappa[...], W, 1), total[:, :N])
    right = jnp.where(in_kappa, pltpu.roll(kappa[...], W + DEPTH, 1), total[:, N:])
    low = lax.axis_index("lat") % 2 == 0
    even_ref[...] = jnp.where(low, right, left)
    odd_ref[...] = jnp.where(low, left, right)


def strips_kernel(odd, even, own_odd, own_even, kappa, u0, after, strips, kstrips, odd_ref, even_ref):
    del after
    low = lax.axis_index("lat") % 2 == 0
    from_left = jnp.where(low, odd[...], even[...])
    from_right = jnp.where(low, even[...], odd[...])
    own_left = jnp.where(low, own_odd[...], own_even[...])
    own_right = jnp.where(low, own_even[...], own_odd[...])
    here = lanes(N)
    strips[0] = jnp.where(here < W, from_left, pltpu.roll(own_left, W, 1))
    strips[1] = jnp.where(here < 3 * NP, pltpu.roll(own_right, N - 2 * NP, 1), pltpu.roll(from_right, 3 * NP, 1))
    strips[2] = jnp.where(here < NP, pltpu.roll(own_right, N - NP, 1), pltpu.roll(own_left, N // 2, 1))
    pick_row = lax.broadcasted_iota(jnp.int32, (N, N), 0)
    pick_col = lax.broadcasted_iota(jnp.int32, (N, N), 1)
    for i, (first, second, skip) in enumerate(((from_left, own_left, 0), (own_right, from_right, 2))):
        pair = jnp.where(here < W + DEPTH, first, pltpu.roll(second, DEPTH, 1))
        spread = (pick_row == W + skip + pick_col // NP).astype(F32)
        kstrips[i] = jnp.dot(pair, spread, precision=lax.Precision.HIGHEST, preferred_element_type=F32)
    low = lax.axis_index("lon") % 2 == 0
    for slot in range(SLOTS):
        if slot < NP:
            top, bottom = u0[slot, TOP : TOP + 8], u0[slot, TOP + N - 8 : TOP + N]
        else:
            if slot < NP + 3:
                field = strips.at[slot - NP]
            elif slot < NP + 5:
                field = kstrips.at[slot - NP - 3]
            else:
                field = kappa
            top, bottom = field[:8], field[N - 8 :]
        even_ref[slot] = jnp.where(low, bottom, top)
        odd_ref[slot] = jnp.where(low, top, bottom)


def strip_step(k, s, edges, scentre, sweight, start, size):
    rows = slice(start, start + size)
    here = lanes(size)
    now = [s[k, i, rows] for i in range(2)]
    moved = pltpu.roll(now[1], NP - 1, 1)
    edges[k, 0, rows] = jnp.where(here % 2 == 0, now[0], moved)
    edges[k, 1, rows] = jnp.where(here % 2 == 0, moved, now[0])
    if k == DEPTH - 1:
        return
    for i in range(2):
        forth, back = pltpu.roll(now[i], NP, 1), pltpu.roll(now[i], N - NP, 1)
        if k == 0 and i == 0:
            back = jnp.where(here >= N - NP, s[0, 2, rows], back)
        if k == 0 and i == 1:
            forth = jnp.where(here < NP, s[0, 2, rows], forth)
        around = s[k, i, start - 1 : start + size - 1] + s[k, i, start + 1 : start + size + 1]
        s[k + 1, i, rows] = scentre[i, rows] * now[i] - sweight[i, rows] * (around + forth + back)


def applied(fields, edges, centre, weight, k, q, parity, start, size):
    rows = slice(start, start + size)
    here = lanes(size)
    field = fields[k][q, rows]
    edge = pltpu.roll(edges[k, parity, rows], N - NP * 4 - q, 1)
    forth = jnp.where(here == 0, edge, pltpu.roll(field, 1, 1))
    back = jnp.where(here == N - 1, edge, pltpu.roll(field, N - 1, 1))
    around = fields[k][q, start - 1 : start + size - 1] + fields[k][q, start + 1 : start + size + 1]
    return centre[rows] * field - weight[rows] * (around + forth + back)


def completed(u1, edges, weight, q, parity, start, size):
    rows = slice(start, start + size)
    here = lanes(size)
    edge = pltpu.roll(edges[0, parity, rows], N - NP * 4 - q, 1)
    edge = jnp.where((here == 0) | (here == N - 1), edge, 0.0)
    return u1[q, rows] - weight[rows] * edge


def outer_columns(s, margins, start, size):
    rows = slice(start, start + size)
    here = lanes(size)
    left, right = s[2, 0, rows], s[2, 1, rows]
    columns = (
        pltpu.roll(left, N - NP, 1),
        pltpu.roll(left, N - 2 * NP + 1, 1),
        pltpu.roll(right, 3 * NP - 2, 1),
        pltpu.roll(right, 2 * NP - 1, 1),
    )
    for j in range(4):
        place = (here + 4 - j) % 4
        value = jnp.where(place == 0, columns[0], columns[1])
        margins[j, rows] = jnp.where(place == 2, columns[2], jnp.where(place == 3, columns[3], value))


def second_completed(u2, margins, q, j, start, size):
    rows = slice(start, start + size)
    here = lanes(size)
    margin = pltpu.roll(margins[j % 4, rows], N - NP * 4 - q, 1)
    return jnp.where((here < 2) | (here >= N - 2), margin, u2[q, rows])


def folded(value):
    return jnp.sum((value * value).reshape(-1, 8, N), axis=0)


def trace_basis(fields, basis, kappa, q, start, size, fifth):
    rows = slice(start, start + size)
    scale = kappa[start - TOP : start - TOP + size]
    v0, v1, v2, v3, v4 = (field[q, rows] for field in fields)
    one, zero = scale * v1, scale * v0
    for i, value in enumerate((one * (v0 + v0), one * v2 + zero * v3, one * v4 + zero * fifth)):
        base = pl.multiple_of((i * NP + q) * PITCH + (start - TOP), 8)
        basis[pl.ds(base, size)] = value


def block_sums(basis, ids, first, last, unroll):
    block = lax.broadcasted_iota(jnp.int32, (NB, N), 0)

    def blocks(step, total):
        high, rest, hot = [], [], []
        for row in [step * ABREAST + i for i in range(ABREAST)]:
            data = basis[pl.ds(row, 3 * NP, stride=PITCH)]
            high.append(data.astype(BF16))
            rest.append((data - high[-1].astype(F32)).astype(BF16))
            hot.append((ids[pl.ds(row, 1)] == block).astype(F32).astype(BF16))
        both = jnp.concatenate([jnp.concatenate(high, axis=1), jnp.concatenate(rest, axis=1)], axis=0)
        hot = jnp.concatenate(hot, axis=1)
        return total + lax.dot_general(both, hot, (((1,), (1,)), ((), ())), preferred_element_type=F32)

    total = lax.fori_loop(first // ABREAST, last // ABREAST, blocks, jnp.zeros((6 * NP, NB), F32), unroll=unroll)
    return total[: 3 * NP] + total[3 * NP :]


def first_kernel(u0, kappa, ids_hbm, u1, u2, centre, weight, ids, sem):
    copy = pltpu.make_async_copy(ids_hbm, ids, sem)
    copy.start()
    inner = slice(TOP, TOP + N)
    ocean = u0[0, inner] * u0[0, inner]
    centre[inner] = ocean * (kappa[...] + 0.25)
    weight[inner] = ocean * 0.0625
    here = lanes(CHUNK)

    def probe_group(group, carry):
        for source, target in ((u0, u1), (u1, u2)):
            for start in range(TOP, TOP + N, CHUNK):
                for j in range(TOGETHER):
                    q = group * TOGETHER + j
                    rows = slice(start, start + CHUNK)
                    field = source[q, rows]
                    forth = jnp.where(here == 0, 0.0, pltpu.roll(field, 1, 1))
                    back = jnp.where(here == N - 1, 0.0, pltpu.roll(field, N - 1, 1))
                    around = source[q, start - 1 : start + CHUNK - 1] + source[q, start + 1 : start + CHUNK + 1]
                    target[q, rows] = centre[rows] * field - weight[rows] * (around + forth + back)
        return carry

    lax.fori_loop(0, NP // TOGETHER, probe_group, 0)
    copy.wait()


def inner_kernel(
    u1_in, u2_in, u0, kappa, ids, strips, kstrips, centre, weight,
    u1, u2, u3, u4, s, basis, moments, sums,
    edges, margins, scentre, sweight,
):
    del u1_in, u2_in
    inner = slice(TOP, TOP + N)
    s[0, 2, inner] = strips[2]
    for i in range(2):
        s[0, i, inner] = strips[i]
        square = strips[i] * strips[i]
        scentre[i, inner] = square * (kstrips[i] + 0.25)
        sweight[i, inner] = square * 0.0625
    for k in range(DEPTH):
        for start in range(TOP, TOP + N, 32):
            strip_step(k, s, edges, scentre, sweight, start, 32)
            if k == 2:
                outer_columns(s, margins, start, 32)
    fields = [u0, u1, u2, u3, u4]

    def probe_group(group, carry):
        probes = [(group * TOGETHER + j, j % 2) for j in range(TOGETHER)]
        for k in range(4):
            totals = [jnp.zeros((8, N), F32) for _ in probes]
            for start in range(TOP, TOP + N, CHUNK):
                for j, (q, parity) in enumerate(probes):
                    if k == 0:
                        result = completed(u1, edges, weight, q, parity, start, CHUNK)
                    elif k == 1:
                        result = second_completed(u2, margins, q, j, start, CHUNK)
                    else:
                        result = applied(fields, edges, centre, weight, k, q, parity, start, CHUNK)
                    fields[k + 1][q, start : start + CHUNK] = result
                    low, high = max(start, TOP + 8), min(start + CHUNK, TOP + N - 8)
                    totals[j] += folded(result[low - start : high - start])
            for (q, _), total in zip(probes, totals):
                moments[k, q] = total
        totals = [jnp.zeros((8, N), F32) for _ in probes]
        for start in range(TOP + 8, TOP + N - 8, FINAL):
            for j, (q, parity) in enumerate(probes):
                result = applied(fields, edges, centre, weight, 4, q, parity, start, FINAL)
                totals[j] += folded(result)
                trace_basis(fields, basis, kappa, q, start, FINAL, result)
        for (q, _), total in zip(probes, totals):
            moments[4, q] = total
        return carry

    lax.fori_loop(0, NP // TOGETHER, probe_group, 0)
    sums[...] = block_sums(basis, ids, 8, N - 8, UNROLL)


def outer_kernel(
    u0_in, u1_in, u2_in, u3_in, u4_in, s_in, basis_in,
    moments, sums, kappa, ids, kstrips, odd, even,
    u0, u1, u2, u3, u4, s, basis, message,
    edges, centre, weight, scentre, sweight,
):
    del u0_in, u1_in, u2_in, u3_in, u4_in, s_in, basis_in
    low = lax.axis_index("lon") % 2 == 0
    bands = (TOP - 8, TOP + N - 8)
    for start, inside, outside, if_low, if_high in (
        (bands[0], 8, 0, odd, even),
        (bands[1], 0, 8, even, odd),
    ):
        rows = slice(start + outside, start + outside + 8)
        own = slice(start + inside, start + inside + 8)
        here = slice(start + inside - TOP, start + inside - TOP + 8)
        halo = [jnp.where(low, if_low[i], if_high[i]) for i in range(SLOTS)]
        for q in range(NP):
            u0[q, rows] = halo[q]
        s[0, 2, rows] = halo[NP + 2]
        for i in range(2):
            s[0, i, rows] = halo[NP + i]
            for where, value, kvalue in ((rows, halo[NP + i], halo[NP + 3 + i]), (own, s[0, i, own], kstrips[i, here])):
                scentre[i, where] = value * value * (kvalue + 0.25)
                sweight[i, where] = value * value * 0.0625
        for where, value, kvalue in ((rows, halo[0], halo[NP + 5]), (own, u0[0, own], kappa[here])):
            centre[where] = value * value * (kvalue + 0.25)
            weight[where] = value * value * 0.0625
    fields = [u0, u1, u2, u3, u4]
    blank = jnp.zeros((8, N), F32)
    for row in (TOP - 16, TOP + N + 8):
        for field in fields:
            for q in range(NP):
                field[q, row : row + 8] = blank
        for k in range(DEPTH):
            for i in range(2):
                s[k, i, row : row + 8] = blank
    for k in range(DEPTH):
        for start in bands:
            strip_step(k, s, edges, scentre, sweight, start, 16)

    heads = []
    for k in range(4):
        stacked = []
        for q in range(NP):
            total = moments[k, q]
            for start, own in ((bands[0], 8), (bands[1], 0)):
                result = applied(fields, edges, centre, weight, k, q, q % 2, start, 16)
                fields[k + 1][q, start : start + 16] = result
                total += folded(result[own : own + 8])
            stacked.append(jnp.sum(total, axis=0, keepdims=True))
        heads.append(jnp.concatenate(stacked, axis=0))
    stacked = []
    for q in range(NP):
        total = moments[4, q]
        for start in (TOP, TOP + N - 8):
            result = applied(fields, edges, centre, weight, 4, q, q % 2, start, 8)
            total += folded(result)
            trace_basis(fields, basis, kappa, q, start, 8, result)
        stacked.append(jnp.sum(total, axis=0, keepdims=True))
    heads.append(jnp.concatenate(stacked, axis=0))
    total = sums[...] + block_sums(basis, ids, 0, 8, 8 // ABREAST) + block_sums(basis, ids, N - 8, N, 8 // ABREAST)
    ocean = u0[0, TOP : TOP + N]
    ocean = ocean * ocean

    ocean_sum = jnp.sum(jnp.sum(ocean, axis=0, keepdims=True), axis=1, keepdims=True)
    columns = [jnp.broadcast_to(ocean_sum, (NP, 1))]
    columns += [jnp.sum(head, axis=1, keepdims=True) for head in heads]
    wide = jnp.zeros((NP, NB), F32)
    spot = lax.broadcasted_iota(jnp.int32, (NP, NB), 1)
    coarse = F32(1.5 * 2**20)
    for k, column in enumerate(columns):
        head = (column + coarse) - coarse
        wide = jnp.where(spot == 2 * k, head, wide)
        wide = jnp.where(spot == 2 * k + 1, column - head, wide)
    half = 3 * NP // 2
    message[:half] = jnp.concatenate([total[:half], total[half:]], axis=1)
    message[half:] = jnp.concatenate([wide[: NP // 2], wide[NP // 2 :]], axis=1)


def two_sum(a, b):
    s = a + b
    t = s - a
    return s, (a - (s - t)) + (b - t)


def quick(a, b):
    s = a + b
    return s, b - (s - a)


def split(a):
    t = a * F32(4097.0)
    high = t - (t - a)
    return high, a - high


def mul(a, b):
    p = a[0] * b[0]
    ah, al = split(a[0])
    bh, bl = split(b[0])
    e = ((ah * bh - p) + ah * bl + al * bh) + al * bl
    return quick(p, e + (a[0] * b[1] + a[1] * b[0]))


def sub(a, b):
    s, e = two_sum(a[0], -b[0])
    return quick(s, e + (a[1] - b[1]))


def inverse(b):
    first = 1.0 / b[0]
    zero = jnp.zeros_like(first)
    rest = sub((jnp.ones_like(first), zero), mul(b, (first, zero)))
    return quick(first, first * rest[0])


def keep(ok, value, other):
    return tuple(jnp.where(ok, v, other) for v in value)


def solve(moment):
    g0, h1, h2, h3, h4, h5 = moment
    tiny = F32(2e-8)
    over = inverse(h1)
    l1, l2 = mul(h2, over), mul(h3, over)
    s11, s12, s22 = sub(h3, mul(h2, l1)), sub(h4, mul(h2, l2)), sub(h5, mul(h3, l2))
    y1, y2 = sub(h1, mul(g0, l1)), sub(h2, mul(g0, l2))
    ok1 = s11[0] > tiny * h3[0]
    over1 = keep(ok1, inverse(keep(ok1, s11, 1.0)), 0.0)
    l21 = mul(s12, over1)
    d2, z2 = sub(s22, mul(s12, l21)), sub(y2, mul(y1, l21))
    ok2 = ok1 & (d2[0] > tiny * h5[0])
    over2 = keep(ok2, inverse(keep(ok2, d2, 1.0)), 0.0)
    c2 = mul(z2, over2)
    c1 = mul(sub(y1, mul(s12, c2)), over1)
    c0 = mul(sub(sub(g0, mul(h2, c1)), mul(h3, c2)), over)
    return c0[0] + c0[1], c1[0] + c1[1], c2[0] + c2[1]


def combine_kernel(message, u0, u2, u4, basis, solution, trace, traces):
    half = 3 * NP // 2
    wide = jnp.concatenate([message[half:, :NB], message[half:, NB:]], axis=0)
    sums = jnp.concatenate([message[:half, :NB], message[:half, NB:]], axis=0)
    moment = []
    for k in range(6):
        head = wide[:, 2 * k : 2 * k + 1]
        rest = wide[:, 2 * k + 1 : 2 * k + 2]
        moment.append(quick(jnp.broadcast_to(head, (NP, N)), jnp.broadcast_to(rest, (NP, N))))
    c0, c1, c2 = solve(moment)
    cells = F32(N * N * 128 // NB)
    total = c0[:, :NB] * sums[:NP] + c1[:, :NB] * sums[NP : 2 * NP] + c2[:, :NB] * sums[2 * NP :]
    traces[...] = total / cells
    for q in range(NP):
        a0, a1, a2 = (c[q : q + 1] for c in (c0, c1, c2))
        solution[q] = a0 * u0[q, TOP : TOP + N] + a1 * u2[q, TOP : TOP + N] + a2 * u4[q, TOP : TOP + N]
        rows = [slice((i * NP + q) * PITCH, (i * NP + q) * PITCH + N) for i in range(3)]
        trace[q] = a0 * basis[rows[0]] + a1 * basis[rows[1]] + a2 * basis[rows[2]]


def pairs(count, offset, closed):
    out = []
    for i in range(offset, count, 2):
        j = (i + 1) % count
        if i + 1 < count or closed:
            out += [(i, j), (j, i)]
    return out


def swap(odd, even, axis, closed):
    count = lax.axis_size(axis)
    odd = lax.ppermute(odd, axis, pairs(count, 1, closed))
    even = lax.ppermute(even, axis, pairs(count, 0, closed))
    return odd, even


def everywhere(value):
    def sent(axis, bits):
        return lax.ppermute(value, axis, [(i, i ^ bits) for i in range(lax.axis_size(axis))])

    value = value + sent("lat", 1)
    for axis, unit in (("lat", 2), ("lon", 1), ("lon", 4)):
        near, far, across = sent(axis, unit), sent(axis, 3 * unit), sent(axis, 2 * unit)
        value = (value + near) + (far + across)
    return value


def per_device(signs, mask, kappa, ids):
    edge, field, strip, plane = (N, N), (NP, ROWS, N), (2, ROWS, N), (ROWS, N)
    halo = (SLOTS, 8, N)
    flat = (3 * NP * PITCH, N)
    ints = jax.ShapeDtypeStruct(edge, jnp.int32)
    signs, mask, kappa, ids = (pltpu.with_memory_space_constraint(x, pltpu.HBM) for x in (signs, mask, kappa, ids))
    own_odd, own_even, u0, kappa = call(
        pack_kernel,
        [edge, edge, field, edge],
        8,
        [
            pltpu.VMEM((NP, N, N), jnp.int32),
            pltpu.VMEM(edge, jnp.int32),
            pltpu.VMEM((NP // 2, 2 * N, 2 * N), BF16),
            pltpu.SemaphoreType.DMA((2 + PARTS,)),
        ],
        specs=[FAR] * 3,
    )(signs, mask, kappa)
    odd, even = swap(own_odd, own_even, "lat", False)
    u1, u2, centre, weight, ids = call(
        first_kernel,
        [field, field, plane, plane, ints],
        8,
        [pltpu.SemaphoreType.DMA],
        specs=[NEAR, NEAR, FAR],
        micros=2,
    )(u0, kappa, ids)
    strips, kstrips, row_odd, row_even = call(strips_kernel, [(3, N, N), (2, N, N), halo, halo], 8)(
        odd, even, own_odd, own_even, kappa, u0, centre
    )
    row_odd, row_even = swap(row_odd, row_even, "lon", True)
    coefficients = [pltpu.VMEM(shape, F32) for shape in (plane, plane, strip, strip)]
    edges = pltpu.VMEM((DEPTH, 2, ROWS, N), F32)
    u1, u2, u3, u4, s, basis, moments, sums = call(
        inner_kernel,
        [field, field, field, field, (DEPTH, 3, ROWS, N), flat, (DEPTH, NP, 8, N), (3 * NP, NB)],
        24,
        [edges, pltpu.VMEM((4, ROWS, N), F32), *coefficients[2:]],
        aliases={0: 0, 1: 1},
        micros=8,
    )(u1, u2, u0, kappa, ids, strips, kstrips, centre, weight)
    u0, u1, u2, u3, u4, s, basis, message = call(
        outer_kernel,
        [field, field, field, field, field, (DEPTH, 3, ROWS, N), flat, (2 * NP, N)],
        24,
        [edges, *coefficients],
        aliases={i: i for i in range(7)},
    )(u0, u1, u2, u3, u4, s, basis, moments, sums, kappa, ids, kstrips, row_odd, row_even)
    message = everywhere(message)
    out = (NP, N, N)
    return tuple(call(combine_kernel, [out, out, (NP, NB)], 16)(message, u0, u2, u4, basis))


def solution(mesh):
    placed = (P(None, "lon", "lat"), P("lon", "lat"), P("lon", "lat"), P("lon", "lat"))
    return jax.shard_map(
        per_device,
        mesh=mesh,
        in_specs=placed,
        out_specs=(P(None, "lon", "lat"), P(None, "lon", "lat"), P()),
        check_vma=False,
    )
```

```python
import jax
import jax.numpy as jnp
from jax import lax
from jax.experimental import pallas as pl
from jax.experimental.pallas import tpu as pltpu
from jax.sharding import PartitionSpec as P

F32 = jnp.float32
BF16 = jnp.bfloat16
NB = 64
NP = 16
N = 128
DEPTH = 5
W = DEPTH * NP
SLOTS = NP + 6
TOP = 16
ROWS = N + 2 * TOP
MIB = 1 << 20
FAR = pl.BlockSpec(memory_space=pltpu.HBM)
NEAR = pl.BlockSpec(memory_space=pltpu.VMEM)
CHUNK = 32
FINAL = 56
PITCH = N + 8
UNROLL = 28
ABREAST = 4
TOGETHER = 16
PARTS = 4


def lanes(rows=8):
    return lax.broadcasted_iota(jnp.int32, (rows, N), 1)


def call(kernel, outs, mib, scratch=(), aliases=None, specs=None, micros=1):
    extra = {} if specs is None else {"in_specs": specs}
    return pl.pallas_call(
        kernel,
        out_shape=[o if isinstance(o, jax.ShapeDtypeStruct) else jax.ShapeDtypeStruct(o, F32) for o in outs],
        scratch_shapes=list(scratch),
        input_output_aliases=aliases or {},
        compiler_params=pltpu.CompilerParams(vmem_limit_bytes=mib * MIB),
        cost_estimate=pl.CostEstimate(flops=0, bytes_accessed=micros * 3_000_000, transcendentals=0),
        **extra,
    )


def pack_kernel(
    signs_hbm, mask_hbm, kappa_hbm,
    odd_ref, even_ref, signs, mask, kappa,
    picks, sems,
):
    part = NP // PARTS
    copies = [
        pltpu.make_async_copy(mask_hbm, mask, sems.at[0]),
        pltpu.make_async_copy(kappa_hbm, kappa, sems.at[1]),
    ]
    for i in range(PARTS):
        probes = pl.ds(i * part, part)
        copies.append(pltpu.make_async_copy(signs_hbm.at[probes], signs.at[probes], sems.at[2 + i]))
    for copy in (copies[0], *copies[2:], copies[1]):
        copy.start()
    lane = lax.broadcasted_iota(jnp.int32, (1, 2 * N), 1)
    side, spot = lane // N, lane % N
    column, probe = spot // NP, spot % NP
    row = lax.broadcasted_iota(jnp.int32, (2 * N, 2 * N), 0)
    for pair in range(NP // 2):
        source = column + (N - DEPTH) * side + N * (probe - 2 * pair)
        wanted = (probe // 2 == pair) & (column < DEPTH)
        source = jnp.where(wanted, source, -1)
        picks[pair] = (row == source).astype(F32).astype(BF16)
    total = jnp.zeros((N, 2 * N), F32)
    copies[0].wait()
    ocean = mask[...].astype(F32)
    for pair in range(NP // 2):
        if pair % (part // 2) == 0:
            copies[2 + pair // (part // 2)].wait()
        fields = []
        for q in (2 * pair, 2 * pair + 1):
            field = signs[q].astype(F32) * ocean
            fields.append(field.astype(BF16))
        total += jnp.dot(jnp.concatenate(fields, axis=1), picks[pair], preferred_element_type=F32)
    here = lanes(N)
    in_kappa = (here >= W) & (here < W + DEPTH)
    copies[1].wait()
    left = jnp.where(in_kappa, pltpu.roll(kappa[...], W, 1), total[:, :N])
    right = jnp.where(in_kappa, pltpu.roll(kappa[...], W + DEPTH, 1), total[:, N:])
    low = lax.axis_index("lat") % 2 == 0
    even_ref[...] = jnp.where(low, right, left)
    odd_ref[...] = jnp.where(low, left, right)


def strips_kernel(odd, even, own_odd, own_even, kappa, u0, after, strips, kstrips, odd_ref, even_ref):
    del after
    low = lax.axis_index("lat") % 2 == 0
    from_left = jnp.where(low, odd[...], even[...])
    from_right = jnp.where(low, even[...], odd[...])
    own_left = jnp.where(low, own_odd[...], own_even[...])
    own_right = jnp.where(low, own_even[...], own_odd[...])
    here = lanes(N)
    strips[0] = jnp.where(here < W, from_left, pltpu.roll(own_left, W, 1))
    strips[1] = jnp.where(here < 3 * NP, pltpu.roll(own_right, N - 2 * NP, 1), pltpu.roll(from_right, 3 * NP, 1))
    strips[2] = jnp.where(here < NP, pltpu.roll(own_right, N - NP, 1), pltpu.roll(own_left, N // 2, 1))
    pick_row = lax.broadcasted_iota(jnp.int32, (N, N), 0)
    pick_col = lax.broadcasted_iota(jnp.int32, (N, N), 1)
    for i, (first, second, skip) in enumerate(((from_left, own_left, 0), (own_right, from_right, 2))):
        pair = jnp.where(here < W + DEPTH, first, pltpu.roll(second, DEPTH, 1))
        spread = (pick_row == W + skip + pick_col // NP).astype(F32)
        kstrips[i] = jnp.dot(pair, spread, precision=lax.Precision.HIGHEST, preferred_element_type=F32)
    low = lax.axis_index("lon") % 2 == 0
    for slot in range(SLOTS):
        if slot < NP:
            top, bottom = u0[slot, TOP : TOP + 8], u0[slot, TOP + N - 8 : TOP + N]
        else:
            if slot < NP + 3:
                field = strips.at[slot - NP]
            elif slot < NP + 5:
                field = kstrips.at[slot - NP - 3]
            else:
                field = kappa
            top, bottom = field[:8], field[N - 8 :]
        even_ref[slot] = jnp.where(low, bottom, top)
        odd_ref[slot] = jnp.where(low, top, bottom)


def strip_step(k, s, edges, scentre, sweight, start, size):
    rows = slice(start, start + size)
    here = lanes(size)
    now = [s[k, i, rows] for i in range(2)]
    moved = pltpu.roll(now[1], NP - 1, 1)
    edges[k, 0, rows] = jnp.where(here % 2 == 0, now[0], moved)
    edges[k, 1, rows] = jnp.where(here % 2 == 0, moved, now[0])
    if k == DEPTH - 1:
        return
    for i in range(2):
        forth, back = pltpu.roll(now[i], NP, 1), pltpu.roll(now[i], N - NP, 1)
        if k == 0 and i == 0:
            back = jnp.where(here >= N - NP, s[0, 2, rows], back)
        if k == 0 and i == 1:
            forth = jnp.where(here < NP, s[0, 2, rows], forth)
        around = s[k, i, start - 1 : start + size - 1] + s[k, i, start + 1 : start + size + 1]
        s[k + 1, i, rows] = scentre[i, rows] * now[i] - sweight[i, rows] * (around + forth + back)


def applied(fields, edges, centre, weight, k, q, parity, start, size):
    rows = slice(start, start + size)
    here = lanes(size)
    field = fields[k][q, rows]
    edge = pltpu.roll(edges[k, parity, rows], N - NP * 4 - q, 1)
    forth = jnp.where(here == 0, edge, pltpu.roll(field, 1, 1))
    back = jnp.where(here == N - 1, edge, pltpu.roll(field, N - 1, 1))
    around = fields[k][q, start - 1 : start + size - 1] + fields[k][q, start + 1 : start + size + 1]
    return centre[rows] * field - weight[rows] * (around + forth + back)


def completed(u1, edges, weight, q, parity, start, size):
    rows = slice(start, start + size)
    here = lanes(size)
    edge = pltpu.roll(edges[0, parity, rows], N - NP * 4 - q, 1)
    edge = jnp.where((here == 0) | (here == N - 1), edge, 0.0)
    return u1[q, rows] - weight[rows] * edge


def outer_columns(s, margins, start, size):
    rows = slice(start, start + size)
    here = lanes(size)
    left, right = s[2, 0, rows], s[2, 1, rows]
    columns = (
        pltpu.roll(left, N - NP, 1),
        pltpu.roll(left, N - 2 * NP + 1, 1),
        pltpu.roll(right, 3 * NP - 2, 1),
        pltpu.roll(right, 2 * NP - 1, 1),
    )
    for j in range(4):
        place = (here + 4 - j) % 4
        value = jnp.where(place == 0, columns[0], columns[1])
        margins[j, rows] = jnp.where(place == 2, columns[2], jnp.where(place == 3, columns[3], value))


def second_completed(u2, margins, q, j, start, size):
    rows = slice(start, start + size)
    here = lanes(size)
    margin = pltpu.roll(margins[j % 4, rows], N - NP * 4 - q, 1)
    return jnp.where((here < 2) | (here >= N - 2), margin, u2[q, rows])


def folded(value):
    return jnp.sum((value * value).reshape(-1, 8, N), axis=0)


def trace_basis(fields, basis, kappa, q, start, size, fifth):
    rows = slice(start, start + size)
    scale = kappa[start - TOP : start - TOP + size]
    v0, v1, v2, v3, v4 = (field[q, rows] for field in fields)
    one, zero = scale * v1, scale * v0
    for i, value in enumerate((one * (v0 + v0), one * v2 + zero * v3, one * v4 + zero * fifth)):
        base = pl.multiple_of((i * NP + q) * PITCH + (start - TOP), 8)
        basis[pl.ds(base, size)] = value


def block_sums(basis, ids, first, last, unroll):
    block = lax.broadcasted_iota(jnp.int32, (NB, N), 0)

    def blocks(step, total):
        high, rest, hot = [], [], []
        for row in [step * ABREAST + i for i in range(ABREAST)]:
            data = basis[pl.ds(row, 3 * NP, stride=PITCH)]
            high.append(data.astype(BF16))
            rest.append((data - high[-1].astype(F32)).astype(BF16))
            hot.append((ids[pl.ds(row, 1)] == block).astype(F32).astype(BF16))
        both = jnp.concatenate([jnp.concatenate(high, axis=1), jnp.concatenate(rest, axis=1)], axis=0)
        hot = jnp.concatenate(hot, axis=1)
        return total + lax.dot_general(both, hot, (((1,), (1,)), ((), ())), preferred_element_type=F32)

    total = lax.fori_loop(first // ABREAST, last // ABREAST, blocks, jnp.zeros((6 * NP, NB), F32), unroll=unroll)
    return total[: 3 * NP] + total[3 * NP :]


def first_kernel(signs, mask, kappa, ids_hbm, u0, u1, u2, centre, weight, ids, sem):
    copy = pltpu.make_async_copy(ids_hbm, ids, sem)
    copy.start()
    inner = slice(TOP, TOP + N)
    ocean = mask[...].astype(F32)
    for q in range(NP):
        u0[q, inner] = signs[q].astype(F32) * ocean
    centre[inner] = ocean * (kappa[...] + 0.25)
    weight[inner] = ocean * 0.0625
    here = lanes(CHUNK)

    def probe_group(group, carry):
        for source, target in ((u0, u1), (u1, u2)):
            for start in range(TOP, TOP + N, CHUNK):
                for j in range(TOGETHER):
                    q = group * TOGETHER + j
                    rows = slice(start, start + CHUNK)
                    field = source[q, rows]
                    forth = jnp.where(here == 0, 0.0, pltpu.roll(field, 1, 1))
                    back = jnp.where(here == N - 1, 0.0, pltpu.roll(field, N - 1, 1))
                    around = source[q, start - 1 : start + CHUNK - 1] + source[q, start + 1 : start + CHUNK + 1]
                    target[q, rows] = centre[rows] * field - weight[rows] * (around + forth + back)
        return carry

    lax.fori_loop(0, NP // TOGETHER, probe_group, 0)
    copy.wait()


def inner_kernel(
    u1_in, u2_in, u0, kappa, ids, strips, kstrips, centre, weight,
    u1, u2, u3, u4, s, basis, moments, sums,
    edges, margins, scentre, sweight,
):
    del u1_in, u2_in
    inner = slice(TOP, TOP + N)
    s[0, 2, inner] = strips[2]
    for i in range(2):
        s[0, i, inner] = strips[i]
        square = strips[i] * strips[i]
        scentre[i, inner] = square * (kstrips[i] + 0.25)
        sweight[i, inner] = square * 0.0625
    for k in range(DEPTH):
        for start in range(TOP, TOP + N, 32):
            strip_step(k, s, edges, scentre, sweight, start, 32)
            if k == 2:
                outer_columns(s, margins, start, 32)
    fields = [u0, u1, u2, u3, u4]

    def probe_group(group, carry):
        probes = [(group * TOGETHER + j, j % 2) for j in range(TOGETHER)]
        for k in range(4):
            totals = [jnp.zeros((8, N), F32) for _ in probes]
            for start in range(TOP, TOP + N, CHUNK):
                for j, (q, parity) in enumerate(probes):
                    if k == 0:
                        result = completed(u1, edges, weight, q, parity, start, CHUNK)
                    elif k == 1:
                        result = second_completed(u2, margins, q, j, start, CHUNK)
                    else:
                        result = applied(fields, edges, centre, weight, k, q, parity, start, CHUNK)
                    fields[k + 1][q, start : start + CHUNK] = result
                    low, high = max(start, TOP + 8), min(start + CHUNK, TOP + N - 8)
                    totals[j] += folded(result[low - start : high - start])
            for (q, _), total in zip(probes, totals):
                moments[k, q] = total
        totals = [jnp.zeros((8, N), F32) for _ in probes]
        for start in range(TOP + 8, TOP + N - 8, FINAL):
            for j, (q, parity) in enumerate(probes):
                result = applied(fields, edges, centre, weight, 4, q, parity, start, FINAL)
                totals[j] += folded(result)
                trace_basis(fields, basis, kappa, q, start, FINAL, result)
        for (q, _), total in zip(probes, totals):
            moments[4, q] = total
        return carry

    lax.fori_loop(0, NP // TOGETHER, probe_group, 0)
    sums[...] = block_sums(basis, ids, 8, N - 8, UNROLL)


def outer_kernel(
    u0_in, u1_in, u2_in, u3_in, u4_in, s_in, basis_in,
    moments, sums, kappa, ids, kstrips, odd, even,
    u0, u1, u2, u3, u4, s, basis, message,
    edges, centre, weight, scentre, sweight,
):
    del u0_in, u1_in, u2_in, u3_in, u4_in, s_in, basis_in
    low = lax.axis_index("lon") % 2 == 0
    bands = (TOP - 8, TOP + N - 8)
    for start, inside, outside, if_low, if_high in (
        (bands[0], 8, 0, odd, even),
        (bands[1], 0, 8, even, odd),
    ):
        rows = slice(start + outside, start + outside + 8)
        own = slice(start + inside, start + inside + 8)
        here = slice(start + inside - TOP, start + inside - TOP + 8)
        halo = [jnp.where(low, if_low[i], if_high[i]) for i in range(SLOTS)]
        for q in range(NP):
            u0[q, rows] = halo[q]
        s[0, 2, rows] = halo[NP + 2]
        for i in range(2):
            s[0, i, rows] = halo[NP + i]
            for where, value, kvalue in ((rows, halo[NP + i], halo[NP + 3 + i]), (own, s[0, i, own], kstrips[i, here])):
                scentre[i, where] = value * value * (kvalue + 0.25)
                sweight[i, where] = value * value * 0.0625
        for where, value, kvalue in ((rows, halo[0], halo[NP + 5]), (own, u0[0, own], kappa[here])):
            centre[where] = value * value * (kvalue + 0.25)
            weight[where] = value * value * 0.0625
    fields = [u0, u1, u2, u3, u4]
    blank = jnp.zeros((8, N), F32)
    for row in (TOP - 16, TOP + N + 8):
        for field in fields:
            for q in range(NP):
                field[q, row : row + 8] = blank
        for k in range(DEPTH):
            for i in range(2):
                s[k, i, row : row + 8] = blank
    for k in range(DEPTH):
        for start in bands:
            strip_step(k, s, edges, scentre, sweight, start, 16)

    heads = []
    for k in range(4):
        stacked = []
        for q in range(NP):
            total = moments[k, q]
            for start, own in ((bands[0], 8), (bands[1], 0)):
                result = applied(fields, edges, centre, weight, k, q, q % 2, start, 16)
                fields[k + 1][q, start : start + 16] = result
                total += folded(result[own : own + 8])
            stacked.append(jnp.sum(total, axis=0, keepdims=True))
        heads.append(jnp.concatenate(stacked, axis=0))
    stacked = []
    for q in range(NP):
        total = moments[4, q]
        for start in (TOP, TOP + N - 8):
            result = applied(fields, edges, centre, weight, 4, q, q % 2, start, 8)
            total += folded(result)
            trace_basis(fields, basis, kappa, q, start, 8, result)
        stacked.append(jnp.sum(total, axis=0, keepdims=True))
    heads.append(jnp.concatenate(stacked, axis=0))
    total = sums[...] + block_sums(basis, ids, 0, 8, 8 // ABREAST) + block_sums(basis, ids, N - 8, N, 8 // ABREAST)
    ocean = u0[0, TOP : TOP + N]
    ocean = ocean * ocean

    ocean_sum = jnp.sum(jnp.sum(ocean, axis=0, keepdims=True), axis=1, keepdims=True)
    columns = [jnp.broadcast_to(ocean_sum, (NP, 1))]
    columns += [jnp.sum(head, axis=1, keepdims=True) for head in heads]
    wide = jnp.zeros((NP, NB), F32)
    spot = lax.broadcasted_iota(jnp.int32, (NP, NB), 1)
    coarse = F32(1.5 * 2**20)
    for k, column in enumerate(columns):
        head = (column + coarse) - coarse
        wide = jnp.where(spot == 2 * k, head, wide)
        wide = jnp.where(spot == 2 * k + 1, column - head, wide)
    half = 3 * NP // 2
    message[:half] = jnp.concatenate([total[:half], total[half:]], axis=1)
    message[half:] = jnp.concatenate([wide[: NP // 2], wide[NP // 2 :]], axis=1)


def two_sum(a, b):
    s = a + b
    t = s - a
    return s, (a - (s - t)) + (b - t)


def quick(a, b):
    s = a + b
    return s, b - (s - a)


def split(a):
    t = a * F32(4097.0)
    high = t - (t - a)
    return high, a - high


def mul(a, b):
    p = a[0] * b[0]
    ah, al = split(a[0])
    bh, bl = split(b[0])
    e = ((ah * bh - p) + ah * bl + al * bh) + al * bl
    return quick(p, e + (a[0] * b[1] + a[1] * b[0]))


def sub(a, b):
    s, e = two_sum(a[0], -b[0])
    return quick(s, e + (a[1] - b[1]))


def inverse(b):
    first = 1.0 / b[0]
    zero = jnp.zeros_like(first)
    rest = sub((jnp.ones_like(first), zero), mul(b, (first, zero)))
    return quick(first, first * rest[0])


def keep(ok, value, other):
    return tuple(jnp.where(ok, v, other) for v in value)


def solve(moment):
    g0, h1, h2, h3, h4, h5 = moment
    tiny = F32(2e-8)
    over = inverse(h1)
    l1, l2 = mul(h2, over), mul(h3, over)
    s11, s12, s22 = sub(h3, mul(h2, l1)), sub(h4, mul(h2, l2)), sub(h5, mul(h3, l2))
    y1, y2 = sub(h1, mul(g0, l1)), sub(h2, mul(g0, l2))
    ok1 = s11[0] > tiny * h3[0]
    over1 = keep(ok1, inverse(keep(ok1, s11, 1.0)), 0.0)
    l21 = mul(s12, over1)
    d2, z2 = sub(s22, mul(s12, l21)), sub(y2, mul(y1, l21))
    ok2 = ok1 & (d2[0] > tiny * h5[0])
    over2 = keep(ok2, inverse(keep(ok2, d2, 1.0)), 0.0)
    c2 = mul(z2, over2)
    c1 = mul(sub(y1, mul(s12, c2)), over1)
    c0 = mul(sub(sub(g0, mul(h2, c1)), mul(h3, c2)), over)
    return c0[0] + c0[1], c1[0] + c1[1], c2[0] + c2[1]


def combine_kernel(message, u0, u2, u4, basis, solution, trace, traces):
    half = 3 * NP // 2
    wide = jnp.concatenate([message[half:, :NB], message[half:, NB:]], axis=0)
    sums = jnp.concatenate([message[:half, :NB], message[:half, NB:]], axis=0)
    moment = []
    for k in range(6):
        head = wide[:, 2 * k : 2 * k + 1]
        rest = wide[:, 2 * k + 1 : 2 * k + 2]
        moment.append(quick(jnp.broadcast_to(head, (NP, N)), jnp.broadcast_to(rest, (NP, N))))
    c0, c1, c2 = solve(moment)
    cells = F32(N * N * 128 // NB)
    total = c0[:, :NB] * sums[:NP] + c1[:, :NB] * sums[NP : 2 * NP] + c2[:, :NB] * sums[2 * NP :]
    traces[...] = total / cells
    for q in range(NP):
        a0, a1, a2 = (c[q : q + 1] for c in (c0, c1, c2))
        solution[q] = a0 * u0[q, TOP : TOP + N] + a1 * u2[q, TOP : TOP + N] + a2 * u4[q, TOP : TOP + N]
        rows = [slice((i * NP + q) * PITCH, (i * NP + q) * PITCH + N) for i in range(3)]
        trace[q] = a0 * basis[rows[0]] + a1 * basis[rows[1]] + a2 * basis[rows[2]]


def pairs(count, offset, closed):
    out = []
    for i in range(offset, count, 2):
        j = (i + 1) % count
        if i + 1 < count or closed:
            out += [(i, j), (j, i)]
    return out


def swap(odd, even, axis, closed):
    count = lax.axis_size(axis)
    odd = lax.ppermute(odd, axis, pairs(count, 1, closed))
    even = lax.ppermute(even, axis, pairs(count, 0, closed))
    return odd, even


def everywhere(value):
    def sent(axis, bits):
        return lax.ppermute(value, axis, [(i, i ^ bits) for i in range(lax.axis_size(axis))])

    value = value + sent("lat", 1)
    for axis, unit in (("lat", 2), ("lon", 1), ("lon", 4)):
        near, far, across = sent(axis, unit), sent(axis, 3 * unit), sent(axis, 2 * unit)
        value = (value + near) + (far + across)
    return value


def per_device(signs, mask, kappa, ids):
    edge, field, strip, plane = (N, N), (NP, ROWS, N), (2, ROWS, N), (ROWS, N)
    halo = (SLOTS, 8, N)
    flat = (3 * NP * PITCH, N)
    ints = jax.ShapeDtypeStruct(edge, jnp.int32)
    signs, mask, kappa, ids = (pltpu.with_memory_space_constraint(x, pltpu.HBM) for x in (signs, mask, kappa, ids))
    own_odd, own_even, signs, mask, kappa = call(
        pack_kernel,
        [edge, edge, jax.ShapeDtypeStruct((NP, N, N), jnp.int32), ints, edge],
        8,
        [
            pltpu.VMEM((NP // 2, 2 * N, 2 * N), BF16),
            pltpu.SemaphoreType.DMA((2 + PARTS,)),
        ],
        specs=[FAR] * 3,
    )(signs, mask, kappa)
    odd, even = swap(own_odd, own_even, "lat", False)
    u0, u1, u2, centre, weight, ids = call(
        first_kernel,
        [field, field, field, plane, plane, ints],
        8,
        [pltpu.SemaphoreType.DMA],
        specs=[NEAR, NEAR, NEAR, FAR],
        micros=2,
    )(signs, mask, kappa, ids)
    strips, kstrips, row_odd, row_even = call(strips_kernel, [(3, N, N), (2, N, N), halo, halo], 8)(
        odd, even, own_odd, own_even, kappa, u0, centre
    )
    row_odd, row_even = swap(row_odd, row_even, "lon", True)
    coefficients = [pltpu.VMEM(shape, F32) for shape in (plane, plane, strip, strip)]
    edges = pltpu.VMEM((DEPTH, 2, ROWS, N), F32)
    u1, u2, u3, u4, s, basis, moments, sums = call(
        inner_kernel,
        [field, field, field, field, (DEPTH, 3, ROWS, N), flat, (DEPTH, NP, 8, N), (3 * NP, NB)],
        24,
        [edges, pltpu.VMEM((4, ROWS, N), F32), *coefficients[2:]],
        aliases={0: 0, 1: 1},
        micros=8,
    )(u1, u2, u0, kappa, ids, strips, kstrips, centre, weight)
    u0, u1, u2, u3, u4, s, basis, message = call(
        outer_kernel,
        [field, field, field, field, field, (DEPTH, 3, ROWS, N), flat, (2 * NP, N)],
        24,
        [edges, *coefficients],
        aliases={i: i for i in range(7)},
    )(u0, u1, u2, u3, u4, s, basis, moments, sums, kappa, ids, kstrips, row_odd, row_even)
    message = everywhere(message)
    out = (NP, N, N)
    return tuple(call(combine_kernel, [out, out, (NP, NB)], 16)(message, u0, u2, u4, basis))


def solution(mesh):
    placed = (P(None, "lon", "lat"), P("lon", "lat"), P("lon", "lat"), P("lon", "lat"))
    return jax.shard_map(
        per_device,
        mesh=mesh,
        in_specs=placed,
        out_specs=(P(None, "lon", "lat"), P(None, "lon", "lat"), P()),
        check_vma=False,
    )
```
